32 devices in a mesh: dp: 8 (over z, x), tensor: 4 (over y, core).
Axes of the slice: x: 2, y: 2, z: 4, core: 2. Of those that a mesh axis runs over, the one named last changes fastest.
Arguments:
- tokens: bfloat16 [2, 4096, 2048], P(None, ('dp', 'tensor')), may hold values from -6 to 6
- cotangent: bfloat16 [2, 4096, 2048], P(None, ('dp', 'tensor')), may hold values from -6 to 6
- token_slots: int32 [2, 4096], P(None, ('dp', 'tensor')), may hold values from 0 to 4095, as said below
- lengths: int32 [2, 8, 3], P(None, 'dp'), may hold values from 1 to 256, 512 in all within a row
- query_weight: bfloat16 [2048, 2048], P('dp', 'tensor'), may hold values from -0.125 to 0.125
- key_projection_weight: bfloat16 [2048, 1024], P('dp', 'tensor'), may hold values from -0.125 to 0.125
- value_projection_weight: bfloat16 [2048, 1024], P('dp', 'tensor'), may hold values from -0.125 to 0.125
- output_weight: bfloat16 [2048, 2048], P(('tensor', 'dp')), may hold values from -0.75 to 0.75
- gate_weight: bfloat16 [2048, 8192], P('dp', 'tensor'), may hold values from -0.125 to 0.125
- up_weight: bfloat16 [2048, 8192], P('dp', 'tensor'), may hold values from -0.125 to 0.125
- down_weight: bfloat16 [8192, 2048], P(('tensor', 'dp')), may hold values from -0.0625 to 0.0625
- prenorm_gain: bfloat16 [2048], P('dp'), may hold values from 0.5 to 1.5
- midnorm_gain: bfloat16 [2048], P('dp'), may hold values from 0.5 to 1.5
Outputs:
- layer_out: bfloat16 [2, 4096, 2048], P(None, ('dp', 'tensor'))
- tokens_grad: bfloat16 [2, 4096, 2048], P(None, ('dp', 'tensor'))
- query_grad: float32 [2048, 2048], P('dp', 'tensor')
- key_grad: float32 [2048, 1024], P('dp', 'tensor')
- value_grad: float32 [2048, 1024], P('dp', 'tensor')
- output_grad: float32 [2048, 2048], P(('tensor', 'dp'))
- gate_grad: float32 [2048, 8192], P('dp', 'tensor')
- up_grad: float32 [2048, 8192], P('dp', 'tensor')
- down_grad: float32 [8192, 2048], P(('tensor', 'dp'))
- prenorm_grad: float32 [2048], P('dp')
- midnorm_grad: float32 [2048], P('dp')
The draws below stay inside these ranges and needn't reach their ends.
Inputs may be any that keep to these rules, and one draw needn't show every extreme that they name: `token_slots`: for each micro-batch a permutation of the token positions; the tokens of one device go 4 to each device of the work layout. Each row of 3 lengths fills the 512 tokens of one data index in one micro-batch.
All inputs are finite; a program needn't handle non-finite values.
Results may differ from the reference program's by a relative error of at most 0.024.
Values may be sent and summed in bfloat16 or wider, within the bound.
No kernel may reach another device: no remote copies, remote signals or barrier semaphores. Data moves between devices by JAX's collectives and lax.ppermute only.
A program may use at most 192 MiB of HBM per device.

```python
import math
import jax
import jax.numpy as jnp
import numpy as np
from jax import lax

MODEL_WIDTH = 2048
QUERY_HEADS = 8
KEY_VALUE_HEADS = 4
HEAD_SIZE = 256
FF = 8192
TOK_DEV = 128
MICRO = 2
SEQS = 3
G = 512
LONGEST = 256
GROUPS = 8
TOKENS = 4096
SENDS = 4


def shuffled(subkey):
    return jax.random.permutation(subkey, TOK_DEV).astype(jnp.int32)


def one_placement(key):
    device_count = TOKENS // TOK_DEV
    source_key, target_key = jax.random.split(key)
    leaving = jax.vmap(shuffled)(jax.random.split(source_key, device_count))
    arriving = jax.vmap(shuffled)(jax.random.split(target_key, device_count))
    target_device = leaving // SENDS
    item_index = leaving % SENDS
    incoming = jnp.arange(device_count, dtype=jnp.int32)[:, None] * SENDS + item_index
    local_row = arriving[target_device, incoming]
    return (target_device * TOK_DEV + local_row).reshape(TOKENS).astype(jnp.int32)


def draw_token_slots(key, part):
    return jax.vmap(one_placement)(jax.random.split(key, MICRO))


def level_of(rng, shape, pieces, low, top_value):
    gain = 1.0
    for axis_at, parts in pieces:
        heights = jax.random.uniform(jax.random.fold_in(jax.random.fold_in(rng, 6), axis_at), (parts,), jnp.float32, low / len(pieces), top_value / len(pieces))
        gain = gain * jnp.repeat(jnp.exp(heights), shape[axis_at] // parts).reshape((-1,) + (1,) * (len(shape) - 1 - axis_at))
    return gain


def profile(amount, total, bound, skew):
    portions = [(1 << 20) // math.isqrt(rank ** skew) + 1 for rank in range(2, amount + 1)]
    rest, holding = total - bound - (amount - 1), [1] * (amount - 1)
    while rest > 0:
        movable = [i for i in range(amount - 1) if holding[i] < bound]
        mass, budget = sum([portions[i] for i in movable]), rest
        for i in movable:
            more = min(bound - holding[i], max(1, budget * portions[i] // mass), rest)
            holding[i] = holding[i] + more
            rest = rest - more
    return np.array([bound] + holding)


def ragged_sizes(stream_key, amount, total, bound, slope):
    if amount == 2:
        one = jax.random.randint(stream_key, (), max(1, total - bound), min(bound, total - 1) + 1)
        return jnp.stack([one, total - one])
    sizes = jnp.asarray(profile(amount, total, bound, slope), jnp.int32)
    pairs = (amount - 1) // 2
    donor, sink = sizes[1:1 + 2 * pairs:2], sizes[2:2 + 2 * pairs:2]
    slack = jnp.minimum(donor - 1, bound - sink)
    moved = jax.random.randint(jax.random.fold_in(stream_key, 1), (pairs,), 0, 1 << 20) % (slack + 1)
    sizes = sizes.at[1:1 + 2 * pairs:2].set(donor - moved).at[2:2 + 2 * pairs:2].set(sink + moved)
    return sizes[jax.random.permutation(jax.random.fold_in(stream_key, 2), amount)]


def centred(stream_key, extent, scale, bound, cuts=(), held_as=jnp.bfloat16):
    values = scale * jax.random.normal(stream_key, extent, jnp.float32)
    if cuts:
        values = values * level_of(stream_key, extent, cuts, -0.22, 0.18)
    return jnp.clip(values, -bound, bound).astype(held_as)


def setup_inputs(seed: int = 0) -> dict:
    seeds = jax.random.split(jax.random.key(seed), 14)
    return {
        "tokens": centred(seeds[0], (MICRO, TOKENS, MODEL_WIDTH), 1.0, 6.0, ((1, 32),)),
        "cotangent": centred(seeds[1], (MICRO, TOKENS, MODEL_WIDTH), 1.0, 6.0, ((1, 32),)),
        "token_slots": draw_token_slots(jax.random.fold_in(seeds[13], 71), 0),
        "lengths": jax.vmap(lambda own: ragged_sizes(own, SEQS, G, LONGEST, 2))(jax.random.split(seeds[3], MICRO * GROUPS)).reshape((MICRO, GROUPS, SEQS)).astype(jnp.int32),
        "query_weight": centred(seeds[4], (MODEL_WIDTH, QUERY_HEADS * HEAD_SIZE), MODEL_WIDTH ** -0.5, 0.125, ((0, 8), (1, 4))),
        "key_projection_weight": centred(seeds[5], (MODEL_WIDTH, KEY_VALUE_HEADS * HEAD_SIZE), MODEL_WIDTH ** -0.5, 0.125, ((0, 8), (1, 4))),
        "value_projection_weight": centred(seeds[6], (MODEL_WIDTH, KEY_VALUE_HEADS * HEAD_SIZE), MODEL_WIDTH ** -0.5, 0.125, ((0, 8), (1, 4))),
        "output_weight": centred(seeds[7], (QUERY_HEADS * HEAD_SIZE, MODEL_WIDTH), (QUERY_HEADS * HEAD_SIZE * 8 // LONGEST) ** -0.5, 0.75, ((0, 32),)),
        "gate_weight": centred(seeds[8], (MODEL_WIDTH, FF), MODEL_WIDTH ** -0.5, 0.125, ((0, 8), (1, 4))),
        "up_weight": centred(seeds[9], (MODEL_WIDTH, FF), MODEL_WIDTH ** -0.5, 0.125, ((0, 8), (1, 4))),
        "down_weight": centred(seeds[10], (FF, MODEL_WIDTH), FF ** -0.5, 0.0625, ((0, 32),)),
        "prenorm_gain": jnp.clip(1.0 + 0.1 * jax.random.normal(seeds[11], (MODEL_WIDTH,), jnp.float32), 0.5, 1.5).astype(jnp.bfloat16),
        "midnorm_gain": jnp.clip(1.0 + 0.1 * jax.random.normal(seeds[12], (MODEL_WIDTH,), jnp.float32), 0.5, 1.5).astype(jnp.bfloat16),
    }


EPSILON = 1e-06
ROPE_BASE = 1000042.0
BLOCK = 512
NEGATIVE = -1e+30
HIGHEST = lax.Precision.HIGHEST

@jax.custom_vjp
def reduced_precision(v):
    return lax.optimization_barrier(v.astype(jnp.bfloat16)).astype(jnp.float32)

@jax.custom_vjp
def reduced_precision_backward(v):
    return v

def low_keep(v):
    return (reduced_precision(v), None)

def low_pass(kept, grad):
    return (grad,)

def back_keep(v):
    return (v, None)

def back_low(kept, grad):
    return (reduced_precision(grad),)
reduced_precision.defvjp(low_keep, low_pass)
reduced_precision_backward.defvjp(back_keep, back_low)

def matrix_multiply(left, right):
    return jnp.dot(left, right, precision=HIGHEST, preferred_element_type=jnp.float32)

def rms_scale(value_heads):
    return lax.rsqrt(lax.optimization_barrier(jnp.mean(value_heads * value_heads, axis=-1, keepdims=True)) + EPSILON)

def rope_tables(positions, head):
    half = head // 2
    frequency = jnp.exp(jnp.arange(half, dtype=jnp.float32) * (-2.0 * math.log(ROPE_BASE) / head))
    angles = positions.astype(jnp.float32)[:, None] * frequency[None, :]
    return (jnp.cos(angles), jnp.sin(angles))

def apply_rotary(value_heads, cosine_table, sine_table):
    half = value_heads.shape[-1] // 2
    first = value_heads[..., :half]
    second = value_heads[..., half:]
    cosine_table = cosine_table[:, None, :]
    sine_table = sine_table[:, None, :]
    return jnp.concatenate([first * cosine_table - second * sine_table, second * cosine_table + first * sine_table], axis=-1)

def sequence_layout(lens, total_count):
    rows = jnp.arange(total_count, dtype=jnp.int32)
    ends = jnp.cumsum(lens).astype(jnp.int32)
    segment = lax.optimization_barrier(jnp.sum((rows[:, None] >= ends[None, :]).astype(jnp.int32), axis=1)).astype(jnp.int32)
    starts = ends - lens.astype(jnp.int32)
    which = segment[:, None] == jnp.arange(lens.shape[0], dtype=jnp.int32)[None, :]
    begin = lax.optimization_barrier(jnp.sum(jnp.where(which, starts[None, :], 0), axis=1)).astype(jnp.int32)
    return (segment, rows - begin)

def layer(params, inputs, segment, positions):
    query_w, key_matrix, value_matrix, output_w, gate_w, up_w, down_w, first_gain, second_gain = params
    total_count = inputs.shape[0]
    scale = 1.0 / math.sqrt(HEAD_SIZE)
    first = rms_scale(inputs)
    first_normed_rows = reduced_precision(inputs * first * first_gain)
    query_heads = reduced_precision_backward(matrix_multiply(first_normed_rows, query_w)).reshape(total_count, QUERY_HEADS, HEAD_SIZE)
    key_heads = reduced_precision_backward(matrix_multiply(first_normed_rows, key_matrix)).reshape(total_count, KEY_VALUE_HEADS, HEAD_SIZE)
    value_heads = reduced_precision(reduced_precision_backward(matrix_multiply(first_normed_rows, value_matrix))).reshape(total_count, KEY_VALUE_HEADS, HEAD_SIZE)
    cosine_table, sine_table = rope_tables(positions, HEAD_SIZE)
    query_rotated = reduced_precision(apply_rotary(query_heads, cosine_table, sine_table)).reshape(total_count, KEY_VALUE_HEADS, QUERY_HEADS // KEY_VALUE_HEADS, HEAD_SIZE)
    key_rot = reduced_precision(apply_rotary(key_heads, cosine_table, sine_table))
    rows = jnp.arange(total_count, dtype=jnp.int32)

    @jax.checkpoint
    def one_block(index):
        start = (index * BLOCK).astype(jnp.int32)
        query_block = lax.dynamic_slice_in_dim(query_rotated, start, BLOCK, 0)
        seg_block = lax.dynamic_slice_in_dim(segment, start, BLOCK, 0)
        row_block = start + jnp.arange(BLOCK, dtype=jnp.int32)
        allowed = (seg_block[:, None] == segment[None, :]) & (row_block[:, None] >= rows[None, :])
        scores = jnp.einsum('qcgd,kcd->cgqk', query_block, key_rot, precision=HIGHEST) * scale
        scores = reduced_precision_backward(scores)
        scores = jnp.where(allowed, scores, NEGATIVE)
        probs = jax.nn.softmax(scores, axis=-1)
        return jnp.einsum('cgqk,kcd->qcgd', reduced_precision(probs), value_heads, precision=HIGHEST)
    heads_out = lax.map(one_block, jnp.arange(total_count // BLOCK, dtype=jnp.int32)).reshape(total_count, QUERY_HEADS * HEAD_SIZE)
    heads_out = reduced_precision(reduced_precision_backward(heads_out))
    residual = inputs + reduced_precision_backward(matrix_multiply(heads_out, output_w))
    second = rms_scale(residual)
    normed_two = reduced_precision(residual * second * second_gain)
    gate = reduced_precision_backward(matrix_multiply(normed_two, gate_w))
    upward = reduced_precision_backward(matrix_multiply(normed_two, up_w))
    hidden = reduced_precision(jax.nn.silu(gate) * upward)
    return residual + reduced_precision_backward(matrix_multiply(hidden, down_w))

def reference(tokens, cotangent, token_slots, lengths, query_weight, key_projection_weight, value_projection_weight, output_weight, gate_weight, up_weight, down_weight, prenorm_gain, midnorm_gain):
    batch = jnp.arange(MICRO, dtype=jnp.int32)[:, None]
    placed = jnp.zeros((MICRO, TOKENS, MODEL_WIDTH), jnp.float32).at[batch, token_slots].set(tokens.astype(jnp.float32))
    placed_cot = jnp.zeros((MICRO, TOKENS, MODEL_WIDTH), jnp.float32).at[batch, token_slots].set(cotangent.astype(jnp.float32))
    group_count = MICRO * GROUPS
    inputs_all = placed.reshape(group_count, G, MODEL_WIDTH)
    cot_all = placed_cot.reshape(group_count, G, MODEL_WIDTH)
    lens_all = lengths.reshape(group_count, SEQS)
    params = tuple((w.astype(jnp.float32) for w in (query_weight, key_projection_weight, value_projection_weight, output_weight, gate_weight, up_weight, down_weight, prenorm_gain, midnorm_gain)))

    def step(carry, packed):
        group_in, group_cot, group_lens = packed
        segment, positions = sequence_layout(group_lens, G)
        result, pullback = jax.vjp(lambda weights, rows: layer(weights, rows, segment, positions), params, group_in)
        d_params, d_rows = pullback(group_cot)
        carry = tuple((acc + extra for acc, extra in zip(carry, d_params)))
        return (carry, (result, d_rows))
    zeros = tuple((jnp.zeros_like(w) for w in params))
    totals, (results, d_inputs) = lax.scan(step, zeros, (inputs_all, cot_all, lens_all))
    results = results.reshape(MICRO, TOKENS, MODEL_WIDTH)
    d_inputs = d_inputs.reshape(MICRO, TOKENS, MODEL_WIDTH)
    index = token_slots[:, :, None]
    layer_out = jnp.take_along_axis(results, index, axis=1).astype(jnp.bfloat16)
    tokens_grad = jnp.take_along_axis(d_inputs, index, axis=1).astype(jnp.bfloat16)
    return (layer_out, tokens_grad, totals[0], totals[1], totals[2], totals[3], totals[4], totals[5], totals[6], totals[7], totals[8])
```

```python
import math

import jax
import jax.numpy as jnp
from jax import lax
from jax.sharding import Mesh, PartitionSpec as P

HEAD_SIZE = 256
EPSILON = 1e-06
ROPE_BASE = 1000042.0
NEGATIVE = -1e30
CHUNKS = 2
F32 = jnp.float32
BF16 = jnp.bfloat16

SWAP = [(0, 1), (1, 0)]
DIAGONAL = [(0, 3), (3, 0), (1, 2), (2, 1)]
Z_NEAR = [(0, 1), (1, 0), (2, 3), (3, 2)]
Z_FAR = [(0, 2), (2, 0), (1, 3), (3, 1)]
Z_ACROSS = [(0, 3), (3, 0), (1, 2), (2, 1)]
Z_MIDDLE = [(1, 2), (2, 1)]
Z_OUTWARD = [(2, 3), (1, 0)]
Z_INWARD = [(3, 2), (0, 1)]


def rms_scale(values):
    return lax.rsqrt(jnp.mean(values * values, axis=-1, keepdims=True) + EPSILON)


def rope_tables(positions, head):
    half = head // 2
    frequency = jnp.exp(jnp.arange(half, dtype=F32) * (-2.0 * math.log(ROPE_BASE) / head))
    angles = positions.astype(F32)[:, None] * frequency[None, :]
    return (jnp.cos(angles), jnp.sin(angles))


def rotate(values, cosine, sine):
    half = values.shape[-1] // 2
    first, second = values[..., :half], values[..., half:]
    cosine, sine = cosine[:, None, :], sine[:, None, :]
    return jnp.concatenate(
        [first * cosine - second * sine, second * cosine + first * sine], axis=-1
    )


def sequence_layout(lens, total):
    rows = jnp.arange(total, dtype=jnp.int32)
    ends = jnp.cumsum(lens)
    segment = jnp.sum((rows[:, None] >= ends[None, :]).astype(jnp.int32), axis=1)
    starts = ends - lens
    which = segment[:, None] == jnp.arange(lens.shape[0], dtype=jnp.int32)[None, :]
    begin = jnp.sum(jnp.where(which, starts[None, :], 0), axis=1)
    return (segment, rows - begin)


def mm(left, right):
    return jnp.dot(left, right, preferred_element_type=F32)


def outer_sum(left, right):
    return lax.dot_general(left, right, (((0,), (0,)), ((), ())), preferred_element_type=F32)


def times_transposed(left, right):
    return lax.dot_general(left, right, (((1,), (1,)), ((), ())), preferred_element_type=F32)


def attend_forward(query, key, value, allowed, scale):
    scores = jnp.einsum("qcgd,kcd->cgqk", query, key, preferred_element_type=F32) * scale
    scores = jnp.where(allowed, scores, NEGATIVE)
    row_max = jnp.max(scores, axis=-1, keepdims=True)
    expo = jnp.exp(scores - row_max)
    row_total = jnp.sum(expo, axis=-1, keepdims=True)
    probs = (expo / row_total).astype(BF16)
    heads = jnp.einsum("cgqk,kcd->qcgd", probs, value, preferred_element_type=F32)
    return (heads.astype(BF16), row_max + jnp.log(row_total))


def attend_backward(query, key, value, d_heads, log_totals, allowed, scale):
    scores = jnp.einsum("qcgd,kcd->cgqk", query, key, preferred_element_type=F32) * scale
    scores = jnp.where(allowed, scores, NEGATIVE)
    probs = jnp.exp(scores - log_totals)
    d_probs = jnp.einsum("qcgd,kcd->cgqk", d_heads, value, preferred_element_type=F32)
    delta = jnp.sum(probs * d_probs, axis=-1, keepdims=True)
    d_scores = (probs * (d_probs - delta)).astype(BF16)
    d_query = jnp.einsum("cgqk,kcd->qcgd", d_scores, key, preferred_element_type=F32) * scale
    d_key = jnp.einsum("cgqk,qcgd->kcd", d_scores, query, preferred_element_type=F32) * scale
    d_value = jnp.einsum(
        "cgqk,qcgd->kcd", probs.astype(BF16), d_heads, preferred_element_type=F32
    )
    return (d_query, d_key, d_value)


def norm_backward(values, scale, gain, d_normed):
    weighted = d_normed * gain
    d_values = scale * weighted - values * scale * scale * scale * jnp.mean(
        weighted * values, axis=-1, keepdims=True
    )
    return (d_values, jnp.sum(d_normed * values * scale, axis=0))


def take(array, index, axis=0):
    return lax.dynamic_index_in_dim(array, index, axis, keepdims=False)


def put(array, piece, index, axis=0):
    return lax.dynamic_update_index_in_dim(array, piece, index, axis)


def in_order(position, own, other, axis=0):
    first = jnp.where(position == 0, own, other)
    second = jnp.where(position == 0, other, own)
    return jnp.stack([first, second], axis=axis)


def gather_z(piece):
    size, here = lax.axis_size("z"), lax.axis_index("z")
    if size != 4:
        return lax.all_gather(piece, "z", axis=0)
    far = lax.ppermute(piece, "z", Z_FAR)
    near = lax.ppermute(piece, "z", Z_NEAR)
    middle = lax.ppermute(piece, "z", Z_MIDDLE)
    outward = lax.ppermute(far, "z", Z_OUTWARD)
    across = jnp.where((here == 1) | (here == 2), middle, outward)
    whole = jnp.zeros((size,) + piece.shape, piece.dtype)
    for step, part in enumerate((piece, near, far, across)):
        whole = put(whole, part, here ^ step)
    return whole


def reduce_z(parts):
    size, here = lax.axis_size("z"), lax.axis_index("z")
    if size != 4:
        return lax.psum_scatter(parts, "z", scatter_dimension=0).astype(F32)
    own, near, far, across = [take(parts, here ^ step) for step in range(4)]
    inward = lax.ppermute(across, "z", Z_INWARD)
    from_near = lax.ppermute(near, "z", Z_NEAR)
    from_middle = lax.ppermute(across, "z", Z_MIDDLE)
    relay = (far.astype(F32) + inward.astype(F32)).astype(BF16)
    from_far = lax.ppermute(relay, "z", Z_FAR)
    return (
        own.astype(F32)
        + from_near.astype(F32)
        + from_middle.astype(F32)
        + from_far.astype(F32)
    )


def gather_tensor(rows):
    here_y, here_c = lax.axis_index("y"), lax.axis_index("c")
    beside = lax.ppermute(rows, "y", SWAP)
    pieces = (
        (rows, here_y, here_c),
        (beside, 1 - here_y, here_c),
        (lax.ppermute(rows, "c", SWAP), here_y, 1 - here_c),
        (lax.ppermute(beside, "c", SWAP), 1 - here_y, 1 - here_c),
    )
    whole = jnp.zeros((rows.shape[0], 4) + rows.shape[1:], rows.dtype)
    for piece, at_y, at_c in pieces:
        whole = put(whole, piece, 2 * at_y + at_c, axis=1)
    return whole


def reduce_tensor(parts):
    here_y, here_c = lax.axis_index("y"), lax.axis_index("c")
    micro, _, rows, width = parts.shape
    parts = parts.reshape(micro, 2, 2, rows, width)
    arrived = lax.ppermute(take(parts, 1 - here_c, 2), "c", SWAP)
    both = take(parts, here_c, 2).astype(F32) + arrived.astype(F32)
    sent = lax.ppermute(take(both, 1 - here_y, 1).astype(BF16), "y", SWAP)
    return take(both, here_y, 1) + sent.astype(F32)


def gather_eight(rows):
    planes = (
        rows,
        lax.ppermute(rows, "x", SWAP),
        lax.ppermute(rows, "y", SWAP),
        lax.ppermute(rows, ("x", "y"), DIAGONAL),
    )
    return jnp.concatenate(planes + tuple(lax.ppermute(plane, "c", SWAP) for plane in planes))


def reduce_eight(parts):
    parts = parts.reshape((8, parts.shape[0] // 8) + parts.shape[1:])
    arrived = lax.ppermute(parts[4:], "c", SWAP)
    sums = parts[:4].astype(F32) + arrived.astype(F32)
    low = sums[1:].astype(BF16)
    return (
        sums[0]
        + lax.ppermute(low[0], "x", SWAP).astype(F32)
        + lax.ppermute(low[1], "y", SWAP).astype(F32)
        + lax.ppermute(low[2], ("x", "y"), DIAGONAL).astype(F32)
    )


def gather_gains(gains):
    size, here = lax.axis_size("z"), lax.axis_index("z")
    pair = in_order(lax.axis_index("x"), gains, lax.ppermute(gains, "x", SWAP))
    if size != 4:
        whole = lax.all_gather(pair, "z", axis=0)
    else:
        whole = jnp.zeros((size,) + pair.shape, pair.dtype)
        whole = put(whole, pair, here)
        for step, pairs in ((1, Z_NEAR), (2, Z_FAR), (3, Z_ACROSS)):
            whole = put(whole, lax.ppermute(pair, "z", pairs), here ^ step)
    return jnp.moveaxis(whole, 2, 0).reshape(gains.shape[0], -1)


def reduce_gains(grads):
    size, here_z, here_x = lax.axis_size("z"), lax.axis_index("z"), lax.axis_index("x")
    parts = grads.reshape(grads.shape[0], size, 2, -1)
    parts = take(parts, here_x, 2) + lax.ppermute(take(parts, 1 - here_x, 2), "x", SWAP)
    if size != 4:
        total = lax.psum_scatter(parts, "z", scatter_dimension=1)
    else:
        total = take(parts, here_z, 1)
        for step, pairs in ((1, Z_NEAR), (2, Z_FAR), (3, Z_ACROSS)):
            total = total + lax.ppermute(take(parts, here_z ^ step, 1), "z", pairs)
    total = total + lax.ppermute(total, "c", SWAP)
    return total + lax.ppermute(total, "y", SWAP)


def body(
    tokens,
    cotangent,
    token_slots,
    lengths,
    query_weight,
    key_projection_weight,
    value_projection_weight,
    output_weight,
    gate_weight,
    up_weight,
    down_weight,
    prenorm_gain,
    midnorm_gain,
):
    z_size = lax.axis_size("z")
    here_x = lax.axis_index("x")
    devices = 8 * z_size
    micro, local_rows, width = tokens.shape
    flat_rows = micro * local_rows
    sends = local_rows // devices
    group_rows = 4 * local_rows
    all_rows = micro * group_rows
    scale = 1.0 / math.sqrt(HEAD_SIZE)
    query_cols = query_weight.shape[1]
    kv_cols = key_projection_weight.shape[1]
    query_local = query_cols // HEAD_SIZE
    kv_local = kv_cols // HEAD_SIZE
    per_group = query_local // kv_local
    fused_cols = query_cols + 2 * kv_cols
    shard_rows = query_weight.shape[0]
    hidden_cols = gate_weight.shape[1]
    block = hidden_cols // (2 * z_size)
    piece = block // CHUNKS
    chunk_cols = z_size * piece
    everywhere = ("z", "x", "y", "c")

    rank = jnp.sum(
        (token_slots[:, None, :] < token_slots[:, :, None]).astype(jnp.int32), axis=2
    )
    order = (
        (rank // sends) * (micro * sends)
        + jnp.arange(micro, dtype=jnp.int32)[:, None] * sends
        + rank % sends
    ).reshape(flat_rows)
    places = jnp.arange(flat_rows, dtype=jnp.int32)
    to_send = (places[:, None] == order[None, :]).astype(BF16)
    local_slot = (token_slots % local_rows).reshape(flat_rows)
    sent_slots = jnp.sum(
        jnp.where(places[:, None] == order[None, :], local_slot[None, :], 0), axis=1
    )

    def exchange(rows):
        return lax.all_to_all(
            rows.reshape((devices, micro * sends) + rows.shape[1:]),
            everywhere,
            split_axis=0,
            concat_axis=0,
            tiled=True,
        ).reshape(rows.shape)

    arrived_slots = exchange(sent_slots)
    arrived_tokens = exchange(mm(to_send, tokens.reshape(flat_rows, width)).astype(BF16))
    arrived_micro = (places // sends) % micro
    to_place = (
        (arrived_slots + arrived_micro * local_rows)[:, None] == places[None, :]
    ).astype(BF16)

    gains = gather_gains(jnp.stack([prenorm_gain, midnorm_gain])).astype(F32)
    gain_one, gain_two = gains[0:1], gains[1:2]

    fused_shard = jnp.concatenate(
        [query_weight, key_projection_weight, value_projection_weight], axis=1
    )
    fused_pair = in_order(here_x, fused_shard, lax.ppermute(fused_shard, "x", SWAP))
    output_pair = in_order(here_x, output_weight, lax.ppermute(output_weight, "x", SWAP))
    fused_full = gather_z(fused_pair).reshape(width, fused_cols)
    output_full = gather_z(output_pair).reshape(query_cols, width)

    def by_parity(weight):
        blocks = weight.reshape(shard_rows, z_size, 2, CHUNKS, piece)
        return (blocks[:, :, 0], blocks[:, :, 1])

    gate_parts, up_parts = by_parity(gate_weight), by_parity(up_weight)
    ff_shards = []
    for chunk in range(CHUNKS):
        even, odd = [
            jnp.concatenate(
                [
                    parts[parity][:, :, chunk].reshape(shard_rows, chunk_cols)
                    for parts in (gate_parts, up_parts)
                ],
                axis=1,
            )
            for parity in range(2)
        ]
        kept = jnp.where(here_x == 0, even, odd)
        leaving = jnp.where(here_x == 0, odd, even)
        ff_shards.append(
            (
                in_order(here_x, kept, lax.ppermute(leaving, "x", SWAP)),
                down_weight[chunk * piece : (chunk + 1) * piece],
            )
        )

    inputs = outer_sum(to_place, arrived_tokens)
    first_scale = rms_scale(inputs)
    first_normed = (inputs * first_scale * gain_one).astype(BF16)
    normed_all = gather_tensor(first_normed.reshape(micro, local_rows, width)).reshape(
        all_rows, width
    )
    fused_heads = mm(normed_all, fused_full)
    saved = []
    heads_list = []
    for index in range(micro):
        segment, positions = sequence_layout(lengths[index, 0], group_rows)
        cosine, sine = rope_tables(positions, HEAD_SIZE)
        row_ids = jnp.arange(group_rows, dtype=jnp.int32)
        allowed = (segment[:, None] == segment[None, :]) & (row_ids[:, None] >= row_ids[None, :])
        mine = fused_heads[index * group_rows : (index + 1) * group_rows]
        query = rotate(
            mine[:, :query_cols].reshape(group_rows, query_local, HEAD_SIZE), cosine, sine
        ).astype(BF16)
        query = query.reshape(group_rows, kv_local, per_group, HEAD_SIZE)
        key = rotate(
            mine[:, query_cols : query_cols + kv_cols].reshape(group_rows, kv_local, HEAD_SIZE),
            cosine,
            sine,
        ).astype(BF16)
        value = (
            mine[:, query_cols + kv_cols :].reshape(group_rows, kv_local, HEAD_SIZE).astype(BF16)
        )
        heads, log_totals = attend_forward(query, key, value, allowed, scale)
        heads_list.append(heads.reshape(group_rows, query_cols))
        saved.append((query, key, value, log_totals, allowed, cosine, sine))
    heads_flat = jnp.concatenate(heads_list)
    attended = reduce_tensor(
        mm(heads_flat, output_full).astype(BF16).reshape(micro, 4, local_rows, width)
    ).reshape(flat_rows, width)
    residual = inputs + attended

    second_scale = rms_scale(residual)
    normed_two = (residual * second_scale * gain_two).astype(BF16)
    normed_two_all = gather_eight(normed_two)
    arrived_cot = exchange(mm(to_send, cotangent.reshape(flat_rows, width)).astype(BF16))
    cot_rows = outer_sum(to_place, arrived_cot).astype(BF16)
    cot_all = gather_eight(cot_rows)

    out_sum = 0.0
    d_normed_sum = 0.0
    gate_kept, gate_moved, down_grads = [], [], []
    for chunk in range(CHUNKS):
        gate_up = gather_z(ff_shards[chunk][0]).reshape(width, 2 * chunk_cols)
        down = gather_z(ff_shards[chunk][1]).reshape(chunk_cols, width)
        both = mm(normed_two_all, gate_up)
        gate, upward = both[:, :chunk_cols], both[:, chunk_cols:]
        sigmoid = jax.nn.sigmoid(gate)
        silu = gate * sigmoid
        hidden = (silu * upward).astype(BF16)
        d_hidden = times_transposed(cot_all, down)
        d_gate = (d_hidden * upward * sigmoid * (1.0 + gate * (1.0 - sigmoid))).astype(BF16)
        d_upward = (d_hidden * silu).astype(BF16)
        d_both = jnp.concatenate([d_gate, d_upward], axis=1)
        down_part = outer_sum(hidden, cot_all).astype(BF16)
        down_grads.append(reduce_z(down_part.reshape(z_size, piece, width)))
        both_part = outer_sum(normed_two_all, d_both).astype(BF16)
        both_sum = reduce_z(both_part.reshape(z_size, 2, shard_rows, 2 * chunk_cols))
        gate_kept.append(take(both_sum, here_x))
        gate_moved.append(
            lax.ppermute(take(both_sum, 1 - here_x).astype(BF16), "x", SWAP).astype(F32)
        )
        out_sum = out_sum + mm(hidden, down)
        d_normed_sum = d_normed_sum + times_transposed(d_both, gate_up)
    down_grad = jnp.concatenate(down_grads, axis=0)
    kept = jnp.stack(gate_kept).reshape(CHUNKS, shard_rows, 2, z_size, piece)
    moved = jnp.stack(gate_moved).reshape(CHUNKS, shard_rows, 2, z_size, piece)
    parity = in_order(here_x, kept, moved)
    gate_grad, up_grad = jnp.transpose(parity, (3, 2, 4, 0, 1, 5)).reshape(
        2, shard_rows, hidden_cols
    )

    layer_rows = residual + reduce_eight(out_sum.astype(BF16))
    d_normed_two = reduce_eight(d_normed_sum.astype(BF16))
    d_through, d_gain_two = norm_backward(residual, second_scale, gain_two, d_normed_two)
    d_residual = cot_rows.astype(F32) + d_through

    d_residual_all = gather_tensor(
        d_residual.astype(BF16).reshape(micro, local_rows, width)
    ).reshape(all_rows, width)
    d_heads_all = times_transposed(d_residual_all, output_full).astype(BF16)
    output_part = outer_sum(heads_flat, d_residual_all).astype(BF16)
    d_fused_list = []
    for index in range(micro):
        query, key, value, log_totals, allowed, cosine, sine = saved[index]
        d_heads = d_heads_all[index * group_rows : (index + 1) * group_rows].reshape(query.shape)
        d_query, d_key, d_value = attend_backward(
            query, key, value, d_heads, log_totals, allowed, scale
        )
        d_query = rotate(
            d_query.reshape(group_rows, query_local, HEAD_SIZE), cosine, -sine
        ).reshape(group_rows, query_cols)
        d_key = rotate(d_key, cosine, -sine).reshape(group_rows, kv_cols)
        d_fused_list.append(
            jnp.concatenate([d_query, d_key, d_value.reshape(group_rows, kv_cols)], axis=1).astype(
                BF16
            )
        )
    d_fused = jnp.concatenate(d_fused_list)
    d_normed_one = reduce_tensor(
        times_transposed(d_fused, fused_full).astype(BF16).reshape(micro, 4, local_rows, width)
    ).reshape(flat_rows, width)
    fused_part = outer_sum(normed_all, d_fused).astype(BF16)

    def reduce_data(part):
        part = part.reshape((z_size, 2, part.shape[0] // (2 * z_size), part.shape[1]))
        arrived = lax.ppermute(take(part, 1 - here_x, 1), "x", SWAP)
        return reduce_z((take(part, here_x, 1).astype(F32) + arrived.astype(F32)).astype(BF16))

    output_grad = reduce_data(output_part)
    fused_grad = reduce_data(fused_part)
    d_first, d_gain_one = norm_backward(inputs, first_scale, gain_one, d_normed_one)
    input_grads = (d_residual + d_first).astype(BF16)
    gain_grads = reduce_gains(jnp.stack([d_gain_one, d_gain_two]))

    def send_back(rows):
        returned = exchange(mm(to_place, rows).astype(BF16))
        return outer_sum(to_send, returned).astype(BF16).reshape(micro, local_rows, width)

    return (
        send_back(layer_rows.astype(BF16)),
        send_back(input_grads),
        fused_grad[:, :query_cols],
        fused_grad[:, query_cols : query_cols + kv_cols],
        fused_grad[:, query_cols + kv_cols :],
        output_grad,
        gate_grad,
        up_grad,
        down_grad,
        gain_grads[0],
        gain_grads[1],
    )


def solution(mesh):
    z_size = mesh.shape["dp"] // 2
    fine = Mesh(mesh.devices.reshape(z_size, 2, 2, 2), ("z", "x", "y", "c"))
    dp, tensor = ("z", "x"), ("y", "c")
    rows, columns, stacked = P(None, dp + tensor, None), P(dp, tensor), P(tensor + dp, None)
    return jax.shard_map(
        body,
        mesh=fine,
        in_specs=(
            rows,
            rows,
            P(None, dp + tensor),
            P(None, dp, None),
            columns,
            columns,
            columns,
            stacked,
            columns,
            columns,
            stacked,
            P(dp),
            P(dp),
        ),
        out_specs=(
            rows,
            rows,
            columns,
            columns,
            columns,
            stacked,
            columns,
            columns,
            stacked,
            P(dp),
            P(dp),
        ),
        check_vma=False,
    )
```

```python
import functools
import math

import jax
import jax.numpy as jnp
from jax import lax
from jax.experimental import pallas as pl
from jax.experimental.layout import Layout, with_layout_constraint
from jax.experimental.pallas import tpu as pltpu
from jax.sharding import Mesh, PartitionSpec as P

HEAD_SIZE = 256
EPSILON = 1e-06
ROPE_BASE = 1000042.0
NEGATIVE = -1e30
LONGEST = 256
CHUNKS = 2
F32 = jnp.float32
BF16 = jnp.bfloat16

SWAP = [(0, 1), (1, 0)]
DIAGONAL = [(0, 3), (3, 0), (1, 2), (2, 1)]
Z_NEAR = [(0, 1), (1, 0), (2, 3), (3, 2)]
Z_FAR = [(0, 2), (2, 0), (1, 3), (3, 1)]
Z_ACROSS = [(0, 3), (3, 0), (1, 2), (2, 1)]


def rms_scale(values):
    return lax.rsqrt(jnp.mean(values * values, axis=-1, keepdims=True) + EPSILON)


def rope_tables(positions, head):
    half = head // 2
    frequency = jnp.exp(jnp.arange(half, dtype=F32) * (-2.0 * math.log(ROPE_BASE) / head))
    angles = positions.astype(F32)[:, None] * frequency[None, :]
    return (jnp.cos(angles), jnp.sin(angles))


def rotate(head, cosine, sine):
    half = head.shape[-1] // 2
    first, second = head[:, :half], head[:, half:]
    return jnp.concatenate(
        [first * cosine - second * sine, second * cosine + first * sine], axis=-1
    )


def sequence_layout(lens, total):
    rows = jnp.arange(total, dtype=jnp.int32)
    ends = jnp.cumsum(lens)
    segment = jnp.sum((rows[:, None] >= ends[None, :]).astype(jnp.int32), axis=1)
    starts = ends - lens
    which = segment[:, None] == jnp.arange(lens.shape[0], dtype=jnp.int32)[None, :]
    begin = jnp.sum(jnp.where(which, starts[None, :], 0), axis=1)
    return (segment, rows - begin)


def mm(left, right):
    return jnp.dot(left, right, preferred_element_type=F32)


def outer_sum(left, right):
    return lax.dot_general(left, right, (((0,), (0,)), ((), ())), preferred_element_type=F32)


def times_transposed(left, right):
    return lax.dot_general(left, right, (((1,), (1,)), ((), ())), preferred_element_type=F32)


def masked_scores(query, key, seg_query, seg_key, row_start, key_start):
    scores = times_transposed(query, key) * (1.0 / math.sqrt(HEAD_SIZE))
    rows = row_start + lax.broadcasted_iota(jnp.int32, scores.shape, 0)
    keys = key_start + lax.broadcasted_iota(jnp.int32, scores.shape, 1)
    allowed = (seg_query == seg_key) & (rows >= keys)
    scores = jnp.where(allowed, scores, NEGATIVE)
    expo = jnp.exp(scores - jnp.max(scores, axis=-1, keepdims=True))
    return expo / jnp.sum(expo, axis=-1, keepdims=True)


def query_blocks(total):
    size = LONGEST
    return [
        (start, start + size, max(0, start - LONGEST)) for start in range(0, total, size)
    ]


def place_rows(place_ref, piece_refs, rows_ref):
    here = place_ref[0]
    size = piece_refs[0].shape[1]
    for step, piece in enumerate(piece_refs):
        start = pl.multiple_of(jnp.bitwise_xor(here, step) * size, size)
        rows_ref[pl.ds(start, size), :] = piece[0]


def spread_rows(place_ref, rows_ref, kept_ref, sent_ref):
    here = place_ref[0]
    size = kept_ref.shape[2]
    for step in range(4):
        start = pl.multiple_of(jnp.bitwise_xor(here, step) * size, size)
        out_ref = sent_ref if step % 2 else kept_ref
        out_ref[step // 2, 0] = rows_ref[pl.ds(start, size), :]


def attention_forward_kernel(
    query_heads,
    place_ref,
    piece0,
    piece1,
    piece2,
    piece3,
    own_ref,
    other_ref,
    output_ref,
    cosine_ref,
    sine_ref,
    seg_query_ref,
    seg_key_ref,
    normed_ref,
    fused_ref,
    heads_ref,
    kept_ref,
    sent_ref,
    rows_ref,
    sums_ref,
):
    place_rows(place_ref, (piece0, piece1, piece2, piece3), rows_ref)
    normed_ref[...] = rows_ref[...]
    half = own_ref.shape[0]
    fused = mm(rows_ref[:, :half], own_ref[...]) + mm(rows_ref[:, half:], other_ref[...])
    cosine, sine = cosine_ref[0], sine_ref[0]
    total = rows_ref.shape[0]
    kv_heads = fused.shape[1] // HEAD_SIZE - query_heads
    for head in range(query_heads + kv_heads // 2):
        columns = slice(head * HEAD_SIZE, (head + 1) * HEAD_SIZE)
        fused_ref[:, columns] = rotate(fused[:, columns], cosine, sine).astype(BF16)
    first_value = (query_heads + kv_heads // 2) * HEAD_SIZE
    fused_ref[:, first_value:] = fused[:, first_value:].astype(BF16)
    per_group = 2 * query_heads // kv_heads
    for head in range(query_heads):
        group = head // per_group
        columns = slice(head * HEAD_SIZE, (head + 1) * HEAD_SIZE)
        at_key = (query_heads + group) * HEAD_SIZE
        at_value = first_value + group * HEAD_SIZE
        for start, stop, low in query_blocks(total):
            probs = masked_scores(
                fused_ref[start:stop, columns],
                fused_ref[low:stop, at_key : at_key + HEAD_SIZE],
                seg_query_ref[0, start:stop],
                seg_key_ref[0, :, low:stop],
                start,
                low,
            )
            heads_ref[start:stop, columns] = mm(
                probs.astype(BF16), fused_ref[low:stop, at_value : at_value + HEAD_SIZE]
            ).astype(BF16)
    sums_ref[...] = mm(heads_ref[...], output_ref[...]).astype(BF16)
    spread_rows(place_ref, sums_ref, kept_ref, sent_ref)


def attention_backward_kernel(
    query_heads,
    block_rows,
    place_ref,
    piece0,
    piece1,
    piece2,
    piece3,
    own_ref,
    other_ref,
    output_ref,
    cosine_ref,
    sine_ref,
    seg_query_ref,
    seg_key_ref,
    normed_ref,
    fused_ref,
    heads_ref,
    kept_ref,
    sent_ref,
    fused_kept_ref,
    fused_sent_ref,
    output_kept_ref,
    output_sent_ref,
    rows_ref,
    sums_ref,
    d_heads_ref,
    d_fused_ref,
    d_key_ref,
    d_value_ref,
    fused_acc,
    output_acc,
):
    index = pl.program_id(0)
    scale = 1.0 / math.sqrt(HEAD_SIZE)
    place_rows(place_ref, (piece0, piece1, piece2, piece3), rows_ref)
    d_heads_ref[...] = times_transposed(rows_ref[...], output_ref[...]).astype(BF16)
    cosine, sine = cosine_ref[0], sine_ref[0]
    total = rows_ref.shape[0]
    kv_heads = fused_ref.shape[1] // HEAD_SIZE - query_heads
    first_value = (query_heads + kv_heads // 2) * HEAD_SIZE
    per_group = 2 * query_heads // kv_heads
    for group in range(kv_heads // 2):
        at_key = (query_heads + group) * HEAD_SIZE
        at_value = first_value + group * HEAD_SIZE
        d_key_ref[...] = jnp.zeros_like(d_key_ref)
        d_value_ref[...] = jnp.zeros_like(d_value_ref)
        for head in range(group * per_group, (group + 1) * per_group):
            columns = slice(head * HEAD_SIZE, (head + 1) * HEAD_SIZE)
            for start, stop, low in query_blocks(total):
                query = fused_ref[start:stop, columns]
                key = fused_ref[low:stop, at_key : at_key + HEAD_SIZE]
                value = fused_ref[low:stop, at_value : at_value + HEAD_SIZE]
                d_heads = d_heads_ref[start:stop, columns]
                probs = masked_scores(
                    query,
                    key,
                    seg_query_ref[0, start:stop],
                    seg_key_ref[0, :, low:stop],
                    start,
                    low,
                )
                d_probs = times_transposed(d_heads, value)
                delta = jnp.sum(probs * d_probs, axis=-1, keepdims=True)
                d_scores = (probs * (d_probs - delta)).astype(BF16)
                d_query = mm(d_scores, key) * scale
                d_fused_ref[start:stop, columns] = rotate(
                    d_query, cosine[start:stop], -sine[start:stop]
                ).astype(BF16)
                d_key_ref[low:stop] += outer_sum(d_scores, query) * scale
                d_value_ref[low:stop] += outer_sum(probs.astype(BF16), d_heads)
        d_fused_ref[:, at_key : at_key + HEAD_SIZE] = rotate(
            d_key_ref[...], cosine, -sine
        ).astype(BF16)
        d_fused_ref[:, at_value : at_value + HEAD_SIZE] = d_value_ref[...].astype(BF16)
    half = own_ref.shape[0]
    sums_ref[:, :half] = times_transposed(d_fused_ref[...], own_ref[...]).astype(BF16)
    sums_ref[:, half:] = times_transposed(d_fused_ref[...], other_ref[...]).astype(BF16)
    spread_rows(place_ref, sums_ref, kept_ref, sent_ref)
    fused_part = outer_sum(normed_ref[...], d_fused_ref[...])
    output_part = outer_sum(heads_ref[...], rows_ref[...])

    @pl.when(index == 0)
    def _():
        fused_acc[...] = fused_part
        output_acc[...] = output_part

    @pl.when(index > 0)
    def _():
        fused_acc[...] += fused_part
        output_acc[...] += output_part

    @pl.when(index == pl.num_programs(0) - 1)
    def _():
        fused_kept_ref[...] = fused_acc[:half].astype(BF16)
        fused_sent_ref[...] = fused_acc[half:].astype(BF16)
        here_x = place_ref[1]
        size = block_rows
        for step in range(output_acc.shape[0] // (2 * size)):
            kept = pl.multiple_of((2 * step + here_x) * size, size)
            sent = pl.multiple_of((2 * step + 1 - here_x) * size, size)
            rows = slice(step * size, (step + 1) * size)
            output_kept_ref[rows] = output_acc[pl.ds(kept, size), :].astype(BF16)
            output_sent_ref[rows] = output_acc[pl.ds(sent, size), :].astype(BF16)


def whole_spec(shape):
    zeros = (0,) * len(shape)
    return pl.BlockSpec(shape, lambda *_: zeros, pipeline_mode=pl.Buffered(1))


def attention_specs(pieces, own, other, output_full, tables, segments):
    micro, rows, width = pieces[0].shape
    total = 4 * rows
    half = tables[0].shape[-1]
    return (
        [pl.BlockSpec(memory_space=pltpu.SMEM)]
        + [pl.BlockSpec((1, rows, width), lambda m: (m, 0, 0))] * 4
        + [whole_spec(own.shape), whole_spec(other.shape), whole_spec(output_full.shape)]
        + [pl.BlockSpec((1, total, half), lambda m: (m, 0, 0))] * 2
        + [
            pl.BlockSpec((1, total, 1), lambda m: (m, 0, 0)),
            pl.BlockSpec((1, 1, total), lambda m: (m, 0, 0)),
        ]
    )


def attention_forward(place, pieces, own, other, output_full, tables, segments):
    micro, rows, width = pieces[0].shape
    total = 4 * rows
    query_cols, fused_cols = output_full.shape[0], own.shape[1]

    def by_micro(columns):
        return pl.BlockSpec((total, columns), lambda m: (m, 0))

    return pl.pallas_call(
        functools.partial(attention_forward_kernel, query_cols // HEAD_SIZE),
        grid=(micro,),
        in_specs=attention_specs(pieces, own, other, output_full, tables, segments),
        out_specs=[
            by_micro(width),
            by_micro(fused_cols),
            by_micro(query_cols),
            pl.BlockSpec((2, 1, rows, width), lambda m: (0, m, 0, 0)),
            pl.BlockSpec((2, 1, rows, width), lambda m: (0, m, 0, 0)),
        ],
        out_shape=[
            jax.ShapeDtypeStruct((micro * total, width), BF16),
            jax.ShapeDtypeStruct((micro * total, fused_cols), BF16),
            jax.ShapeDtypeStruct((micro * total, query_cols), BF16),
            jax.ShapeDtypeStruct((2, micro, rows, width), BF16),
            jax.ShapeDtypeStruct((2, micro, rows, width), BF16),
        ],
        scratch_shapes=[pltpu.VMEM((total, width), BF16), pltpu.VMEM((total, width), BF16)],
        compiler_params=pltpu.CompilerParams(vmem_limit_bytes=56 << 20),
    )(place, *pieces, own, other, output_full, *tables, *segments)


def attention_backward(
    place, pieces, own, other, output_full, tables, segments, normed, fused, heads, block_rows
):
    micro, rows, width = pieces[0].shape
    total = 4 * rows
    query_cols, fused_cols = output_full.shape[0], own.shape[1]

    def by_micro(columns):
        return pl.BlockSpec((total, columns), lambda m: (m, 0))

    return pl.pallas_call(
        functools.partial(attention_backward_kernel, query_cols // HEAD_SIZE, block_rows),
        grid=(micro,),
        in_specs=attention_specs(pieces, own, other, output_full, tables, segments)
        + [by_micro(width), by_micro(fused_cols), by_micro(query_cols)],
        out_specs=[
            pl.BlockSpec((2, 1, rows, width), lambda m: (0, m, 0, 0)),
            pl.BlockSpec((2, 1, rows, width), lambda m: (0, m, 0, 0)),
            whole_spec((width // 2, fused_cols)),
            whole_spec((width // 2, fused_cols)),
            whole_spec((query_cols // 2, width)),
            whole_spec((query_cols // 2, width)),
        ],
        out_shape=[
            jax.ShapeDtypeStruct((2, micro, rows, width), BF16),
            jax.ShapeDtypeStruct((2, micro, rows, width), BF16),
            jax.ShapeDtypeStruct((width // 2, fused_cols), BF16),
            jax.ShapeDtypeStruct((width // 2, fused_cols), BF16),
            jax.ShapeDtypeStruct((query_cols // 2, width), BF16),
            jax.ShapeDtypeStruct((query_cols // 2, width), BF16),
        ],
        scratch_shapes=[
            pltpu.VMEM((total, width), BF16),
            pltpu.VMEM((total, width), BF16),
            pltpu.VMEM((total, query_cols), BF16),
            pltpu.VMEM((total, fused_cols), BF16),
            pltpu.VMEM((total, HEAD_SIZE), F32),
            pltpu.VMEM((total, HEAD_SIZE), F32),
            pltpu.VMEM((width, fused_cols), F32),
            pltpu.VMEM((query_cols, width), F32),
        ],
        compiler_params=pltpu.CompilerParams(vmem_limit_bytes=60 << 20),
    )(place, *pieces, own, other, output_full, *tables, *segments, normed, fused, heads)


def feedforward_kernel(previous, last, normed_ref, cot_ref, weights_ref, *refs):
    refs = list(refs)
    before = [refs.pop(0) for _ in range(2)] if previous else []
    down_ref = refs.pop()
    hidden_ref, d_both_ref, *sums = refs
    pieces, _, fused = weights_ref.shape
    columns, width = down_ref.shape
    rows, piece = width // pieces, columns // pieces
    index = pl.program_id(0)

    @pl.when(index == 0)
    def _():
        for step in range(pieces):
            for part in range(width // fused):
                start = rows + part * piece
                down_ref[step * piece : (step + 1) * piece, part * fused : (part + 1) * fused] = (
                    weights_ref[step, start : start + piece, :]
                )

    both = mm(normed_ref[:, :rows], weights_ref[0, :rows, :])
    for step in range(1, pieces):
        both = both + mm(normed_ref[:, step * rows : (step + 1) * rows], weights_ref[step, :rows, :])
    gate, upward = both[:, :columns], both[:, columns:]
    sigmoid = 1.0 / (1.0 + jnp.exp(-gate))
    silu = gate * sigmoid
    hidden_ref[...] = (silu * upward).astype(BF16)
    d_hidden = times_transposed(cot_ref[...], down_ref[...])
    d_both_ref[:, :columns] = (
        d_hidden * upward * sigmoid * (1.0 + gate * (1.0 - sigmoid))
    ).astype(BF16)
    d_both_ref[:, columns:] = (d_hidden * silu).astype(BF16)

    def write(out_ref, d_normed_ref):
        out = mm(hidden_ref[...], down_ref[...])
        if previous:
            out = out + before[0][...]
        out_ref[...] = out.astype(out_ref.dtype)
        for step in range(pieces):
            at = slice(step * rows, (step + 1) * rows)
            d_normed = times_transposed(d_both_ref[...], weights_ref[step, :rows, :])
            if previous:
                d_normed = d_normed + before[1][:, at]
            d_normed_ref[:, at] = d_normed.astype(d_normed_ref.dtype)

    if not last:
        write(*sums)
        return

    @pl.when(index < 4)
    def _():
        write(*sums[1::2])

    @pl.when(index >= 4)
    def _():
        write(*sums[0::2])


def feedforward(normed, cot, weights, columns, previous, last):
    rows, width = normed.shape
    size = rows // 8

    def blocks(count):
        return pl.BlockSpec((size, count), lambda i: ((i + 4) % 8, 0))

    if last:
        sums = [
            pl.BlockSpec((size, width), lambda i: (jnp.maximum(i - 4, 0), 0)),
            pl.BlockSpec((size, width), lambda i: (jnp.minimum(i, 3), 0)),
        ] * 2
        shapes = [jax.ShapeDtypeStruct((rows // 2, width), BF16)] * 4
    else:
        sums = [blocks(width)] * 2
        shapes = [jax.ShapeDtypeStruct((rows, width), F32)] * 2
    return pl.pallas_call(
        functools.partial(feedforward_kernel, bool(previous), last),
        grid=(8,),
        in_specs=[blocks(width), blocks(width), whole_spec(weights.shape)]
        + [blocks(width)] * len(previous),
        out_specs=[blocks(columns), blocks(2 * columns)] + sums,
        out_shape=[
            jax.ShapeDtypeStruct((rows, columns), BF16),
            jax.ShapeDtypeStruct((rows, 2 * columns), BF16),
        ]
        + shapes,
        scratch_shapes=[pltpu.VMEM((columns, width), BF16)],
        compiler_params=pltpu.CompilerParams(vmem_limit_bytes=56 << 20),
    )(normed, cot, weights, *previous)


def feedforward_grads_kernel(normed_ref, d_both_ref, hidden_ref, cot_ref, out_ref, down_ref):
    index = pl.program_id(0)
    rows, fused = normed_ref.shape[1], d_both_ref.shape[1]
    piece = down_ref.shape[0] // pl.num_programs(0)

    @pl.when(index == 0)
    def _():
        down_ref[...] = outer_sum(hidden_ref[...], cot_ref[...]).astype(BF16)

    out_ref[0, :rows, :] = outer_sum(normed_ref[...], d_both_ref[...]).astype(BF16)
    mine = down_ref[pl.ds(pl.multiple_of(index * piece, piece), piece), :]
    for part in range(down_ref.shape[1] // fused):
        start = rows + part * piece
        out_ref[0, start : start + piece, :] = mine[:, part * fused : (part + 1) * fused]


def feedforward_grads(normed, d_both, hidden, cot, pieces):
    rows, width = normed.shape
    columns = hidden.shape[1]
    fused = d_both.shape[1]
    out_rows = width // pieces + (columns // pieces) * (width // fused)
    return pl.pallas_call(
        feedforward_grads_kernel,
        grid=(pieces,),
        in_specs=[
            pl.BlockSpec((rows, width // pieces), lambda i: (0, i)),
            whole_spec(d_both.shape),
            whole_spec(hidden.shape),
            whole_spec(cot.shape),
        ],
        out_specs=pl.BlockSpec((1, out_rows, fused), lambda i: (i, 0, 0)),
        out_shape=jax.ShapeDtypeStruct((pieces, out_rows, fused), BF16),
        scratch_shapes=[pltpu.VMEM((columns, width), BF16)],
        compiler_params=pltpu.CompilerParams(vmem_limit_bytes=56 << 20),
    )(normed, d_both, hidden, cot)


def assemble_kernel(pieces, place_ref, *refs):
    inputs, outputs = refs[:-2], refs[-2:]
    here_x = place_ref[1]
    chunks = len(inputs) // 2
    half = inputs[0].shape[1] // 2
    size = half // pieces
    for which, out_ref in enumerate(outputs):
        for step in range(pieces):
            columns = slice(which * half + step * size, which * half + (step + 1) * size)
            own = [inputs[2 * chunk][:, columns].astype(F32) for chunk in range(chunks)]
            moved = [inputs[2 * chunk + 1][:, columns].astype(F32) for chunk in range(chunks)]
            even = [jnp.where(here_x == 0, a, b) for a, b in zip(own, moved)]
            odd = [jnp.where(here_x == 0, b, a) for a, b in zip(own, moved)]
            span = 2 * chunks * size
            out_ref[:, step * span : (step + 1) * span] = jnp.concatenate(even + odd, axis=1)


def assemble(place, inputs, pieces, columns):
    rows, width = inputs[0].shape
    size = min(rows, 64)
    return pl.pallas_call(
        functools.partial(assemble_kernel, pieces),
        grid=(rows // size,),
        in_specs=[pl.BlockSpec(memory_space=pltpu.SMEM)]
        + [pl.BlockSpec((size, width), lambda i: (i, 0))] * len(inputs),
        out_specs=[pl.BlockSpec((size, columns), lambda i: (i, 0))] * 2,
        out_shape=[jax.ShapeDtypeStruct((rows, columns), F32)] * 2,
    )(place, *inputs)


def norm_backward(values, scale, gain, d_normed):
    weighted = d_normed * gain
    d_values = scale * weighted - values * scale * scale * scale * jnp.mean(
        weighted * values, axis=-1, keepdims=True
    )
    return (d_values, jnp.sum(d_normed * values * scale, axis=0))


def take(array, index, axis=0):
    return lax.dynamic_index_in_dim(array, index, axis, keepdims=False)


def choose(position, own, other):
    return [jnp.where(position == 0, own, other), jnp.where(position == 0, other, own)]


def in_order(position, own, other, axis=0):
    return jnp.stack(choose(position, own, other), axis=axis)


def rows_major(array):
    return with_layout_constraint(array, Layout(major_to_minor=tuple(range(array.ndim))))


def gather_z(piece):
    return rows_major(lax.all_gather(rows_major(piece), "z", axis=0))


def reduce_z(parts):
    return lax.psum_scatter(parts, "z", scatter_dimension=0)


def tie(*values):
    return lax.optimization_barrier(values)


def swap_blocks(rows, size, here):
    blocks = []
    for start in range(0, rows.shape[1], 2 * size):
        first, second = rows[:, start : start + size], rows[:, start + size : start + 2 * size]
        blocks += choose(here, first, second)
    return blocks


def gather_tensor(rows):
    beside = lax.ppermute(rows, "y", SWAP)
    return (
        rows,
        lax.ppermute(rows, "c", SWAP),
        beside,
        lax.ppermute(beside, "c", SWAP),
    )


def reduce_tensor(kept, sent):
    arrived = lax.ppermute(sent, "c", SWAP).astype(F32)
    moved = (kept[1].astype(F32) + arrived[1]).astype(BF16)
    return kept[0].astype(F32) + arrived[0] + lax.ppermute(moved, "y", SWAP).astype(F32)


def gather_planes(rows):
    return (
        rows,
        lax.ppermute(rows, "x", SWAP),
        lax.ppermute(rows, "y", SWAP),
        lax.ppermute(rows, ("x", "y"), DIAGONAL),
    )


def join_planes(planes):
    return jnp.concatenate(planes + tuple(lax.ppermute(plane, "c", SWAP) for plane in planes))


def reduce_eight(kept, sent):
    kept = kept.reshape((4, kept.shape[0] // 4) + kept.shape[1:])
    arrived = lax.ppermute(sent.reshape(kept.shape), "c", SWAP)
    sums = [kept[step].astype(F32) + arrived[step].astype(F32) for step in range(4)]
    return sums[0], [part.astype(BF16) for part in sums[1:]]


def finish_eight(total, leaving):
    routes = (("x", SWAP), ("y", SWAP), (("x", "y"), DIAGONAL))
    for part, (axes, pairs) in zip(leaving, routes):
        total = total + lax.ppermute(part, axes, pairs).astype(F32)
    return total


def body(
    tokens,
    cotangent,
    token_slots,
    lengths,
    query_weight,
    key_projection_weight,
    value_projection_weight,
    output_weight,
    gate_weight,
    up_weight,
    down_weight,
    prenorm_gain,
    midnorm_gain,
):
    z_size = lax.axis_size("z")
    here_x = lax.axis_index("x")
    devices = 8 * z_size
    micro, local_rows, width = tokens.shape
    flat_rows = micro * local_rows
    sends = local_rows // devices
    group_rows = 4 * local_rows
    query_cols = query_weight.shape[1]
    kv_cols = key_projection_weight.shape[1]
    fused_cols = query_cols + 2 * kv_cols
    shard_rows = query_weight.shape[0]
    hidden_cols = gate_weight.shape[1]
    block = hidden_cols // (2 * z_size)
    piece = block // CHUNKS
    chunk_cols = z_size * piece
    everywhere = ("z", "x", "y", "c")

    rank = jnp.sum(
        (token_slots[:, None, :] < token_slots[:, :, None]).astype(jnp.int32), axis=2
    )
    order = (
        (rank // sends) * (micro * sends)
        + jnp.arange(micro, dtype=jnp.int32)[:, None] * sends
        + rank % sends
    ).reshape(flat_rows)
    places = jnp.arange(flat_rows, dtype=jnp.int32)
    to_send = (places[:, None] == order[None, :]).astype(BF16)
    local_slot = (token_slots % local_rows).reshape(flat_rows)

    def exchange(rows):
        return lax.all_to_all(
            rows.reshape((devices, micro * sends) + rows.shape[1:]),
            everywhere,
            split_axis=0,
            concat_axis=0,
            tiled=True,
        ).reshape(rows.shape)

    gains = jnp.stack([prenorm_gain, midnorm_gain]).reshape(micro * sends, -1)
    leaving = jnp.concatenate(
        [
            tokens.reshape(flat_rows, width),
            jnp.broadcast_to(local_slot[:, None], (flat_rows, gains.shape[1])).astype(BF16),
        ],
        axis=1,
    )
    leaving = jnp.concatenate(
        [mm(to_send, leaving).astype(BF16), jnp.tile(gains, (devices, 1))], axis=1
    )
    fused_shard = jnp.concatenate(
        [query_weight, key_projection_weight, value_projection_weight], axis=1
    )
    leaving, gate_weight, up_weight, down_weight, cotangent = tie(
        leaving, gate_weight, up_weight, down_weight, cotangent
    )
    arrived = exchange(leaving)
    cot_leaving = mm(to_send, cotangent.reshape(flat_rows, width)).astype(BF16)
    cot_leaving, arrived = tie(cot_leaving, arrived)
    arrived_cot = exchange(cot_leaving)
    arrived_tokens = arrived[:, :width]
    arrived_slots = arrived[:, width].astype(jnp.int32)
    arrived_gains = arrived[:, width + gains.shape[1] :].reshape(
        2 * z_size, 4, 2, -1, gains.shape[1]
    )[:, 0]
    gains = jnp.swapaxes(arrived_gains, 0, 1).reshape(2, width).astype(F32)
    gain_one, gain_two = gains[0:1], gains[1:2]
    arrived_micro = (places // sends) % micro
    to_place = (
        (arrived_slots + arrived_micro * local_rows)[:, None] == places[None, :]
    ).astype(BF16)

    def by_parity(weight):
        blocks = weight.reshape(shard_rows, z_size, 2, CHUNKS, piece)
        return (blocks[:, :, 0], blocks[:, :, 1])

    gate_parts, up_parts = by_parity(gate_weight), by_parity(up_weight)
    ff_shards = []
    for chunk in range(CHUNKS):
        even, odd = [
            jnp.concatenate(
                [
                    parts[parity][:, :, chunk].reshape(shard_rows, chunk_cols)
                    for parts in (gate_parts, up_parts)
                ],
                axis=1,
            )
            for parity in range(2)
        ]
        kept = jnp.where(here_x == 0, even, odd)
        leaving = jnp.where(here_x == 0, odd, even)
        down = down_weight[chunk * piece : (chunk + 1) * piece]
        down_parts = [
            down[:, start : start + 2 * chunk_cols] for start in range(0, width, 2 * chunk_cols)
        ]
        ff_shards.append(
            jnp.concatenate(
                choose(here_x, kept, lax.ppermute(leaving, "x", SWAP)) + down_parts
            )
        )

    fused_own = gather_z(fused_shard).reshape(width // 2, fused_cols)
    fused_own, output_weight, arrived_tokens, *ff_shards = tie(
        fused_own, output_weight, arrived_tokens, *ff_shards
    )
    output_own = gather_z(output_weight)
    fused_other = lax.ppermute(fused_own, "x", SWAP)

    inputs = outer_sum(to_place, arrived_tokens)
    first_scale = rms_scale(inputs)
    first_normed = (inputs * first_scale * gain_one).astype(BF16)
    blocks = swap_blocks(first_normed, shard_rows, here_x)
    first_normed = jnp.concatenate(blocks[0::2] + blocks[1::2], axis=1)
    first_shard, first_normed = tie(ff_shards[0], first_normed)
    ff_weights = [gather_z(first_shard)]
    place = jnp.stack([2 * lax.axis_index("y") + lax.axis_index("c"), here_x]).astype(jnp.int32)
    segments, tables = [], []
    for index in range(micro):
        segment, positions = sequence_layout(lengths[index, 0], group_rows)
        segments.append(segment)
        tables.append(rope_tables(positions, HEAD_SIZE))
    segments = jnp.stack(segments)
    segments = (segments[:, :, None], segments[:, None, :])
    tables = tuple(jnp.stack(table) for table in zip(*tables))
    rows_own = first_normed.reshape(micro, local_rows, width)
    rows_beside = lax.ppermute(rows_own, "y", SWAP)
    output_other = lax.ppermute(output_own, "x", SWAP)
    rows_own, rows_beside, fused_other = tie(rows_own, rows_beside, fused_other)
    output_full = in_order(here_x, output_own, output_other, axis=1).reshape(query_cols, width)
    shared = (fused_own, fused_other, output_full, tables, segments)
    pieces = (
        rows_own,
        lax.ppermute(rows_own, "c", SWAP),
        rows_beside,
        lax.ppermute(rows_beside, "c", SWAP),
    )
    normed_all, fused, heads, kept, sent = attention_forward(place, pieces, *shared)
    cot_rows = outer_sum(to_place, arrived_cot).astype(BF16)
    cot_planes = gather_planes(cot_rows)
    kept, sent, *cot_planes = tie(kept, sent, *cot_planes)
    for shard in ff_shards[1:]:
        shard, sent = tie(shard, sent)
        ff_weights.append(gather_z(shard))
    attended = reduce_tensor(kept, sent).reshape(flat_rows, width)
    cot_all = join_planes(tuple(cot_planes))
    residual = inputs + attended

    second_scale = rms_scale(residual)
    normed_two = (residual * second_scale * gain_two).astype(BF16)
    normed_two_all = join_planes(gather_planes(normed_two))

    previous = ()
    gate_kept, gate_moved, down_grads = [], [], []
    for chunk in range(CHUNKS):
        hidden, d_both, *previous = feedforward(
            normed_two_all, cot_all, ff_weights[chunk], chunk_cols, previous, chunk == CHUNKS - 1
        )
        part = feedforward_grads(normed_two_all, d_both, hidden, cot_all, z_size)
        if chunk == CHUNKS - 1:
            d_own, d_leaving = reduce_eight(*previous[2:])
            part, d_own = tie(part, d_own)
        total = reduce_z(part)
        own, other = choose(here_x, total[:shard_rows], total[shard_rows : 2 * shard_rows])
        gate_kept.append(own)
        gate_moved.append(other)
        down_grads.append(
            jnp.concatenate(
                [
                    total[start : start + piece]
                    for start in range(2 * shard_rows, total.shape[0], piece)
                ],
                axis=1,
            )
        )
    down_grad = jnp.concatenate(down_grads, axis=0).astype(F32)

    d_normed_two = finish_eight(d_own, d_leaving)
    d_through, d_gain_two = norm_backward(residual, second_scale, gain_two, d_normed_two)
    d_residual = cot_rows.astype(F32) + d_through

    pieces = gather_tensor(d_residual.astype(BF16).reshape(micro, local_rows, width))
    out_own, out_leaving = reduce_eight(*previous[:2])
    *pieces, out_own = tie(*pieces, out_own)
    out_over_x = lax.ppermute(jnp.stack([out_leaving[0], out_leaving[2]]), "x", SWAP)
    kept, sent, *weight_parts = attention_backward(
        place, pieces, *shared, normed_all, fused, heads, output_weight.shape[0]
    )
    kept, sent, out_over_x = tie(kept, sent, out_over_x)
    out_over_y = (out_leaving[1].astype(F32) + out_over_x[1].astype(F32)).astype(BF16)
    layer_rows = (
        residual
        + (out_own + out_over_x[0].astype(F32))
        + lax.ppermute(out_over_y, "y", SWAP).astype(F32)
    )
    d_normed_one = reduce_tensor(kept, sent).reshape(flat_rows, width)
    swapped = swap_blocks(
        jnp.concatenate(
            [
                d_normed_one[:, side * (width // 2) + start : side * (width // 2) + start + shard_rows]
                for start in range(0, width // 2, shard_rows)
                for side in range(2)
            ],
            axis=1,
        ),
        shard_rows,
        here_x,
    )
    d_normed_one = jnp.concatenate(swapped, axis=1)

    def reduce_x(kept, leaving):
        return (kept.astype(F32) + lax.ppermute(leaving, "x", SWAP).astype(F32)).astype(BF16)

    def reduce_data(total):
        return reduce_z(total.reshape(z_size, -1, total.shape[-1])).astype(F32)

    output_total, fused_sent = tie(reduce_x(*weight_parts[2:]), weight_parts[1])
    fused_total, *gate_moved = tie(reduce_x(weight_parts[0], fused_sent), *gate_moved)
    gate_moved = [lax.ppermute(part, "x", SWAP) for part in gate_moved]
    output_grad = reduce_data(output_total)
    fused_grad = reduce_data(fused_total)
    d_first, d_gain_one = norm_backward(inputs, first_scale, gain_one, d_normed_one)
    input_grads = (d_residual + d_first).astype(BF16)

    gain_grads = jnp.stack([d_gain_one, d_gain_two])
    high = gain_grads.astype(BF16)
    low = (gain_grads - high.astype(F32)).astype(BF16)
    riders = jnp.stack([high, low]).reshape(2, 2, 2 * z_size, 1, shard_rows)
    riders = jnp.broadcast_to(
        jnp.transpose(riders, (2, 3, 0, 1, 4)), (2 * z_size, 4, 2, 2, shard_rows)
    ).reshape(flat_rows, -1)

    back = jnp.concatenate([layer_rows.astype(BF16), input_grads], axis=1)
    returned = exchange(jnp.concatenate([mm(to_place, back).astype(BF16), riders], axis=1))
    returned, *gate_moved = tie(returned, *gate_moved)
    gate_up_grads = assemble(
        place, [part for pair in zip(gate_kept, gate_moved) for part in pair], z_size, hidden_cols
    )
    outputs = outer_sum(to_send, returned[:, : 2 * width]).astype(BF16)
    outputs = outputs.reshape(micro, local_rows, 2 * width)
    gain_grads = jnp.sum(
        returned[:, 2 * width :].astype(F32).reshape(devices, 2, 2, shard_rows), axis=(0, 1)
    )

    return (
        outputs[:, :, :width],
        outputs[:, :, width:],
        fused_grad[:, :query_cols],
        fused_grad[:, query_cols : query_cols + kv_cols],
        fused_grad[:, query_cols + kv_cols :],
        output_grad,
        *gate_up_grads,
        down_grad,
        gain_grads[0],
        gain_grads[1],
    )


def solution(mesh):
    z_size = mesh.shape["dp"] // 2
    fine = Mesh(mesh.devices.reshape(z_size, 2, 2, 2), ("z", "x", "y", "c"))
    dp, tensor = ("z", "x"), ("y", "c")
    rows, columns, stacked = P(None, dp + tensor, None), P(dp, tensor), P(tensor + dp, None)
    return jax.shard_map(
        body,
        mesh=fine,
        in_specs=(
            rows,
            rows,
            P(None, dp + tensor),
            P(None, dp, None),
            columns,
            columns,
            columns,
            stacked,
            columns,
            columns,
            stacked,
            P(dp),
            P(dp),
        ),
        out_specs=(
            rows,
            rows,
            columns,
            columns,
            columns,
            stacked,
            columns,
            columns,
            stacked,
            P(dp),
            P(dp),
        ),
        check_vma=False,
    )
```

```python
import functools
import math

import jax
import jax.numpy as jnp
from jax import lax
from jax.experimental import pallas as pl
from jax.experimental.layout import Layout, with_layout_constraint
from jax.experimental.pallas import tpu as pltpu
from jax.sharding import Mesh, PartitionSpec as P

HEAD_SIZE = 256
EPSILON = 1e-06
ROPE_BASE = 1000042.0
NEGATIVE = -1e30
LONGEST = 256
CHUNKS = 2
F32 = jnp.float32
BF16 = jnp.bfloat16

SWAP = [(0, 1), (1, 0)]
DIAGONAL = [(0, 3), (3, 0), (1, 2), (2, 1)]
Z_NEAR = [(0, 1), (1, 0), (2, 3), (3, 2)]
Z_FAR = [(0, 2), (2, 0), (1, 3), (3, 1)]
Z_ACROSS = [(0, 3), (3, 0), (1, 2), (2, 1)]


def rms_scale(values):
    return lax.rsqrt(jnp.mean(values * values, axis=-1, keepdims=True) + EPSILON)


def rope_tables(positions, head):
    half = head // 2
    frequency = jnp.exp(jnp.arange(half, dtype=F32) * (-2.0 * math.log(ROPE_BASE) / head))
    angles = positions.astype(F32)[:, None] * frequency[None, :]
    return (jnp.cos(angles), jnp.sin(angles))


def rotate(head, cosine, sine):
    half = head.shape[-1] // 2
    first, second = head[:, :half], head[:, half:]
    return jnp.concatenate(
        [first * cosine - second * sine, second * cosine + first * sine], axis=-1
    )


def sequence_layout(lens, total):
    rows = jnp.arange(total, dtype=jnp.int32)
    ends = jnp.cumsum(lens)
    segment = jnp.sum((rows[:, None] >= ends[None, :]).astype(jnp.int32), axis=1)
    starts = ends - lens
    which = segment[:, None] == jnp.arange(lens.shape[0], dtype=jnp.int32)[None, :]
    begin = jnp.sum(jnp.where(which, starts[None, :], 0), axis=1)
    return (segment, rows - begin)


def mm(left, right):
    return jnp.dot(left, right, preferred_element_type=F32)


def outer_sum(left, right):
    return lax.dot_general(left, right, (((0,), (0,)), ((), ())), preferred_element_type=F32)


def times_transposed(left, right):
    return lax.dot_general(left, right, (((1,), (1,)), ((), ())), preferred_element_type=F32)


def masked_scores(query, key, seg_query, seg_key, row_start, key_start):
    scores = times_transposed(query, key) * (1.0 / math.sqrt(HEAD_SIZE))
    rows = row_start + lax.broadcasted_iota(jnp.int32, scores.shape, 0)
    keys = key_start + lax.broadcasted_iota(jnp.int32, scores.shape, 1)
    allowed = (seg_query == seg_key) & (rows >= keys)
    scores = jnp.where(allowed, scores, NEGATIVE)
    expo = jnp.exp(scores - jnp.max(scores, axis=-1, keepdims=True))
    return expo / jnp.sum(expo, axis=-1, keepdims=True)


def query_blocks(total):
    size = LONGEST
    return [
        (start, start + size, max(0, start - LONGEST)) for start in range(0, total, size)
    ]


def place_rows(place_ref, piece_refs, rows_ref):
    here = place_ref[0]
    size = piece_refs[0].shape[1]
    for step, piece in enumerate(piece_refs):
        start = pl.multiple_of(jnp.bitwise_xor(here, step) * size, size)
        rows_ref[pl.ds(start, size), :] = piece[0]


def spread_rows(place_ref, rows_ref, kept_ref, sent_ref):
    here = place_ref[0]
    size = kept_ref.shape[2]
    for step in range(4):
        start = pl.multiple_of(jnp.bitwise_xor(here, step) * size, size)
        out_ref = sent_ref if step % 2 else kept_ref
        out_ref[step // 2, 0] = rows_ref[pl.ds(start, size), :]


def attention_forward_kernel(
    query_heads,
    place_ref,
    piece0,
    piece1,
    piece2,
    piece3,
    own_ref,
    other_ref,
    output_ref,
    cosine_ref,
    sine_ref,
    seg_query_ref,
    seg_key_ref,
    normed_ref,
    fused_ref,
    heads_ref,
    kept_ref,
    sent_ref,
    rows_ref,
    sums_ref,
):
    place_rows(place_ref, (piece0, piece1, piece2, piece3), rows_ref)
    normed_ref[...] = rows_ref[...]
    half = own_ref.shape[0]
    fused = mm(rows_ref[:, :half], own_ref[...]) + mm(rows_ref[:, half:], other_ref[...])
    cosine, sine = cosine_ref[0], sine_ref[0]
    total = rows_ref.shape[0]
    kv_heads = fused.shape[1] // HEAD_SIZE - query_heads
    for head in range(query_heads + kv_heads // 2):
        columns = slice(head * HEAD_SIZE, (head + 1) * HEAD_SIZE)
        fused_ref[:, columns] = rotate(fused[:, columns], cosine, sine).astype(BF16)
    first_value = (query_heads + kv_heads // 2) * HEAD_SIZE
    fused_ref[:, first_value:] = fused[:, first_value:].astype(BF16)
    per_group = 2 * query_heads // kv_heads
    for head in range(query_heads):
        group = head // per_group
        columns = slice(head * HEAD_SIZE, (head + 1) * HEAD_SIZE)
        at_key = (query_heads + group) * HEAD_SIZE
        at_value = first_value + group * HEAD_SIZE
        for start, stop, low in query_blocks(total):
            probs = masked_scores(
                fused_ref[start:stop, columns],
                fused_ref[low:stop, at_key : at_key + HEAD_SIZE],
                seg_query_ref[0, start:stop],
                seg_key_ref[0, :, low:stop],
                start,
                low,
            )
            heads_ref[start:stop, columns] = mm(
                probs.astype(BF16), fused_ref[low:stop, at_value : at_value + HEAD_SIZE]
            ).astype(BF16)
    sums_ref[...] = mm(heads_ref[...], output_ref[...]).astype(BF16)
    spread_rows(place_ref, sums_ref, kept_ref, sent_ref)


def attention_backward_kernel(
    query_heads,
    block_rows,
    place_ref,
    piece0,
    piece1,
    piece2,
    piece3,
    own_ref,
    other_ref,
    output_ref,
    cosine_ref,
    sine_ref,
    seg_query_ref,
    seg_key_ref,
    normed_ref,
    fused_ref,
    heads_ref,
    kept_ref,
    sent_ref,
    fused_kept_ref,
    fused_sent_ref,
    output_kept_ref,
    output_sent_ref,
    rows_ref,
    sums_ref,
    d_heads_ref,
    d_fused_ref,
    d_key_ref,
    d_value_ref,
    fused_acc,
    output_acc,
):
    index = pl.program_id(0)
    scale = 1.0 / math.sqrt(HEAD_SIZE)
    place_rows(place_ref, (piece0, piece1, piece2, piece3), rows_ref)
    d_heads_ref[...] = times_transposed(rows_ref[...], output_ref[...]).astype(BF16)
    cosine, sine = cosine_ref[0], sine_ref[0]
    total = rows_ref.shape[0]
    kv_heads = fused_ref.shape[1] // HEAD_SIZE - query_heads
    first_value = (query_heads + kv_heads // 2) * HEAD_SIZE
    per_group = 2 * query_heads // kv_heads
    for group in range(kv_heads // 2):
        at_key = (query_heads + group) * HEAD_SIZE
        at_value = first_value + group * HEAD_SIZE
        d_key_ref[...] = jnp.zeros_like(d_key_ref)
        d_value_ref[...] = jnp.zeros_like(d_value_ref)
        for head in range(group * per_group, (group + 1) * per_group):
            columns = slice(head * HEAD_SIZE, (head + 1) * HEAD_SIZE)
            for start, stop, low in query_blocks(total):
                query = fused_ref[start:stop, columns]
                key = fused_ref[low:stop, at_key : at_key + HEAD_SIZE]
                value = fused_ref[low:stop, at_value : at_value + HEAD_SIZE]
                d_heads = d_heads_ref[start:stop, columns]
                probs = masked_scores(
                    query,
                    key,
                    seg_query_ref[0, start:stop],
                    seg_key_ref[0, :, low:stop],
                    start,
                    low,
                )
                d_probs = times_transposed(d_heads, value)
                delta = jnp.sum(probs * d_probs, axis=-1, keepdims=True)
                d_scores = (probs * (d_probs - delta)).astype(BF16)
                d_query = mm(d_scores, key) * scale
                d_fused_ref[start:stop, columns] = rotate(
                    d_query, cosine[start:stop], -sine[start:stop]
                ).astype(BF16)
                d_key_ref[low:stop] += outer_sum(d_scores, query) * scale
                d_value_ref[low:stop] += outer_sum(probs.astype(BF16), d_heads)
        d_fused_ref[:, at_key : at_key + HEAD_SIZE] = rotate(
            d_key_ref[...], cosine, -sine
        ).astype(BF16)
        d_fused_ref[:, at_value : at_value + HEAD_SIZE] = d_value_ref[...].astype(BF16)
    half = own_ref.shape[0]
    sums_ref[:, :half] = times_transposed(d_fused_ref[...], own_ref[...]).astype(BF16)
    sums_ref[:, half:] = times_transposed(d_fused_ref[...], other_ref[...]).astype(BF16)
    spread_rows(place_ref, sums_ref, kept_ref, sent_ref)
    fused_part = outer_sum(normed_ref[...], d_fused_ref[...])
    output_part = outer_sum(heads_ref[...], rows_ref[...])

    @pl.when(index == 0)
    def _():
        fused_acc[...] = fused_part
        output_acc[...] = output_part

    @pl.when(index > 0)
    def _():
        fused_acc[...] += fused_part
        output_acc[...] += output_part

    @pl.when(index == pl.num_programs(0) - 1)
    def _():
        fused_kept_ref[...] = fused_acc[:half].astype(BF16)
        fused_sent_ref[...] = fused_acc[half:].astype(BF16)
        here_x = place_ref[1]
        size = block_rows
        for step in range(output_acc.shape[0] // (2 * size)):
            kept = pl.multiple_of((2 * step + here_x) * size, size)
            sent = pl.multiple_of((2 * step + 1 - here_x) * size, size)
            rows = slice(step * size, (step + 1) * size)
            output_kept_ref[rows] = output_acc[pl.ds(kept, size), :].astype(BF16)
            output_sent_ref[rows] = output_acc[pl.ds(sent, size), :].astype(BF16)


def whole_spec(shape):
    zeros = (0,) * len(shape)
    return pl.BlockSpec(shape, lambda *_: zeros, pipeline_mode=pl.Buffered(1))


def attention_specs(pieces, own, other, output_full, tables, segments):
    micro, rows, width = pieces[0].shape
    total = 4 * rows
    half = tables[0].shape[-1]
    return (
        [pl.BlockSpec(memory_space=pltpu.SMEM)]
        + [pl.BlockSpec((1, rows, width), lambda m: (m, 0, 0))] * 4
        + [whole_spec(own.shape), whole_spec(other.shape), whole_spec(output_full.shape)]
        + [pl.BlockSpec((1, total, half), lambda m: (m, 0, 0))] * 2
        + [
            pl.BlockSpec((1, total, 1), lambda m: (m, 0, 0)),
            pl.BlockSpec((1, 1, total), lambda m: (m, 0, 0)),
        ]
    )


def attention_forward(place, pieces, own, other, output_full, tables, segments):
    micro, rows, width = pieces[0].shape
    total = 4 * rows
    query_cols, fused_cols = output_full.shape[0], own.shape[1]

    def by_micro(columns):
        return pl.BlockSpec((total, columns), lambda m: (m, 0))

    return pl.pallas_call(
        functools.partial(attention_forward_kernel, query_cols // HEAD_SIZE),
        grid=(micro,),
        in_specs=attention_specs(pieces, own, other, output_full, tables, segments),
        out_specs=[
            by_micro(width),
            by_micro(fused_cols),
            by_micro(query_cols),
            pl.BlockSpec((2, 1, rows, width), lambda m: (0, m, 0, 0)),
            pl.BlockSpec((2, 1, rows, width), lambda m: (0, m, 0, 0)),
        ],
        out_shape=[
            jax.ShapeDtypeStruct((micro * total, width), BF16),
            jax.ShapeDtypeStruct((micro * total, fused_cols), BF16),
            jax.ShapeDtypeStruct((micro * total, query_cols), BF16),
            jax.ShapeDtypeStruct((2, micro, rows, width), BF16),
            jax.ShapeDtypeStruct((2, micro, rows, width), BF16),
        ],
        scratch_shapes=[pltpu.VMEM((total, width), BF16), pltpu.VMEM((total, width), BF16)],
        compiler_params=pltpu.CompilerParams(vmem_limit_bytes=56 << 20),
    )(place, *pieces, own, other, output_full, *tables, *segments)


def attention_backward(
    place, pieces, own, other, output_full, tables, segments, normed, fused, heads, block_rows
):
    micro, rows, width = pieces[0].shape
    total = 4 * rows
    query_cols, fused_cols = output_full.shape[0], own.shape[1]

    def by_micro(columns):
        return pl.BlockSpec((total, columns), lambda m: (m, 0))

    return pl.pallas_call(
        functools.partial(attention_backward_kernel, query_cols // HEAD_SIZE, block_rows),
        grid=(micro,),
        in_specs=attention_specs(pieces, own, other, output_full, tables, segments)
        + [by_micro(width), by_micro(fused_cols), by_micro(query_cols)],
        out_specs=[
            pl.BlockSpec((2, 1, rows, width), lambda m: (0, m, 0, 0)),
            pl.BlockSpec((2, 1, rows, width), lambda m: (0, m, 0, 0)),
            whole_spec((width // 2, fused_cols)),
            whole_spec((width // 2, fused_cols)),
            whole_spec((query_cols // 2, width)),
            whole_spec((query_cols // 2, width)),
        ],
        out_shape=[
            jax.ShapeDtypeStruct((2, micro, rows, width), BF16),
            jax.ShapeDtypeStruct((2, micro, rows, width), BF16),
            jax.ShapeDtypeStruct((width // 2, fused_cols), BF16),
            jax.ShapeDtypeStruct((width // 2, fused_cols), BF16),
            jax.ShapeDtypeStruct((query_cols // 2, width), BF16),
            jax.ShapeDtypeStruct((query_cols // 2, width), BF16),
        ],
        scratch_shapes=[
            pltpu.VMEM((total, width), BF16),
            pltpu.VMEM((total, width), BF16),
            pltpu.VMEM((total, query_cols), BF16),
            pltpu.VMEM((total, fused_cols), BF16),
            pltpu.VMEM((total, HEAD_SIZE), F32),
            pltpu.VMEM((total, HEAD_SIZE), F32),
            pltpu.VMEM((width, fused_cols), F32),
            pltpu.VMEM((query_cols, width), F32),
        ],
        compiler_params=pltpu.CompilerParams(vmem_limit_bytes=60 << 20),
    )(place, *pieces, own, other, output_full, *tables, *segments, normed, fused, heads)


def feedforward_kernel(previous, last, normed_ref, cot_ref, weights_ref, *refs):
    refs = list(refs)
    before = [refs.pop(0) for _ in range(2)] if previous else []
    down_ref = refs.pop()
    hidden_ref, d_both_ref, *sums = refs
    pieces, _, fused = weights_ref.shape
    columns, width = down_ref.shape
    rows, piece = width // pieces, columns // pieces
    index = pl.program_id(0)

    @pl.when(index == 0)
    def _():
        for step in range(pieces):
            for part in range(width // fused):
                start = rows + part * piece
                down_ref[step * piece : (step + 1) * piece, part * fused : (part + 1) * fused] = (
                    weights_ref[step, start : start + piece, :]
                )

    both = mm(normed_ref[:, :rows], weights_ref[0, :rows, :])
    for step in range(1, pieces):
        both = both + mm(normed_ref[:, step * rows : (step + 1) * rows], weights_ref[step, :rows, :])
    gate, upward = both[:, :columns], both[:, columns:]
    sigmoid = 1.0 / (1.0 + jnp.exp(-gate))
    silu = gate * sigmoid
    hidden_ref[...] = (silu * upward).astype(BF16)
    d_hidden = times_transposed(cot_ref[...], down_ref[...])
    d_both_ref[:, :columns] = (
        d_hidden * upward * sigmoid * (1.0 + gate * (1.0 - sigmoid))
    ).astype(BF16)
    d_both_ref[:, columns:] = (d_hidden * silu).astype(BF16)

    def write(out_ref, d_normed_ref):
        out = mm(hidden_ref[...], down_ref[...])
        if previous:
            out = out + before[0][...]
        out_ref[...] = out.astype(out_ref.dtype)
        for step in range(pieces):
            at = slice(step * rows, (step + 1) * rows)
            d_normed = times_transposed(d_both_ref[...], weights_ref[step, :rows, :])
            if previous:
                d_normed = d_normed + before[1][:, at]
            d_normed_ref[:, at] = d_normed.astype(d_normed_ref.dtype)

    if not last:
        write(*sums)
        return

    @pl.when(index < 4)
    def _():
        write(*sums[1::2])

    @pl.when(index >= 4)
    def _():
        write(*sums[0::2])


def feedforward(normed, cot, weights, columns, previous, last):
    rows, width = normed.shape
    size = rows // 8

    def blocks(count):
        return pl.BlockSpec((size, count), lambda i: ((i + 4) % 8, 0))

    if last:
        sums = [
            pl.BlockSpec((size, width), lambda i: (jnp.maximum(i - 4, 0), 0)),
            pl.BlockSpec((size, width), lambda i: (jnp.minimum(i, 3), 0)),
        ] * 2
        shapes = [jax.ShapeDtypeStruct((rows // 2, width), BF16)] * 4
    else:
        sums = [blocks(width)] * 2
        shapes = [jax.ShapeDtypeStruct((rows, width), F32)] * 2
    return pl.pallas_call(
        functools.partial(feedforward_kernel, bool(previous), last),
        grid=(8,),
        in_specs=[blocks(width), blocks(width), whole_spec(weights.shape)]
        + [blocks(width)] * len(previous),
        out_specs=[blocks(columns), blocks(2 * columns)] + sums,
        out_shape=[
            jax.ShapeDtypeStruct((rows, columns), BF16),
            jax.ShapeDtypeStruct((rows, 2 * columns), BF16),
        ]
        + shapes,
        scratch_shapes=[pltpu.VMEM((columns, width), BF16)],
        compiler_params=pltpu.CompilerParams(vmem_limit_bytes=56 << 20),
    )(normed, cot, weights, *previous)


def feedforward_grads_kernel(normed_ref, d_both_ref, hidden_ref, cot_ref, out_ref, down_ref):
    index = pl.program_id(0)
    rows, fused = normed_ref.shape[1], d_both_ref.shape[1]
    piece = down_ref.shape[0] // pl.num_programs(0)

    @pl.when(index == 0)
    def _():
        down_ref[...] = outer_sum(hidden_ref[...], cot_ref[...]).astype(BF16)

    out_ref[0, :rows, :] = outer_sum(normed_ref[...], d_both_ref[...]).astype(BF16)
    mine = down_ref[pl.ds(pl.multiple_of(index * piece, piece), piece), :]
    for part in range(down_ref.shape[1] // fused):
        start = rows + part * piece
        out_ref[0, start : start + piece, :] = mine[:, part * fused : (part + 1) * fused]


def feedforward_grads(normed, d_both, hidden, cot, pieces):
    rows, width = normed.shape
    columns = hidden.shape[1]
    fused = d_both.shape[1]
    out_rows = width // pieces + (columns // pieces) * (width // fused)
    return pl.pallas_call(
        feedforward_grads_kernel,
        grid=(pieces,),
        in_specs=[
            pl.BlockSpec((rows, width // pieces), lambda i: (0, i)),
            whole_spec(d_both.shape),
            whole_spec(hidden.shape),
            whole_spec(cot.shape),
        ],
        out_specs=pl.BlockSpec((1, out_rows, fused), lambda i: (i, 0, 0)),
        out_shape=jax.ShapeDtypeStruct((pieces, out_rows, fused), BF16),
        scratch_shapes=[pltpu.VMEM((columns, width), BF16)],
        compiler_params=pltpu.CompilerParams(vmem_limit_bytes=56 << 20),
    )(normed, d_both, hidden, cot)


def split_kernel(pieces, place_ref, gate_ref, up_ref, *refs):
    here_x = place_ref[1]
    chunks = len(refs) // 2
    size = gate_ref.shape[1] // (2 * chunks * pieces)
    for chunk in range(chunks):
        sides = []
        for side in range(2):
            starts = [(2 * chunks * step + side * chunks + chunk) * size for step in range(pieces)]
            sides.append(
                jnp.concatenate(
                    [ref[:, at : at + size] for ref in (gate_ref, up_ref) for at in starts], axis=1
                )
            )
        refs[2 * chunk][...] = jnp.where(here_x == 0, sides[0], sides[1])
        refs[2 * chunk + 1][...] = jnp.where(here_x == 0, sides[1], sides[0])


def split(place, gate, up, pieces):
    rows, columns = gate.shape
    size = min(rows, 64)
    fused = 2 * columns // (2 * CHUNKS)
    return pl.pallas_call(
        functools.partial(split_kernel, pieces),
        grid=(rows // size,),
        in_specs=[pl.BlockSpec(memory_space=pltpu.SMEM)]
        + [pl.BlockSpec((size, columns), lambda i: (i, 0))] * 2,
        out_specs=[pl.BlockSpec((size, fused), lambda i: (i, 0))] * (2 * CHUNKS),
        out_shape=[jax.ShapeDtypeStruct((rows, fused), BF16)] * (2 * CHUNKS),
    )(place, gate, up)


def assemble_kernel(pieces, place_ref, *refs):
    inputs, outputs = refs[:-2], refs[-2:]
    here_x = place_ref[1]
    chunks = len(inputs) // 2
    half = inputs[0].shape[1] // 2
    size = half // pieces
    for which, out_ref in enumerate(outputs):
        for step in range(pieces):
            columns = slice(which * half + step * size, which * half + (step + 1) * size)
            own = [inputs[2 * chunk][:, columns].astype(F32) for chunk in range(chunks)]
            moved = [inputs[2 * chunk + 1][:, columns].astype(F32) for chunk in range(chunks)]
            even = [jnp.where(here_x == 0, a, b) for a, b in zip(own, moved)]
            odd = [jnp.where(here_x == 0, b, a) for a, b in zip(own, moved)]
            span = 2 * chunks * size
            out_ref[:, step * span : (step + 1) * span] = jnp.concatenate(even + odd, axis=1)


def assemble(place, inputs, pieces, columns):
    rows, width = inputs[0].shape
    size = min(rows, 64)
    return pl.pallas_call(
        functools.partial(assemble_kernel, pieces),
        grid=(rows // size,),
        in_specs=[pl.BlockSpec(memory_space=pltpu.SMEM)]
        + [pl.BlockSpec((size, width), lambda i: (i, 0))] * len(inputs),
        out_specs=[pl.BlockSpec((size, columns), lambda i: (i, 0))] * 2,
        out_shape=[jax.ShapeDtypeStruct((rows, columns), F32)] * 2,
    )(place, *inputs)


def norm_backward(values, scale, gain, d_normed):
    weighted = d_normed * gain
    d_values = scale * weighted - values * scale * scale * scale * jnp.mean(
        weighted * values, axis=-1, keepdims=True
    )
    return (d_values, jnp.sum(d_normed * values * scale, axis=0))


def take(array, index, axis=0):
    return lax.dynamic_index_in_dim(array, index, axis, keepdims=False)


def choose(position, own, other):
    return [jnp.where(position == 0, own, other), jnp.where(position == 0, other, own)]


def in_order(position, own, other, axis=0):
    return jnp.stack(choose(position, own, other), axis=axis)


def rows_major(array):
    return with_layout_constraint(array, Layout(major_to_minor=tuple(range(array.ndim))))


def gather_z(piece):
    return rows_major(lax.all_gather(rows_major(piece), "z", axis=0))


def reduce_z(parts):
    return lax.psum_scatter(parts, "z", scatter_dimension=0)


def tie(*values):
    return lax.optimization_barrier(values)


def swap_blocks(rows, size, here):
    blocks = []
    for start in range(0, rows.shape[1], 2 * size):
        first, second = rows[:, start : start + size], rows[:, start + size : start + 2 * size]
        blocks += choose(here, first, second)
    return blocks


def gather_tensor(rows):
    beside = lax.ppermute(rows, "y", SWAP)
    return (
        rows,
        lax.ppermute(rows, "c", SWAP),
        beside,
        lax.ppermute(beside, "c", SWAP),
    )


def reduce_tensor(kept, sent):
    arrived = lax.ppermute(sent, "c", SWAP).astype(F32)
    moved = (kept[1].astype(F32) + arrived[1]).astype(BF16)
    return kept[0].astype(F32) + arrived[0] + lax.ppermute(moved, "y", SWAP).astype(F32)


def gather_planes(rows):
    return (
        rows,
        lax.ppermute(rows, "x", SWAP),
        lax.ppermute(rows, "y", SWAP),
        lax.ppermute(rows, ("x", "y"), DIAGONAL),
    )


def join_planes(planes):
    return jnp.concatenate(planes + tuple(lax.ppermute(plane, "c", SWAP) for plane in planes))


def reduce_eight(kept, sent):
    kept = kept.reshape((4, kept.shape[0] // 4) + kept.shape[1:])
    arrived = lax.ppermute(sent.reshape(kept.shape), "c", SWAP)
    sums = [kept[step].astype(F32) + arrived[step].astype(F32) for step in range(4)]
    return sums[0], [part.astype(BF16) for part in sums[1:]]


def send_eight(leaving):
    routes = (("x", SWAP), ("y", SWAP), (("x", "y"), DIAGONAL))
    return [lax.ppermute(part, axes, pairs) for part, (axes, pairs) in zip(leaving, routes)]


def body(
    tokens,
    cotangent,
    token_slots,
    lengths,
    query_weight,
    key_projection_weight,
    value_projection_weight,
    output_weight,
    gate_weight,
    up_weight,
    down_weight,
    prenorm_gain,
    midnorm_gain,
):
    z_size = lax.axis_size("z")
    here_x = lax.axis_index("x")
    devices = 8 * z_size
    micro, local_rows, width = tokens.shape
    flat_rows = micro * local_rows
    sends = local_rows // devices
    group_rows = 4 * local_rows
    query_cols = query_weight.shape[1]
    kv_cols = key_projection_weight.shape[1]
    fused_cols = query_cols + 2 * kv_cols
    shard_rows = query_weight.shape[0]
    hidden_cols = gate_weight.shape[1]
    block = hidden_cols // (2 * z_size)
    piece = block // CHUNKS
    chunk_cols = z_size * piece
    everywhere = ("z", "x", "y", "c")
    place = jnp.stack([2 * lax.axis_index("y") + lax.axis_index("c"), here_x]).astype(jnp.int32)

    rank = jnp.sum(
        (token_slots[:, None, :] < token_slots[:, :, None]).astype(jnp.int32), axis=2
    )
    order = (
        (rank // sends) * (micro * sends)
        + jnp.arange(micro, dtype=jnp.int32)[:, None] * sends
        + rank % sends
    ).reshape(flat_rows)
    places = jnp.arange(flat_rows, dtype=jnp.int32)
    to_send = (places[:, None] == order[None, :]).astype(BF16)
    local_slot = (token_slots % local_rows).reshape(flat_rows)

    def by_device(rows):
        return rows.reshape((devices, micro * sends) + rows.shape[1:])

    def exchange(blocks):
        return lax.all_to_all(
            blocks, everywhere, split_axis=0, concat_axis=0, tiled=True
        ).reshape((flat_rows,) + blocks.shape[2:])

    gains = jnp.stack([prenorm_gain, midnorm_gain]).reshape(micro * sends, -1)
    leaving = jnp.concatenate(
        [
            tokens.reshape(flat_rows, width),
            jnp.broadcast_to(local_slot[:, None], (flat_rows, gains.shape[1])).astype(BF16),
        ],
        axis=1,
    )
    leaving = jnp.concatenate(
        [mm(to_send, leaving).astype(BF16), jnp.tile(gains, (devices, 1))], axis=1
    )
    fused_shard = jnp.concatenate(
        [query_weight, key_projection_weight, value_projection_weight], axis=1
    )
    leaving, fused_shard, gate_weight, down_weight, cotangent = tie(
        by_device(leaving), fused_shard, gate_weight, down_weight, cotangent
    )
    arrived = exchange(leaving)
    cot_leaving = mm(to_send, cotangent.reshape(flat_rows, width)).astype(BF16)
    cot_leaving, arrived = tie(cot_leaving, arrived)
    arrived_cot = exchange(by_device(cot_leaving))
    arrived_tokens = arrived[:, :width]
    arrived_slots = arrived[:, width].astype(jnp.int32)
    arrived_gains = arrived[:, width + gains.shape[1] :].reshape(
        2 * z_size, 4, 2, -1, gains.shape[1]
    )[:, 0]
    gains = jnp.swapaxes(arrived_gains, 0, 1).reshape(2, width).astype(F32)
    gain_one, gain_two = gains[0:1], gains[1:2]
    arrived_micro = (places // sends) % micro
    to_place = (
        (arrived_slots + arrived_micro * local_rows)[:, None] == places[None, :]
    ).astype(BF16)

    halves = split(place, gate_weight, up_weight, z_size)
    ff_shards = []
    for chunk in range(CHUNKS):
        kept, leaving = halves[2 * chunk : 2 * chunk + 2]
        down = down_weight[chunk * piece : (chunk + 1) * piece]
        down_parts = [
            down[:, start : start + 2 * chunk_cols] for start in range(0, width, 2 * chunk_cols)
        ]
        ff_shards.append(
            jnp.concatenate(
                choose(here_x, kept, lax.ppermute(leaving, "x", SWAP)) + down_parts
            )
        )

    fused_own = gather_z(fused_shard).reshape(width // 2, fused_cols)
    fused_own, output_weight, arrived_tokens, *ff_shards = tie(
        fused_own, output_weight, arrived_tokens, *ff_shards
    )
    output_own = gather_z(output_weight)
    fused_other = lax.ppermute(fused_own, "x", SWAP)

    inputs = outer_sum(to_place, arrived_tokens)
    first_scale = rms_scale(inputs)
    first_normed = (inputs * first_scale * gain_one).astype(BF16)
    blocks = swap_blocks(first_normed, shard_rows, here_x)
    first_normed = jnp.concatenate(blocks[0::2] + blocks[1::2], axis=1)
    first_shard, first_normed = tie(ff_shards[0], first_normed)
    ff_weights = [gather_z(first_shard)]
    segments, tables = [], []
    for index in range(micro):
        segment, positions = sequence_layout(lengths[index, 0], group_rows)
        segments.append(segment)
        tables.append(rope_tables(positions, HEAD_SIZE))
    segments = jnp.stack(segments)
    segments = (segments[:, :, None], segments[:, None, :])
    tables = tuple(jnp.stack(table) for table in zip(*tables))
    rows_own = first_normed.reshape(micro, local_rows, width)
    rows_beside = lax.ppermute(rows_own, "y", SWAP)
    output_other = lax.ppermute(output_own, "x", SWAP)
    rows_own, rows_beside, fused_other = tie(rows_own, rows_beside, fused_other)
    output_full = in_order(here_x, output_own, output_other, axis=1).reshape(query_cols, width)
    pieces = (
        rows_own,
        lax.ppermute(rows_own, "c", SWAP),
        rows_beside,
        lax.ppermute(rows_beside, "c", SWAP),
    )
    cot_rows = outer_sum(to_place, arrived_cot).astype(BF16)
    cot_beside = lax.ppermute(cot_rows, "y", SWAP)
    cot_pair, output_full = tie(jnp.stack([cot_rows, cot_beside]), output_full)
    cot_over_x = lax.ppermute(cot_pair, "x", SWAP)
    shared = (fused_own, fused_other, output_full, tables, segments)
    normed_all, fused, heads, kept, sent = attention_forward(place, pieces, *shared)
    for shard in ff_shards[1:]:
        shard, sent = tie(shard, sent)
        ff_weights.append(gather_z(shard))
    attended = reduce_tensor(kept, sent).reshape(flat_rows, width)
    cot_over_x, attended = tie(cot_over_x, attended)
    cot_all = join_planes((cot_pair[0], cot_over_x[0], cot_pair[1], cot_over_x[1]))
    residual = inputs + attended

    second_scale = rms_scale(residual)
    normed_two = (residual * second_scale * gain_two).astype(BF16)
    normed_two_all = join_planes(gather_planes(normed_two))

    previous = ()
    gate_kept, gate_moved, down_grads = [], [], []
    for chunk in range(CHUNKS):
        hidden, d_both, *previous = feedforward(
            normed_two_all, cot_all, ff_weights[chunk], chunk_cols, previous, chunk == CHUNKS - 1
        )
        if chunk == CHUNKS - 1:
            d_own, d_leaving = reduce_eight(*previous[2:])
            d_both, *d_leaving = tie(d_both, *d_leaving)
        part = feedforward_grads(normed_two_all, d_both, hidden, cot_all, z_size)
        if chunk == CHUNKS - 1:
            part, *d_arrived = tie(part, *send_eight(d_leaving))
        total = reduce_z(part)
        own, other = choose(here_x, total[:shard_rows], total[shard_rows : 2 * shard_rows])
        gate_kept.append(own)
        gate_moved.append(other)
        down_grads.append(
            jnp.concatenate(
                [
                    total[start : start + piece]
                    for start in range(2 * shard_rows, total.shape[0], piece)
                ],
                axis=1,
            )
        )
    down_grad = jnp.concatenate(down_grads, axis=0).astype(F32)

    d_normed_two = d_own + sum(part.astype(F32) for part in d_arrived)
    d_through, d_gain_two = norm_backward(residual, second_scale, gain_two, d_normed_two)
    d_residual = cot_rows.astype(F32) + d_through

    d_residual, *out_parts = tie(d_residual, *previous[:2])
    out_own, out_leaving = reduce_eight(*out_parts)
    pieces = gather_tensor(d_residual.astype(BF16).reshape(micro, local_rows, width))
    out_over_x = lax.ppermute(jnp.stack([out_leaving[0], out_leaving[2]]), "x", SWAP)
    kept, sent, *weight_parts = attention_backward(
        place, pieces, *shared, normed_all, fused, heads, output_weight.shape[0]
    )
    kept, sent, out_over_x = tie(kept, sent, out_over_x)
    out_over_y = (out_leaving[1].astype(F32) + out_over_x[1].astype(F32)).astype(BF16)
    layer_rows = (
        residual
        + (out_own + out_over_x[0].astype(F32))
        + lax.ppermute(out_over_y, "y", SWAP).astype(F32)
    )
    d_normed_one = reduce_tensor(kept, sent).reshape(flat_rows, width)
    swapped = swap_blocks(
        jnp.concatenate(
            [
                d_normed_one[:, side * (width // 2) + start : side * (width // 2) + start + shard_rows]
                for start in range(0, width // 2, shard_rows)
                for side in range(2)
            ],
            axis=1,
        ),
        shard_rows,
        here_x,
    )
    d_normed_one = jnp.concatenate(swapped, axis=1)

    def reduce_x(kept, leaving):
        return (kept.astype(F32) + lax.ppermute(leaving, "x", SWAP).astype(F32)).astype(BF16)

    def reduce_data(total):
        return reduce_z(total.reshape(z_size, -1, total.shape[-1])).astype(F32)

    output_total, fused_sent = tie(reduce_x(*weight_parts[2:]), weight_parts[1])
    fused_total, *gate_moved = tie(reduce_x(weight_parts[0], fused_sent), *gate_moved)
    gate_moved = [lax.ppermute(part, "x", SWAP) for part in gate_moved]
    output_grad = reduce_data(output_total)
    fused_grad = reduce_data(fused_total)
    d_first, d_gain_one = norm_backward(inputs, first_scale, gain_one, d_normed_one)
    input_grads = (d_residual + d_first).astype(BF16)

    gain_grads = jnp.stack([d_gain_one, d_gain_two])
    high = gain_grads.astype(BF16)
    low = (gain_grads - high.astype(F32)).astype(BF16)
    riders = jnp.stack([high, low]).reshape(2, 2, 2 * z_size, 1, shard_rows)
    riders = jnp.broadcast_to(
        jnp.transpose(riders, (2, 3, 0, 1, 4)), (2 * z_size, 4, 2, 2, shard_rows)
    ).reshape(flat_rows, -1)

    back = jnp.concatenate([layer_rows.astype(BF16), input_grads], axis=1)
    returned = exchange(
        by_device(jnp.concatenate([mm(to_place, back).astype(BF16), riders], axis=1))
    )
    gate_up_grads = assemble(
        place, [part for pair in zip(gate_kept, gate_moved) for part in pair], z_size, hidden_cols
    )
    returned, *gate_up_grads = tie(returned, *gate_up_grads)
    outputs = outer_sum(to_send, returned[:, : 2 * width]).astype(BF16)
    outputs = outputs.reshape(micro, local_rows, 2 * width)
    gain_grads = jnp.sum(
        returned[:, 2 * width :].astype(F32).reshape(devices, 2, 2, shard_rows), axis=(0, 1)
    )

    return (
        outputs[:, :, :width],
        outputs[:, :, width:],
        fused_grad[:, :query_cols],
        fused_grad[:, query_cols : query_cols + kv_cols],
        fused_grad[:, query_cols + kv_cols :],
        output_grad,
        *gate_up_grads,
        down_grad,
        gain_grads[0],
        gain_grads[1],
    )


def solution(mesh):
    z_size = mesh.shape["dp"] // 2
    fine = Mesh(mesh.devices.reshape(z_size, 2, 2, 2), ("z", "x", "y", "c"))
    dp, tensor = ("z", "x"), ("y", "c")
    rows, columns, stacked = P(None, dp + tensor, None), P(dp, tensor), P(tensor + dp, None)
    return jax.shard_map(
        body,
        mesh=fine,
        in_specs=(
            rows,
            rows,
            P(None, dp + tensor),
            P(None, dp, None),
            columns,
            columns,
            columns,
            stacked,
            columns,
            columns,
            stacked,
            P(dp),
            P(dp),
        ),
        out_specs=(
            rows,
            rows,
            columns,
            columns,
            columns,
            stacked,
            columns,
            columns,
            stacked,
            P(dp),
            P(dp),
        ),
        check_vma=False,
    )
```

```python
import functools
import math

import jax
import jax.numpy as jnp
from jax import lax
from jax.experimental import pallas as pl
from jax.experimental.layout import Layout, with_layout_constraint
from jax.experimental.pallas import tpu as pltpu
from jax.sharding import Mesh, PartitionSpec as P

HEAD_SIZE = 256
EPSILON = 1e-06
ROPE_BASE = 1000042.0
NEGATIVE = -1e30
LONGEST = 256
CHUNKS = 2
F32 = jnp.float32
BF16 = jnp.bfloat16

SWAP = [(0, 1), (1, 0)]
DIAGONAL = [(0, 3), (3, 0), (1, 2), (2, 1)]
Z_NEAR = [(0, 1), (1, 0), (2, 3), (3, 2)]
Z_FAR = [(0, 2), (2, 0), (1, 3), (3, 1)]
Z_ACROSS = [(0, 3), (3, 0), (1, 2), (2, 1)]


def rms_scale(values):
    return lax.rsqrt(jnp.mean(values * values, axis=-1, keepdims=True) + EPSILON)


def rope_tables(positions, head):
    half = head // 2
    frequency = jnp.exp(jnp.arange(half, dtype=F32) * (-2.0 * math.log(ROPE_BASE) / head))
    angles = positions.astype(F32)[:, None] * frequency[None, :]
    return (jnp.cos(angles), jnp.sin(angles))


def rotate(head, cosine, sine):
    half = head.shape[-1] // 2
    first, second = head[:, :half], head[:, half:]
    return jnp.concatenate(
        [first * cosine - second * sine, second * cosine + first * sine], axis=-1
    )


def sequence_layout(lens, total):
    rows = jnp.arange(total, dtype=jnp.int32)
    ends = jnp.cumsum(lens)
    segment = jnp.sum((rows[:, None] >= ends[None, :]).astype(jnp.int32), axis=1)
    starts = ends - lens
    which = segment[:, None] == jnp.arange(lens.shape[0], dtype=jnp.int32)[None, :]
    begin = jnp.sum(jnp.where(which, starts[None, :], 0), axis=1)
    return (segment, rows - begin)


def mm(left, right):
    return jnp.dot(left, right, preferred_element_type=F32)


def outer_sum(left, right):
    return lax.dot_general(left, right, (((0,), (0,)), ((), ())), preferred_element_type=F32)


def times_transposed(left, right):
    return lax.dot_general(left, right, (((1,), (1,)), ((), ())), preferred_element_type=F32)


def masked_scores(query, key, seg_query, seg_key, row_start, key_start):
    scores = times_transposed(query, key) * (1.0 / math.sqrt(HEAD_SIZE))
    rows = row_start + lax.broadcasted_iota(jnp.int32, scores.shape, 0)
    keys = key_start + lax.broadcasted_iota(jnp.int32, scores.shape, 1)
    allowed = (seg_query == seg_key) & (rows >= keys)
    scores = jnp.where(allowed, scores, NEGATIVE)
    expo = jnp.exp(scores - jnp.max(scores, axis=-1, keepdims=True))
    return expo / jnp.sum(expo, axis=-1, keepdims=True)


def query_blocks(total):
    size = LONGEST
    return [
        (start, start + size, max(0, start - LONGEST)) for start in range(0, total, size)
    ]


def place_rows(place_ref, piece_refs, rows_ref):
    here = place_ref[0]
    size = piece_refs[0].shape[1]
    for step, piece in enumerate(piece_refs):
        start = pl.multiple_of(jnp.bitwise_xor(here, step) * size, size)
        rows_ref[pl.ds(start, size), :] = piece[0]


def spread_rows(place_ref, rows_ref, kept_ref, sent_ref):
    here = place_ref[0]
    size = kept_ref.shape[2]
    for step in range(4):
        start = pl.multiple_of(jnp.bitwise_xor(here, step) * size, size)
        out_ref = sent_ref if step % 2 else kept_ref
        out_ref[step // 2, 0] = rows_ref[pl.ds(start, size), :]


def attention_forward_kernel(
    query_heads,
    place_ref,
    piece0,
    piece1,
    piece2,
    piece3,
    own_ref,
    other_ref,
    output_ref,
    cosine_ref,
    sine_ref,
    seg_query_ref,
    seg_key_ref,
    normed_ref,
    fused_ref,
    heads_ref,
    kept_ref,
    sent_ref,
    rows_ref,
    sums_ref,
):
    place_rows(place_ref, (piece0, piece1, piece2, piece3), rows_ref)
    normed_ref[...] = rows_ref[...]
    half = own_ref.shape[0]
    fused = mm(rows_ref[:, :half], own_ref[...]) + mm(rows_ref[:, half:], other_ref[...])
    cosine, sine = cosine_ref[0], sine_ref[0]
    total = rows_ref.shape[0]
    kv_heads = fused.shape[1] // HEAD_SIZE - query_heads
    for head in range(query_heads + kv_heads // 2):
        columns = slice(head * HEAD_SIZE, (head + 1) * HEAD_SIZE)
        fused_ref[:, columns] = rotate(fused[:, columns], cosine, sine).astype(BF16)
    first_value = (query_heads + kv_heads // 2) * HEAD_SIZE
    fused_ref[:, first_value:] = fused[:, first_value:].astype(BF16)
    per_group = 2 * query_heads // kv_heads
    for head in range(query_heads):
        group = head // per_group
        columns = slice(head * HEAD_SIZE, (head + 1) * HEAD_SIZE)
        at_key = (query_heads + group) * HEAD_SIZE
        at_value = first_value + group * HEAD_SIZE
        for start, stop, low in query_blocks(total):
            probs = masked_scores(
                fused_ref[start:stop, columns],
                fused_ref[low:stop, at_key : at_key + HEAD_SIZE],
                seg_query_ref[0, start:stop],
                seg_key_ref[0, :, low:stop],
                start,
                low,
            )
            heads_ref[start:stop, columns] = mm(
                probs.astype(BF16), fused_ref[low:stop, at_value : at_value + HEAD_SIZE]
            ).astype(BF16)
    sums_ref[...] = mm(heads_ref[...], output_ref[...]).astype(BF16)
    spread_rows(place_ref, sums_ref, kept_ref, sent_ref)


def attention_backward_kernel(
    query_heads,
    block_rows,
    place_ref,
    piece0,
    piece1,
    piece2,
    piece3,
    own_ref,
    other_ref,
    output_ref,
    cosine_ref,
    sine_ref,
    seg_query_ref,
    seg_key_ref,
    normed_ref,
    fused_ref,
    heads_ref,
    kept_ref,
    sent_ref,
    fused_kept_ref,
    fused_sent_ref,
    output_kept_ref,
    output_sent_ref,
    rows_ref,
    sums_ref,
    d_heads_ref,
    d_fused_ref,
    d_key_ref,
    d_value_ref,
    fused_acc,
    output_acc,
):
    index = pl.program_id(0)
    scale = 1.0 / math.sqrt(HEAD_SIZE)
    place_rows(place_ref, (piece0, piece1, piece2, piece3), rows_ref)
    d_heads_ref[...] = times_transposed(rows_ref[...], output_ref[...]).astype(BF16)
    cosine, sine = cosine_ref[0], sine_ref[0]
    total = rows_ref.shape[0]
    kv_heads = fused_ref.shape[1] // HEAD_SIZE - query_heads
    first_value = (query_heads + kv_heads // 2) * HEAD_SIZE
    per_group = 2 * query_heads // kv_heads
    for group in range(kv_heads // 2):
        at_key = (query_heads + group) * HEAD_SIZE
        at_value = first_value + group * HEAD_SIZE
        d_key_ref[...] = jnp.zeros_like(d_key_ref)
        d_value_ref[...] = jnp.zeros_like(d_value_ref)
        for head in range(group * per_group, (group + 1) * per_group):
            columns = slice(head * HEAD_SIZE, (head + 1) * HEAD_SIZE)
            for start, stop, low in query_blocks(total):
                query = fused_ref[start:stop, columns]
                key = fused_ref[low:stop, at_key : at_key + HEAD_SIZE]
                value = fused_ref[low:stop, at_value : at_value + HEAD_SIZE]
                d_heads = d_heads_ref[start:stop, columns]
                probs = masked_scores(
                    query,
                    key,
                    seg_query_ref[0, start:stop],
                    seg_key_ref[0, :, low:stop],
                    start,
                    low,
                )
                d_probs = times_transposed(d_heads, value)
                delta = jnp.sum(probs * d_probs, axis=-1, keepdims=True)
                d_scores = (probs * (d_probs - delta)).astype(BF16)
                d_query = mm(d_scores, key) * scale
                d_fused_ref[start:stop, columns] = rotate(
                    d_query, cosine[start:stop], -sine[start:stop]
                ).astype(BF16)
                d_key_ref[low:stop] += outer_sum(d_scores, query) * scale
                d_value_ref[low:stop] += outer_sum(probs.astype(BF16), d_heads)
        d_fused_ref[:, at_key : at_key + HEAD_SIZE] = rotate(
            d_key_ref[...], cosine, -sine
        ).astype(BF16)
        d_fused_ref[:, at_value : at_value + HEAD_SIZE] = d_value_ref[...].astype(BF16)
    half = own_ref.shape[0]
    sums_ref[:, :half] = times_transposed(d_fused_ref[...], own_ref[...]).astype(BF16)
    sums_ref[:, half:] = times_transposed(d_fused_ref[...], other_ref[...]).astype(BF16)
    spread_rows(place_ref, sums_ref, kept_ref, sent_ref)
    fused_part = outer_sum(normed_ref[...], d_fused_ref[...])
    output_part = outer_sum(heads_ref[...], rows_ref[...])

    @pl.when(index == 0)
    def _():
        fused_acc[...] = fused_part
        output_acc[...] = output_part

    @pl.when(index > 0)
    def _():
        fused_acc[...] += fused_part
        output_acc[...] += output_part

    @pl.when(index == pl.num_programs(0) - 1)
    def _():
        fused_kept_ref[...] = fused_acc[:half].astype(BF16)
        fused_sent_ref[...] = fused_acc[half:].astype(BF16)
        here_x = place_ref[1]
        size = block_rows
        for step in range(output_acc.shape[0] // (2 * size)):
            kept = pl.multiple_of((2 * step + here_x) * size, size)
            sent = pl.multiple_of((2 * step + 1 - here_x) * size, size)
            rows = slice(step * size, (step + 1) * size)
            output_kept_ref[rows] = output_acc[pl.ds(kept, size), :].astype(BF16)
            output_sent_ref[rows] = output_acc[pl.ds(sent, size), :].astype(BF16)


def whole_spec(shape):
    zeros = (0,) * len(shape)
    return pl.BlockSpec(shape, lambda *_: zeros, pipeline_mode=pl.Buffered(1))


def attention_specs(pieces, own, other, output_full, tables, segments):
    micro, rows, width = pieces[0].shape
    total = 4 * rows
    half = tables[0].shape[-1]
    return (
        [pl.BlockSpec(memory_space=pltpu.SMEM)]
        + [pl.BlockSpec((1, rows, width), lambda m: (m, 0, 0))] * 4
        + [whole_spec(own.shape), whole_spec(other.shape), whole_spec(output_full.shape)]
        + [pl.BlockSpec((1, total, half), lambda m: (m, 0, 0))] * 2
        + [
            pl.BlockSpec((1, total, 1), lambda m: (m, 0, 0)),
            pl.BlockSpec((1, 1, total), lambda m: (m, 0, 0)),
        ]
    )


def attention_forward(place, pieces, own, other, output_full, tables, segments):
    micro, rows, width = pieces[0].shape
    total = 4 * rows
    query_cols, fused_cols = output_full.shape[0], own.shape[1]

    def by_micro(columns):
        return pl.BlockSpec((total, columns), lambda m: (m, 0))

    return pl.pallas_call(
        functools.partial(attention_forward_kernel, query_cols // HEAD_SIZE),
        grid=(micro,),
        in_specs=attention_specs(pieces, own, other, output_full, tables, segments),
        out_specs=[
            by_micro(width),
            by_micro(fused_cols),
            by_micro(query_cols),
            pl.BlockSpec((2, 1, rows, width), lambda m: (0, m, 0, 0)),
            pl.BlockSpec((2, 1, rows, width), lambda m: (0, m, 0, 0)),
        ],
        out_shape=[
            jax.ShapeDtypeStruct((micro * total, width), BF16),
            jax.ShapeDtypeStruct((micro * total, fused_cols), BF16),
            jax.ShapeDtypeStruct((micro * total, query_cols), BF16),
            jax.ShapeDtypeStruct((2, micro, rows, width), BF16),
            jax.ShapeDtypeStruct((2, micro, rows, width), BF16),
        ],
        scratch_shapes=[pltpu.VMEM((total, width), BF16), pltpu.VMEM((total, width), BF16)],
        compiler_params=pltpu.CompilerParams(vmem_limit_bytes=56 << 20),
    )(place, *pieces, own, other, output_full, *tables, *segments)


def attention_backward(
    place, pieces, own, other, output_full, tables, segments, normed, fused, heads, block_rows
):
    micro, rows, width = pieces[0].shape
    total = 4 * rows
    query_cols, fused_cols = output_full.shape[0], own.shape[1]

    def by_micro(columns):
        return pl.BlockSpec((total, columns), lambda m: (m, 0))

    return pl.pallas_call(
        functools.partial(attention_backward_kernel, query_cols // HEAD_SIZE, block_rows),
        grid=(micro,),
        in_specs=attention_specs(pieces, own, other, output_full, tables, segments)
        + [by_micro(width), by_micro(fused_cols), by_micro(query_cols)],
        out_specs=[
            pl.BlockSpec((2, 1, rows, width), lambda m: (0, m, 0, 0)),
            pl.BlockSpec((2, 1, rows, width), lambda m: (0, m, 0, 0)),
            whole_spec((width // 2, fused_cols)),
            whole_spec((width // 2, fused_cols)),
            whole_spec((query_cols // 2, width)),
            whole_spec((query_cols // 2, width)),
        ],
        out_shape=[
            jax.ShapeDtypeStruct((2, micro, rows, width), BF16),
            jax.ShapeDtypeStruct((2, micro, rows, width), BF16),
            jax.ShapeDtypeStruct((width // 2, fused_cols), BF16),
            jax.ShapeDtypeStruct((width // 2, fused_cols), BF16),
            jax.ShapeDtypeStruct((query_cols // 2, width), BF16),
            jax.ShapeDtypeStruct((query_cols // 2, width), BF16),
        ],
        scratch_shapes=[
            pltpu.VMEM((total, width), BF16),
            pltpu.VMEM((total, width), BF16),
            pltpu.VMEM((total, query_cols), BF16),
            pltpu.VMEM((total, fused_cols), BF16),
            pltpu.VMEM((total, HEAD_SIZE), F32),
            pltpu.VMEM((total, HEAD_SIZE), F32),
            pltpu.VMEM((width, fused_cols), F32),
            pltpu.VMEM((query_cols, width), F32),
        ],
        compiler_params=pltpu.CompilerParams(vmem_limit_bytes=60 << 20),
    )(place, *pieces, own, other, output_full, *tables, *segments, normed, fused, heads)


def feedforward_kernel(previous, last, normed_ref, cot_ref, weights_ref, *refs):
    refs = list(refs)
    before = [refs.pop(0) for _ in range(2)] if previous else []
    down_ref = refs.pop()
    hidden_ref, d_both_ref, *sums = refs
    pieces, _, fused = weights_ref.shape
    columns, width = down_ref.shape
    rows, piece = width // pieces, columns // pieces
    index = pl.program_id(0)

    @pl.when(index == 0)
    def _():
        for step in range(pieces):
            for part in range(width // fused):
                start = rows + part * piece
                down_ref[step * piece : (step + 1) * piece, part * fused : (part + 1) * fused] = (
                    weights_ref[step, start : start + piece, :]
                )

    both = mm(normed_ref[:, :rows], weights_ref[0, :rows, :])
    for step in range(1, pieces):
        both = both + mm(normed_ref[:, step * rows : (step + 1) * rows], weights_ref[step, :rows, :])
    gate, upward = both[:, :columns], both[:, columns:]
    sigmoid = 1.0 / (1.0 + jnp.exp(-gate))
    silu = gate * sigmoid
    hidden_ref[...] = (silu * upward).astype(BF16)
    d_hidden = times_transposed(cot_ref[...], down_ref[...])
    d_both_ref[:, :columns] = (
        d_hidden * upward * sigmoid * (1.0 + gate * (1.0 - sigmoid))
    ).astype(BF16)
    d_both_ref[:, columns:] = (d_hidden * silu).astype(BF16)

    def write(out_ref, d_normed_ref):
        out = mm(hidden_ref[...], down_ref[...])
        if previous:
            out = out + before[0][...]
        out_ref[...] = out.astype(out_ref.dtype)
        for step in range(pieces):
            at = slice(step * rows, (step + 1) * rows)
            d_normed = times_transposed(d_both_ref[...], weights_ref[step, :rows, :])
            if previous:
                d_normed = d_normed + before[1][:, at]
            d_normed_ref[:, at] = d_normed.astype(d_normed_ref.dtype)

    if not last:
        write(*sums)
        return

    @pl.when(index < 4)
    def _():
        write(*sums[1::2])

    @pl.when(index >= 4)
    def _():
        write(*sums[0::2])


def feedforward(normed, cot, weights, columns, previous, last):
    rows, width = normed.shape
    size = rows // 8

    def blocks(count):
        return pl.BlockSpec((size, count), lambda i: ((i + 4) % 8, 0))

    if last:
        sums = [
            pl.BlockSpec((size, width), lambda i: (jnp.maximum(i - 4, 0), 0)),
            pl.BlockSpec((size, width), lambda i: (jnp.minimum(i, 3), 0)),
        ] * 2
        shapes = [jax.ShapeDtypeStruct((rows // 2, width), BF16)] * 4
    else:
        sums = [blocks(width)] * 2
        shapes = [jax.ShapeDtypeStruct((rows, width), F32)] * 2
    return pl.pallas_call(
        functools.partial(feedforward_kernel, bool(previous), last),
        grid=(8,),
        in_specs=[blocks(width), blocks(width), whole_spec(weights.shape)]
        + [blocks(width)] * len(previous),
        out_specs=[blocks(columns), blocks(2 * columns)] + sums,
        out_shape=[
            jax.ShapeDtypeStruct((rows, columns), BF16),
            jax.ShapeDtypeStruct((rows, 2 * columns), BF16),
        ]
        + shapes,
        scratch_shapes=[pltpu.VMEM((columns, width), BF16)],
        compiler_params=pltpu.CompilerParams(vmem_limit_bytes=56 << 20),
    )(normed, cot, weights, *previous)


def feedforward_grads_kernel(normed_ref, d_both_ref, hidden_ref, cot_ref, out_ref, down_ref):
    index = pl.program_id(0)
    rows, fused = normed_ref.shape[1], d_both_ref.shape[1]
    piece = down_ref.shape[0] // pl.num_programs(0)

    @pl.when(index == 0)
    def _():
        down_ref[...] = outer_sum(hidden_ref[...], cot_ref[...]).astype(BF16)

    out_ref[0, :rows, :] = outer_sum(normed_ref[...], d_both_ref[...]).astype(BF16)
    mine = down_ref[pl.ds(pl.multiple_of(index * piece, piece), piece), :]
    for part in range(down_ref.shape[1] // fused):
        start = rows + part * piece
        out_ref[0, start : start + piece, :] = mine[:, part * fused : (part + 1) * fused]


def feedforward_grads(normed, d_both, hidden, cot, pieces):
    rows, width = normed.shape
    columns = hidden.shape[1]
    fused = d_both.shape[1]
    out_rows = width // pieces + (columns // pieces) * (width // fused)
    return pl.pallas_call(
        feedforward_grads_kernel,
        grid=(pieces,),
        in_specs=[
            pl.BlockSpec((rows, width // pieces), lambda i: (0, i)),
            whole_spec(d_both.shape),
            whole_spec(hidden.shape),
            whole_spec(cot.shape),
        ],
        out_specs=pl.BlockSpec((1, out_rows, fused), lambda i: (i, 0, 0)),
        out_shape=jax.ShapeDtypeStruct((pieces, out_rows, fused), BF16),
        scratch_shapes=[pltpu.VMEM((columns, width), BF16)],
        compiler_params=pltpu.CompilerParams(vmem_limit_bytes=56 << 20),
    )(normed, d_both, hidden, cot)


def split_kernel(pieces, place_ref, gate_ref, up_ref, *refs):
    here_x = place_ref[1]
    chunks = len(refs) // 2
    size = gate_ref.shape[1] // (2 * chunks * pieces)
    for chunk in range(chunks):
        sides = []
        for side in range(2):
            starts = [(2 * chunks * step + side * chunks + chunk) * size for step in range(pieces)]
            sides.append(
                jnp.concatenate(
                    [ref[:, at : at + size] for ref in (gate_ref, up_ref) for at in starts], axis=1
                )
            )
        refs[2 * chunk][...] = jnp.where(here_x == 0, sides[0], sides[1])
        refs[2 * chunk + 1][...] = jnp.where(here_x == 0, sides[1], sides[0])


def split(place, gate, up, pieces):
    rows, columns = gate.shape
    size = min(rows, 64)
    fused = 2 * columns // (2 * CHUNKS)
    return pl.pallas_call(
        functools.partial(split_kernel, pieces),
        grid=(rows // size,),
        in_specs=[pl.BlockSpec(memory_space=pltpu.SMEM)]
        + [pl.BlockSpec((size, columns), lambda i: (i, 0))] * 2,
        out_specs=[pl.BlockSpec((size, fused), lambda i: (i, 0))] * (2 * CHUNKS),
        out_shape=[jax.ShapeDtypeStruct((rows, fused), BF16)] * (2 * CHUNKS),
    )(place, gate, up)


def assemble_kernel(pieces, place_ref, *refs):
    inputs, outputs = refs[:-2], refs[-2:]
    here_x = place_ref[1]
    chunks = len(inputs) // 2
    half = inputs[0].shape[1] // 2
    size = half // pieces
    for which, out_ref in enumerate(outputs):
        for step in range(pieces):
            columns = slice(which * half + step * size, which * half + (step + 1) * size)
            own = [inputs[2 * chunk][:, columns].astype(F32) for chunk in range(chunks)]
            moved = [inputs[2 * chunk + 1][:, columns].astype(F32) for chunk in range(chunks)]
            even = [jnp.where(here_x == 0, a, b) for a, b in zip(own, moved)]
            odd = [jnp.where(here_x == 0, b, a) for a, b in zip(own, moved)]
            span = 2 * chunks * size
            out_ref[:, step * span : (step + 1) * span] = jnp.concatenate(even + odd, axis=1)


def assemble(place, inputs, pieces, columns):
    rows, width = inputs[0].shape
    size = min(rows, 64)
    return pl.pallas_call(
        functools.partial(assemble_kernel, pieces),
        grid=(rows // size,),
        in_specs=[pl.BlockSpec(memory_space=pltpu.SMEM)]
        + [pl.BlockSpec((size, width), lambda i: (i, 0))] * len(inputs),
        out_specs=[pl.BlockSpec((size, columns), lambda i: (i, 0))] * 2,
        out_shape=[jax.ShapeDtypeStruct((rows, columns), F32)] * 2,
    )(place, *inputs)


def norm_backward(values, scale, gain, d_normed):
    weighted = d_normed * gain
    d_values = scale * weighted - values * scale * scale * scale * jnp.mean(
        weighted * values, axis=-1, keepdims=True
    )
    return (d_values, jnp.sum(d_normed * values * scale, axis=0))


def take(array, index, axis=0):
    return lax.dynamic_index_in_dim(array, index, axis, keepdims=False)


def choose(position, own, other):
    return [jnp.where(position == 0, own, other), jnp.where(position == 0, other, own)]


def in_order(position, own, other, axis=0):
    return jnp.stack(choose(position, own, other), axis=axis)


def rows_major(array):
    return with_layout_constraint(array, Layout(major_to_minor=tuple(range(array.ndim))))


def gather_z(piece):
    return rows_major(lax.all_gather(rows_major(piece), "z", axis=0))


def reduce_z(parts):
    return lax.psum_scatter(parts, "z", scatter_dimension=0)


def tie(*values):
    return lax.optimization_barrier(values)


def swap_blocks(rows, size, here):
    blocks = []
    for start in range(0, rows.shape[1], 2 * size):
        first, second = rows[:, start : start + size], rows[:, start + size : start + 2 * size]
        blocks += choose(here, first, second)
    return blocks


def gather_tensor(rows):
    beside = lax.ppermute(rows, "y", SWAP)
    return (
        rows,
        lax.ppermute(rows, "c", SWAP),
        beside,
        lax.ppermute(beside, "c", SWAP),
    )


def reduce_tensor(kept, sent):
    arrived = lax.ppermute(sent, "c", SWAP).astype(F32)
    moved = (kept[1].astype(F32) + arrived[1]).astype(BF16)
    return kept[0].astype(F32) + arrived[0] + lax.ppermute(moved, "y", SWAP).astype(F32)


def gather_planes(rows):
    return (
        rows,
        lax.ppermute(rows, "x", SWAP),
        lax.ppermute(rows, "y", SWAP),
        lax.ppermute(rows, ("x", "y"), DIAGONAL),
    )


def join_planes(planes):
    return jnp.concatenate(planes + tuple(lax.ppermute(plane, "c", SWAP) for plane in planes))


def reduce_eight(kept, sent):
    kept = kept.reshape((4, kept.shape[0] // 4) + kept.shape[1:])
    arrived = lax.ppermute(sent.reshape(kept.shape), "c", SWAP)
    sums = [kept[step].astype(F32) + arrived[step].astype(F32) for step in range(4)]
    return sums[0], [part.astype(BF16) for part in sums[1:]]


def send_eight(leaving):
    routes = (("x", SWAP), ("y", SWAP), (("x", "y"), DIAGONAL))
    return [lax.ppermute(part, axes, pairs) for part, (axes, pairs) in zip(leaving, routes)]


def body(
    tokens,
    cotangent,
    token_slots,
    lengths,
    query_weight,
    key_projection_weight,
    value_projection_weight,
    output_weight,
    gate_weight,
    up_weight,
    down_weight,
    prenorm_gain,
    midnorm_gain,
):
    z_size = lax.axis_size("z")
    here_x = lax.axis_index("x")
    devices = 8 * z_size
    micro, local_rows, width = tokens.shape
    flat_rows = micro * local_rows
    sends = local_rows // devices
    group_rows = 4 * local_rows
    query_cols = query_weight.shape[1]
    kv_cols = key_projection_weight.shape[1]
    fused_cols = query_cols + 2 * kv_cols
    shard_rows = query_weight.shape[0]
    hidden_cols = gate_weight.shape[1]
    block = hidden_cols // (2 * z_size)
    piece = block // CHUNKS
    chunk_cols = z_size * piece
    everywhere = ("z", "x", "y", "c")
    place = jnp.stack([2 * lax.axis_index("y") + lax.axis_index("c"), here_x]).astype(jnp.int32)

    fused_shard = jnp.concatenate(
        [query_weight, key_projection_weight, value_projection_weight], axis=1
    )
    fused_shard, token_slots = tie(fused_shard, token_slots)

    rank = jnp.sum(
        (token_slots[:, None, :] < token_slots[:, :, None]).astype(jnp.int32), axis=2
    )
    order = (
        (rank // sends) * (micro * sends)
        + jnp.arange(micro, dtype=jnp.int32)[:, None] * sends
        + rank % sends
    ).reshape(flat_rows)
    places = jnp.arange(flat_rows, dtype=jnp.int32)
    to_send = (places[:, None] == order[None, :]).astype(BF16)
    local_slot = (token_slots % local_rows).reshape(flat_rows)

    def by_device(rows):
        return rows.reshape((devices, micro * sends) + rows.shape[1:])

    def exchange(blocks):
        return lax.all_to_all(
            blocks, everywhere, split_axis=0, concat_axis=0, tiled=True
        ).reshape((flat_rows,) + blocks.shape[2:])

    gains = jnp.stack([prenorm_gain, midnorm_gain]).reshape(micro * sends, -1)
    leaving = jnp.concatenate(
        [
            tokens.reshape(flat_rows, width),
            jnp.broadcast_to(local_slot[:, None], (flat_rows, gains.shape[1])).astype(BF16),
        ],
        axis=1,
    )
    leaving = jnp.concatenate(
        [mm(to_send, leaving).astype(BF16), jnp.tile(gains, (devices, 1))], axis=1
    )
    leaving, gate_weight, down_weight, cotangent = tie(
        by_device(leaving), gate_weight, down_weight, cotangent
    )
    arrived = exchange(leaving)
    cot_leaving = mm(to_send, cotangent.reshape(flat_rows, width)).astype(BF16)
    cot_leaving, arrived = tie(cot_leaving, arrived)
    arrived_cot = exchange(by_device(cot_leaving))
    arrived_tokens = arrived[:, :width]
    arrived_slots = arrived[:, width].astype(jnp.int32)
    arrived_gains = arrived[:, width + gains.shape[1] :].reshape(
        2 * z_size, 4, 2, -1, gains.shape[1]
    )[:, 0]
    gains = jnp.swapaxes(arrived_gains, 0, 1).reshape(2, width).astype(F32)
    gain_one, gain_two = gains[0:1], gains[1:2]
    arrived_micro = (places // sends) % micro
    to_place = (
        (arrived_slots + arrived_micro * local_rows)[:, None] == places[None, :]
    ).astype(BF16)

    halves = split(place, gate_weight, up_weight, z_size)
    ff_shards = []
    for chunk in range(CHUNKS):
        kept, leaving = halves[2 * chunk : 2 * chunk + 2]
        down = down_weight[chunk * piece : (chunk + 1) * piece]
        down_parts = [
            down[:, start : start + 2 * chunk_cols] for start in range(0, width, 2 * chunk_cols)
        ]
        ff_shards.append(
            jnp.concatenate(
                choose(here_x, kept, lax.ppermute(leaving, "x", SWAP)) + down_parts
            )
        )

    fused_own = gather_z(fused_shard).reshape(width // 2, fused_cols)
    fused_own, output_weight, arrived_tokens, *ff_shards = tie(
        fused_own, output_weight, arrived_tokens, *ff_shards
    )
    output_own = gather_z(output_weight)
    fused_other = lax.ppermute(fused_own, "x", SWAP)

    inputs = outer_sum(to_place, arrived_tokens)
    first_scale = rms_scale(inputs)
    first_normed = (inputs * first_scale * gain_one).astype(BF16)
    blocks = swap_blocks(first_normed, shard_rows, here_x)
    first_normed = jnp.concatenate(blocks[0::2] + blocks[1::2], axis=1)
    first_shard, first_normed = tie(ff_shards[0], first_normed)
    ff_weights = [gather_z(first_shard)]
    segments, tables = [], []
    for index in range(micro):
        segment, positions = sequence_layout(lengths[index, 0], group_rows)
        segments.append(segment)
        tables.append(rope_tables(positions, HEAD_SIZE))
    segments = jnp.stack(segments)
    segments = (segments[:, :, None], segments[:, None, :])
    tables = tuple(jnp.stack(table) for table in zip(*tables))
    rows_own = first_normed.reshape(micro, local_rows, width)
    rows_beside = lax.ppermute(rows_own, "y", SWAP)
    output_other = lax.ppermute(output_own, "x", SWAP)
    rows_own, rows_beside, fused_other = tie(rows_own, rows_beside, fused_other)
    output_full = in_order(here_x, output_own, output_other, axis=1).reshape(query_cols, width)
    pieces = (
        rows_own,
        lax.ppermute(rows_own, "c", SWAP),
        rows_beside,
        lax.ppermute(rows_beside, "c", SWAP),
    )
    cot_rows = outer_sum(to_place, arrived_cot).astype(BF16)
    cot_beside = lax.ppermute(cot_rows, "y", SWAP)
    cot_rows, cot_beside, output_full = tie(cot_rows, cot_beside, output_full)
    cot_over_x = lax.ppermute(cot_rows, "x", SWAP)
    cot_across = lax.ppermute(cot_beside, "x", SWAP)
    shared = (fused_own, fused_other, output_full, tables, segments)
    normed_all, fused, heads, kept, sent = attention_forward(place, pieces, *shared)
    kept, sent, cot_over_x = tie(kept, sent, cot_over_x)
    for shard in ff_shards[1:]:
        shard, sent = tie(shard, sent)
        ff_weights.append(gather_z(shard))
    attended = reduce_tensor(kept, sent).reshape(flat_rows, width)
    cot_across, attended = tie(cot_across, attended)
    cot_all = join_planes((cot_rows, cot_over_x, cot_beside, cot_across))
    residual = inputs + attended

    second_scale = rms_scale(residual)
    normed_two = (residual * second_scale * gain_two).astype(BF16)
    planes = list(gather_planes(normed_two))
    planes[1], cot_all = tie(planes[1], cot_all)
    normed_two_all = join_planes(tuple(planes))

    previous = ()
    gate_kept, gate_moved, down_grads = [], [], []
    for chunk in range(CHUNKS):
        hidden, d_both, *previous = feedforward(
            normed_two_all, cot_all, ff_weights[chunk], chunk_cols, previous, chunk == CHUNKS - 1
        )
        if chunk == CHUNKS - 1:
            d_own, d_leaving = reduce_eight(*previous[2:])
            d_both, *d_leaving = tie(d_both, *d_leaving)
        part = feedforward_grads(normed_two_all, d_both, hidden, cot_all, z_size)
        if chunk == CHUNKS - 1:
            part, *d_arrived = tie(part, *send_eight(d_leaving))
        total = reduce_z(part)
        own, other = choose(here_x, total[:shard_rows], total[shard_rows : 2 * shard_rows])
        gate_kept.append(own)
        gate_moved.append(other)
        down_grads.append(
            jnp.concatenate(
                [
                    total[start : start + piece]
                    for start in range(2 * shard_rows, total.shape[0], piece)
                ],
                axis=1,
            )
        )
    down_grad = jnp.concatenate(down_grads, axis=0).astype(F32)

    d_normed_two = d_own + sum(part.astype(F32) for part in d_arrived)
    d_through, d_gain_two = norm_backward(residual, second_scale, gain_two, d_normed_two)
    d_residual = cot_rows.astype(F32) + d_through

    d_residual, *out_parts = tie(d_residual, *previous[:2])
    out_own, out_leaving = reduce_eight(*out_parts)
    pieces = gather_tensor(d_residual.astype(BF16).reshape(micro, local_rows, width))
    out_over_x = lax.ppermute(jnp.stack([out_leaving[0], out_leaving[2]]), "x", SWAP)
    kept, sent, *weight_parts = attention_backward(
        place, pieces, *shared, normed_all, fused, heads, output_weight.shape[0]
    )
    kept, sent, out_over_x = tie(kept, sent, out_over_x)
    out_over_y = (out_leaving[1].astype(F32) + out_over_x[1].astype(F32)).astype(BF16)
    layer_rows = (
        residual
        + (out_own + out_over_x[0].astype(F32))
        + lax.ppermute(out_over_y, "y", SWAP).astype(F32)
    )
    d_normed_one = reduce_tensor(kept, sent).reshape(flat_rows, width)
    swapped = swap_blocks(
        jnp.concatenate(
            [
                d_normed_one[:, side * (width // 2) + start : side * (width // 2) + start + shard_rows]
                for start in range(0, width // 2, shard_rows)
                for side in range(2)
            ],
            axis=1,
        ),
        shard_rows,
        here_x,
    )
    d_normed_one = jnp.concatenate(swapped, axis=1)

    def reduce_x(kept, leaving):
        return (kept.astype(F32) + lax.ppermute(leaving, "x", SWAP).astype(F32)).astype(BF16)

    def reduce_data(total):
        return reduce_z(total.reshape(z_size, -1, total.shape[-1])).astype(F32)

    output_total, fused_sent = tie(reduce_x(*weight_parts[2:]), weight_parts[1])
    fused_total, *gate_moved = tie(reduce_x(weight_parts[0], fused_sent), *gate_moved)
    gate_moved = [lax.ppermute(part, "x", SWAP) for part in gate_moved]
    output_grad = reduce_data(output_total)
    fused_grad = reduce_data(fused_total)
    d_first, d_gain_one = norm_backward(inputs, first_scale, gain_one, d_normed_one)
    input_grads = (d_residual + d_first).astype(BF16)

    gain_grads = jnp.stack([d_gain_one, d_gain_two])
    high = gain_grads.astype(BF16)
    low = (gain_grads - high.astype(F32)).astype(BF16)
    riders = jnp.stack([high, low]).reshape(2, 2, 2 * z_size, 1, shard_rows)
    riders = jnp.broadcast_to(
        jnp.transpose(riders, (2, 3, 0, 1, 4)), (2 * z_size, 4, 2, 2, shard_rows)
    ).reshape(flat_rows, -1)

    back = jnp.concatenate([layer_rows.astype(BF16), input_grads], axis=1)
    returned = exchange(
        by_device(jnp.concatenate([mm(to_place, back).astype(BF16), riders], axis=1))
    )
    gate_up_grads = assemble(
        place, [part for pair in zip(gate_kept, gate_moved) for part in pair], z_size, hidden_cols
    )
    returned, *gate_up_grads = tie(returned, *gate_up_grads)
    outputs = outer_sum(to_send, returned[:, : 2 * width]).astype(BF16)
    outputs = outputs.reshape(micro, local_rows, 2 * width)
    gain_grads = jnp.sum(
        returned[:, 2 * width :].astype(F32).reshape(devices, 2, 2, shard_rows), axis=(0, 1)
    )

    return (
        outputs[:, :, :width],
        outputs[:, :, width:],
        fused_grad[:, :query_cols],
        fused_grad[:, query_cols : query_cols + kv_cols],
        fused_grad[:, query_cols + kv_cols :],
        output_grad,
        *gate_up_grads,
        down_grad,
        gain_grads[0],
        gain_grads[1],
    )


def solution(mesh):
    z_size = mesh.shape["dp"] // 2
    fine = Mesh(mesh.devices.reshape(z_size, 2, 2, 2), ("z", "x", "y", "c"))
    dp, tensor = ("z", "x"), ("y", "c")
    rows, columns, stacked = P(None, dp + tensor, None), P(dp, tensor), P(tensor + dp, None)
    return jax.shard_map(
        body,
        mesh=fine,
        in_specs=(
            rows,
            rows,
            P(None, dp + tensor),
            P(None, dp, None),
            columns,
            columns,
            columns,
            stacked,
            columns,
            columns,
            stacked,
            P(dp),
            P(dp),
        ),
        out_specs=(
            rows,
            rows,
            columns,
            columns,
            columns,
            stacked,
            columns,
            columns,
            stacked,
            P(dp),
            P(dp),
        ),
        check_vma=False,
    )
```

```python
import functools
import math

import jax
import jax.numpy as jnp
from jax import lax
from jax.experimental import pallas as pl
from jax.experimental.layout import Layout, with_layout_constraint
from jax.experimental.pallas import tpu as pltpu
from jax.sharding import Mesh, PartitionSpec as P

HEAD_SIZE = 256
EPSILON = 1e-06
ROPE_BASE = 1000042.0
NEGATIVE = -1e30
LONGEST = 256
CHUNKS = 2
F32 = jnp.float32
BF16 = jnp.bfloat16

SWAP = [(0, 1), (1, 0)]
DIAGONAL = [(0, 3), (3, 0), (1, 2), (2, 1)]
Z_NEAR = [(0, 1), (1, 0), (2, 3), (3, 2)]
Z_FAR = [(0, 2), (2, 0), (1, 3), (3, 1)]
Z_ACROSS = [(0, 3), (3, 0), (1, 2), (2, 1)]


def rms_scale(values):
    return lax.rsqrt(jnp.mean(values * values, axis=-1, keepdims=True) + EPSILON)


def rope_tables(positions, head):
    half = head // 2
    frequency = jnp.exp(jnp.arange(half, dtype=F32) * (-2.0 * math.log(ROPE_BASE) / head))
    angles = positions.astype(F32)[:, None] * frequency[None, :]
    return (jnp.cos(angles), jnp.sin(angles))


def rotate(head, cosine, sine):
    half = head.shape[-1] // 2
    first, second = head[:, :half], head[:, half:]
    return jnp.concatenate(
        [first * cosine - second * sine, second * cosine + first * sine], axis=-1
    )


def sequence_layout(lens, total):
    rows = jnp.arange(total, dtype=jnp.int32)
    ends = jnp.cumsum(lens)
    segment = jnp.sum((rows[:, None] >= ends[None, :]).astype(jnp.int32), axis=1)
    starts = ends - lens
    which = segment[:, None] == jnp.arange(lens.shape[0], dtype=jnp.int32)[None, :]
    begin = jnp.sum(jnp.where(which, starts[None, :], 0), axis=1)
    return (segment, rows - begin)


def mm(left, right):
    return jnp.dot(left, right, preferred_element_type=F32)


def outer_sum(left, right):
    return lax.dot_general(left, right, (((0,), (0,)), ((), ())), preferred_element_type=F32)


def times_transposed(left, right):
    return lax.dot_general(left, right, (((1,), (1,)), ((), ())), preferred_element_type=F32)


def masked_scores(query, key, seg_query, seg_key, row_start, key_start):
    scores = times_transposed(query, key) * (1.0 / math.sqrt(HEAD_SIZE))
    rows = row_start + lax.broadcasted_iota(jnp.int32, scores.shape, 0)
    keys = key_start + lax.broadcasted_iota(jnp.int32, scores.shape, 1)
    allowed = (seg_query == seg_key) & (rows >= keys)
    scores = jnp.where(allowed, scores, NEGATIVE)
    expo = jnp.exp(scores - jnp.max(scores, axis=-1, keepdims=True))
    return expo / jnp.sum(expo, axis=-1, keepdims=True)


def query_blocks(total):
    size = LONGEST
    return [
        (start, start + size, max(0, start - LONGEST)) for start in range(0, total, size)
    ]


def place_rows(place_ref, piece_refs, rows_ref):
    here = place_ref[0]
    size = piece_refs[0].shape[1]
    for step, piece in enumerate(piece_refs):
        start = pl.multiple_of(jnp.bitwise_xor(here, step) * size, size)
        rows_ref[pl.ds(start, size), :] = piece[0]


def spread_rows(place_ref, rows_ref, kept_ref, sent_ref):
    here = place_ref[0]
    size = kept_ref.shape[2]
    for step in range(4):
        start = pl.multiple_of(jnp.bitwise_xor(here, step) * size, size)
        out_ref = sent_ref if step % 2 else kept_ref
        out_ref[step // 2, 0] = rows_ref[pl.ds(start, size), :]


def attention_forward_kernel(
    query_heads,
    place_ref,
    piece0,
    piece1,
    piece2,
    piece3,
    own_ref,
    other_ref,
    output_ref,
    cosine_ref,
    sine_ref,
    seg_query_ref,
    seg_key_ref,
    normed_ref,
    fused_ref,
    heads_ref,
    kept_ref,
    sent_ref,
    rows_ref,
    sums_ref,
):
    place_rows(place_ref, (piece0, piece1, piece2, piece3), rows_ref)
    normed_ref[...] = rows_ref[...]
    half = own_ref.shape[0]
    fused = mm(rows_ref[:, :half], own_ref[...]) + mm(rows_ref[:, half:], other_ref[...])
    cosine, sine = cosine_ref[0], sine_ref[0]
    total = rows_ref.shape[0]
    kv_heads = fused.shape[1] // HEAD_SIZE - query_heads
    for head in range(query_heads + kv_heads // 2):
        columns = slice(head * HEAD_SIZE, (head + 1) * HEAD_SIZE)
        fused_ref[:, columns] = rotate(fused[:, columns], cosine, sine).astype(BF16)
    first_value = (query_heads + kv_heads // 2) * HEAD_SIZE
    fused_ref[:, first_value:] = fused[:, first_value:].astype(BF16)
    per_group = 2 * query_heads // kv_heads
    for head in range(query_heads):
        group = head // per_group
        columns = slice(head * HEAD_SIZE, (head + 1) * HEAD_SIZE)
        at_key = (query_heads + group) * HEAD_SIZE
        at_value = first_value + group * HEAD_SIZE
        for start, stop, low in query_blocks(total):
            probs = masked_scores(
                fused_ref[start:stop, columns],
                fused_ref[low:stop, at_key : at_key + HEAD_SIZE],
                seg_query_ref[0, start:stop],
                seg_key_ref[0, :, low:stop],
                start,
                low,
            )
            heads_ref[start:stop, columns] = mm(
                probs.astype(BF16), fused_ref[low:stop, at_value : at_value + HEAD_SIZE]
            ).astype(BF16)
    sums_ref[...] = mm(heads_ref[...], output_ref[...]).astype(BF16)
    spread_rows(place_ref, sums_ref, kept_ref, sent_ref)


def attention_backward_kernel(
    query_heads,
    block_rows,
    place_ref,
    piece0,
    piece1,
    piece2,
    piece3,
    own_ref,
    other_ref,
    output_ref,
    cosine_ref,
    sine_ref,
    seg_query_ref,
    seg_key_ref,
    normed_ref,
    fused_ref,
    heads_ref,
    kept_ref,
    sent_ref,
    fused_kept_ref,
    fused_sent_ref,
    output_kept_ref,
    output_sent_ref,
    rows_ref,
    sums_ref,
    d_heads_ref,
    d_fused_ref,
    d_key_ref,
    d_value_ref,
    fused_acc,
    output_acc,
):
    index = pl.program_id(0)
    scale = 1.0 / math.sqrt(HEAD_SIZE)
    place_rows(place_ref, (piece0, piece1, piece2, piece3), rows_ref)
    d_heads_ref[...] = times_transposed(rows_ref[...], output_ref[...]).astype(BF16)
    cosine, sine = cosine_ref[0], sine_ref[0]
    total = rows_ref.shape[0]
    kv_heads = fused_ref.shape[1] // HEAD_SIZE - query_heads
    first_value = (query_heads + kv_heads // 2) * HEAD_SIZE
    per_group = 2 * query_heads // kv_heads
    for group in range(kv_heads // 2):
        at_key = (query_heads + group) * HEAD_SIZE
        at_value = first_value + group * HEAD_SIZE
        d_key_ref[...] = jnp.zeros_like(d_key_ref)
        d_value_ref[...] = jnp.zeros_like(d_value_ref)
        for head in range(group * per_group, (group + 1) * per_group):
            columns = slice(head * HEAD_SIZE, (head + 1) * HEAD_SIZE)
            for start, stop, low in query_blocks(total):
                query = fused_ref[start:stop, columns]
                key = fused_ref[low:stop, at_key : at_key + HEAD_SIZE]
                value = fused_ref[low:stop, at_value : at_value + HEAD_SIZE]
                d_heads = d_heads_ref[start:stop, columns]
                probs = masked_scores(
                    query,
                    key,
                    seg_query_ref[0, start:stop],
                    seg_key_ref[0, :, low:stop],
                    start,
                    low,
                )
                d_probs = times_transposed(d_heads, value)
                delta = jnp.sum(probs * d_probs, axis=-1, keepdims=True)
                d_scores = (probs * (d_probs - delta)).astype(BF16)
                d_query = mm(d_scores, key) * scale
                d_fused_ref[start:stop, columns] = rotate(
                    d_query, cosine[start:stop], -sine[start:stop]
                ).astype(BF16)
                d_key_ref[low:stop] += outer_sum(d_scores, query) * scale
                d_value_ref[low:stop] += outer_sum(probs.astype(BF16), d_heads)
        d_fused_ref[:, at_key : at_key + HEAD_SIZE] = rotate(
            d_key_ref[...], cosine, -sine
        ).astype(BF16)
        d_fused_ref[:, at_value : at_value + HEAD_SIZE] = d_value_ref[...].astype(BF16)
    half = own_ref.shape[0]
    sums_ref[:, :half] = times_transposed(d_fused_ref[...], own_ref[...]).astype(BF16)
    sums_ref[:, half:] = times_transposed(d_fused_ref[...], other_ref[...]).astype(BF16)
    spread_rows(place_ref, sums_ref, kept_ref, sent_ref)
    fused_part = outer_sum(normed_ref[...], d_fused_ref[...])
    output_part = outer_sum(heads_ref[...], rows_ref[...])

    @pl.when(index == 0)
    def _():
        fused_acc[...] = fused_part
        output_acc[...] = output_part

    @pl.when(index > 0)
    def _():
        fused_acc[...] += fused_part
        output_acc[...] += output_part

    @pl.when(index == pl.num_programs(0) - 1)
    def _():
        fused_kept_ref[...] = fused_acc[:half].astype(BF16)
        fused_sent_ref[...] = fused_acc[half:].astype(BF16)
        here_x = place_ref[1]
        size = block_rows
        for step in range(output_acc.shape[0] // (2 * size)):
            kept = pl.multiple_of((2 * step + here_x) * size, size)
            sent = pl.multiple_of((2 * step + 1 - here_x) * size, size)
            rows = slice(step * size, (step + 1) * size)
            output_kept_ref[rows] = output_acc[pl.ds(kept, size), :].astype(BF16)
            output_sent_ref[rows] = output_acc[pl.ds(sent, size), :].astype(BF16)


def whole_spec(shape):
    zeros = (0,) * len(shape)
    return pl.BlockSpec(shape, lambda *_: zeros, pipeline_mode=pl.Buffered(1))


def attention_specs(pieces, own, other, output_full, tables, segments):
    micro, rows, width = pieces[0].shape
    total = 4 * rows
    half = tables[0].shape[-1]
    return (
        [pl.BlockSpec(memory_space=pltpu.SMEM)]
        + [pl.BlockSpec((1, rows, width), lambda m: (m, 0, 0))] * 4
        + [whole_spec(own.shape), whole_spec(other.shape), whole_spec(output_full.shape)]
        + [pl.BlockSpec((1, total, half), lambda m: (m, 0, 0))] * 2
        + [
            pl.BlockSpec((1, total, 1), lambda m: (m, 0, 0)),
            pl.BlockSpec((1, 1, total), lambda m: (m, 0, 0)),
        ]
    )


def attention_forward(place, pieces, own, other, output_full, tables, segments):
    micro, rows, width = pieces[0].shape
    total = 4 * rows
    query_cols, fused_cols = output_full.shape[0], own.shape[1]

    def by_micro(columns):
        return pl.BlockSpec((total, columns), lambda m: (m, 0))

    return pl.pallas_call(
        functools.partial(attention_forward_kernel, query_cols // HEAD_SIZE),
        grid=(micro,),
        in_specs=attention_specs(pieces, own, other, output_full, tables, segments),
        out_specs=[
            by_micro(width),
            by_micro(fused_cols),
            by_micro(query_cols),
            pl.BlockSpec((2, 1, rows, width), lambda m: (0, m, 0, 0)),
            pl.BlockSpec((2, 1, rows, width), lambda m: (0, m, 0, 0)),
        ],
        out_shape=[
            jax.ShapeDtypeStruct((micro * total, width), BF16),
            jax.ShapeDtypeStruct((micro * total, fused_cols), BF16),
            jax.ShapeDtypeStruct((micro * total, query_cols), BF16),
            jax.ShapeDtypeStruct((2, micro, rows, width), BF16),
            jax.ShapeDtypeStruct((2, micro, rows, width), BF16),
        ],
        scratch_shapes=[pltpu.VMEM((total, width), BF16), pltpu.VMEM((total, width), BF16)],
        compiler_params=pltpu.CompilerParams(vmem_limit_bytes=56 << 20),
    )(place, *pieces, own, other, output_full, *tables, *segments)


def attention_backward(
    place, pieces, own, other, output_full, tables, segments, normed, fused, heads, block_rows
):
    micro, rows, width = pieces[0].shape
    total = 4 * rows
    query_cols, fused_cols = output_full.shape[0], own.shape[1]

    def by_micro(columns):
        return pl.BlockSpec((total, columns), lambda m: (m, 0))

    return pl.pallas_call(
        functools.partial(attention_backward_kernel, query_cols // HEAD_SIZE, block_rows),
        grid=(micro,),
        in_specs=attention_specs(pieces, own, other, output_full, tables, segments)
        + [by_micro(width), by_micro(fused_cols), by_micro(query_cols)],
        out_specs=[
            pl.BlockSpec((2, 1, rows, width), lambda m: (0, m, 0, 0)),
            pl.BlockSpec((2, 1, rows, width), lambda m: (0, m, 0, 0)),
            whole_spec((width // 2, fused_cols)),
            whole_spec((width // 2, fused_cols)),
            whole_spec((query_cols // 2, width)),
            whole_spec((query_cols // 2, width)),
        ],
        out_shape=[
            jax.ShapeDtypeStruct((2, micro, rows, width), BF16),
            jax.ShapeDtypeStruct((2, micro, rows, width), BF16),
            jax.ShapeDtypeStruct((width // 2, fused_cols), BF16),
            jax.ShapeDtypeStruct((width // 2, fused_cols), BF16),
            jax.ShapeDtypeStruct((query_cols // 2, width), BF16),
            jax.ShapeDtypeStruct((query_cols // 2, width), BF16),
        ],
        scratch_shapes=[
            pltpu.VMEM((total, width), BF16),
            pltpu.VMEM((total, width), BF16),
            pltpu.VMEM((total, query_cols), BF16),
            pltpu.VMEM((total, fused_cols), BF16),
            pltpu.VMEM((total, HEAD_SIZE), F32),
            pltpu.VMEM((total, HEAD_SIZE), F32),
            pltpu.VMEM((width, fused_cols), F32),
            pltpu.VMEM((query_cols, width), F32),
        ],
        compiler_params=pltpu.CompilerParams(vmem_limit_bytes=60 << 20),
    )(place, *pieces, own, other, output_full, *tables, *segments, normed, fused, heads)


def feedforward_kernel(count, last, normed_ref, cot_ref, weights_ref, *refs):
    refs = list(refs)
    earlier = [[refs.pop(0) for _ in range(3)] for _ in range(count)]
    down_ref = refs.pop()
    hidden_ref, d_both_ref, *sums = refs
    pieces, _, fused = weights_ref.shape
    columns, width = down_ref.shape
    rows, piece = width // pieces, columns // pieces
    index = pl.program_id(0)

    @pl.when(index == 0)
    def _():
        for step in range(pieces):
            for part in range(width // fused):
                start = rows + part * piece
                down_ref[step * piece : (step + 1) * piece, part * fused : (part + 1) * fused] = (
                    weights_ref[step, start : start + piece, :]
                )

    both = mm(normed_ref[:, :rows], weights_ref[0, :rows, :])
    for step in range(1, pieces):
        both = both + mm(normed_ref[:, step * rows : (step + 1) * rows], weights_ref[step, :rows, :])
    gate, upward = both[:, :columns], both[:, columns:]
    sigmoid = 1.0 / (1.0 + jnp.exp(-gate))
    silu = gate * sigmoid
    hidden_ref[...] = (silu * upward).astype(BF16)
    d_hidden = times_transposed(cot_ref[...], down_ref[...])
    d_both_ref[:, :columns] = (
        d_hidden * upward * sigmoid * (1.0 + gate * (1.0 - sigmoid))
    ).astype(BF16)
    d_both_ref[:, columns:] = (d_hidden * silu).astype(BF16)

    if not last:
        return

    def write(out_ref, d_normed_ref):
        for part in range(width // fused):
            at = slice(part * fused, (part + 1) * fused)
            start = rows + part * piece
            out = mm(hidden_ref[...], down_ref[:, at])
            for hidden_before, _, weights_before in earlier:
                for step in range(pieces):
                    out = out + mm(
                        hidden_before[:, step * piece : (step + 1) * piece],
                        weights_before[step, start : start + piece, :],
                    )
            out_ref[:, at] = out.astype(BF16)
        for step in range(pieces):
            at = slice(step * rows, (step + 1) * rows)
            d_normed = times_transposed(d_both_ref[...], weights_ref[step, :rows, :])
            for _, d_both_before, weights_before in earlier:
                d_normed = d_normed + times_transposed(
                    d_both_before[...], weights_before[step, :rows, :]
                )
            d_normed_ref[:, at] = d_normed.astype(BF16)

    @pl.when(index < 4)
    def _():
        write(*sums[1::2])

    @pl.when(index >= 4)
    def _():
        write(*sums[0::2])


def feedforward(normed, cot, weights, columns, earlier, last):
    rows, width = normed.shape
    size = rows // 8

    def blocks(count):
        return pl.BlockSpec((size, count), lambda i: ((i + 4) % 8, 0))

    sums, shapes = [], []
    if last:
        sums = [
            pl.BlockSpec((size, width), lambda i: (jnp.maximum(i - 4, 0), 0)),
            pl.BlockSpec((size, width), lambda i: (jnp.minimum(i, 3), 0)),
        ] * 2
        shapes = [jax.ShapeDtypeStruct((rows // 2, width), BF16)] * 4
    earlier_specs = [
        spec
        for _, _, before in earlier
        for spec in (blocks(columns), blocks(2 * columns), whole_spec(before.shape))
    ]
    return pl.pallas_call(
        functools.partial(feedforward_kernel, len(earlier), last),
        grid=(8,),
        in_specs=[blocks(width), blocks(width), whole_spec(weights.shape)] + earlier_specs,
        out_specs=[blocks(columns), blocks(2 * columns)] + sums,
        out_shape=[
            jax.ShapeDtypeStruct((rows, columns), BF16),
            jax.ShapeDtypeStruct((rows, 2 * columns), BF16),
        ]
        + shapes,
        scratch_shapes=[pltpu.VMEM((columns, width), BF16)],
        compiler_params=pltpu.CompilerParams(vmem_limit_bytes=56 << 20),
    )(normed, cot, weights, *[array for before in earlier for array in before])


def feedforward_grads_kernel(normed_ref, d_both_ref, hidden_ref, cot_ref, out_ref, down_ref):
    index = pl.program_id(0)
    rows, fused = normed_ref.shape[1], d_both_ref.shape[1]
    piece = down_ref.shape[0] // pl.num_programs(0)

    @pl.when(index == 0)
    def _():
        down_ref[...] = outer_sum(hidden_ref[...], cot_ref[...]).astype(BF16)

    out_ref[0, :rows, :] = outer_sum(normed_ref[...], d_both_ref[...]).astype(BF16)
    mine = down_ref[pl.ds(pl.multiple_of(index * piece, piece), piece), :]
    for part in range(down_ref.shape[1] // fused):
        start = rows + part * piece
        out_ref[0, start : start + piece, :] = mine[:, part * fused : (part + 1) * fused]


def feedforward_grads(normed, d_both, hidden, cot, pieces):
    rows, width = normed.shape
    columns = hidden.shape[1]
    fused = d_both.shape[1]
    out_rows = width // pieces + (columns // pieces) * (width // fused)
    return pl.pallas_call(
        feedforward_grads_kernel,
        grid=(pieces,),
        in_specs=[
            pl.BlockSpec((rows, width // pieces), lambda i: (0, i)),
            whole_spec(d_both.shape),
            whole_spec(hidden.shape),
            whole_spec(cot.shape),
        ],
        out_specs=pl.BlockSpec((1, out_rows, fused), lambda i: (i, 0, 0)),
        out_shape=jax.ShapeDtypeStruct((pieces, out_rows, fused), BF16),
        scratch_shapes=[pltpu.VMEM((columns, width), BF16)],
        compiler_params=pltpu.CompilerParams(vmem_limit_bytes=56 << 20),
    )(normed, d_both, hidden, cot)


def split_kernel(pieces, place_ref, gate_ref, up_ref, *refs):
    here_x = place_ref[1]
    chunks = len(refs) // 2
    size = gate_ref.shape[1] // (2 * chunks * pieces)
    for chunk in range(chunks):
        sides = []
        for side in range(2):
            starts = [(2 * chunks * step + side * chunks + chunk) * size for step in range(pieces)]
            sides.append(
                jnp.concatenate(
                    [ref[:, at : at + size] for ref in (gate_ref, up_ref) for at in starts], axis=1
                )
            )
        refs[2 * chunk][...] = jnp.where(here_x == 0, sides[0], sides[1])
        refs[2 * chunk + 1][...] = jnp.where(here_x == 0, sides[1], sides[0])


def split(place, gate, up, pieces):
    rows, columns = gate.shape
    size = min(rows, 64)
    fused = 2 * columns // (2 * CHUNKS)
    return pl.pallas_call(
        functools.partial(split_kernel, pieces),
        grid=(rows // size,),
        in_specs=[pl.BlockSpec(memory_space=pltpu.SMEM)]
        + [pl.BlockSpec((size, columns), lambda i: (i, 0))] * 2,
        out_specs=[pl.BlockSpec((size, fused), lambda i: (i, 0))] * (2 * CHUNKS),
        out_shape=[jax.ShapeDtypeStruct((rows, fused), BF16)] * (2 * CHUNKS),
    )(place, gate, up)


def assemble_kernel(pieces, place_ref, *refs):
    inputs, outputs = refs[:-2], refs[-2:]
    here_x = place_ref[1]
    chunks = len(inputs) // 2
    half = inputs[0].shape[1] // 2
    size = half // pieces
    for which, out_ref in enumerate(outputs):
        for step in range(pieces):
            columns = slice(which * half + step * size, which * half + (step + 1) * size)
            own = [inputs[2 * chunk][:, columns].astype(F32) for chunk in range(chunks)]
            moved = [inputs[2 * chunk + 1][:, columns].astype(F32) for chunk in range(chunks)]
            even = [jnp.where(here_x == 0, a, b) for a, b in zip(own, moved)]
            odd = [jnp.where(here_x == 0, b, a) for a, b in zip(own, moved)]
            span = 2 * chunks * size
            out_ref[:, step * span : (step + 1) * span] = jnp.concatenate(even + odd, axis=1)


def assemble(place, inputs, pieces, columns):
    rows, width = inputs[0].shape
    size = min(rows, 64)
    return pl.pallas_call(
        functools.partial(assemble_kernel, pieces),
        grid=(rows // size,),
        in_specs=[pl.BlockSpec(memory_space=pltpu.SMEM)]
        + [pl.BlockSpec((size, width), lambda i: (i, 0))] * len(inputs),
        out_specs=[pl.BlockSpec((size, columns), lambda i: (i, 0))] * 2,
        out_shape=[jax.ShapeDtypeStruct((rows, columns), F32)] * 2,
    )(place, *inputs)


def norm_backward(values, scale, gain, d_normed):
    weighted = d_normed * gain
    d_values = scale * weighted - values * scale * scale * scale * jnp.mean(
        weighted * values, axis=-1, keepdims=True
    )
    return (d_values, jnp.sum(d_normed * values * scale, axis=0))


def take(array, index, axis=0):
    return lax.dynamic_index_in_dim(array, index, axis, keepdims=False)


def choose(position, own, other):
    return [jnp.where(position == 0, own, other), jnp.where(position == 0, other, own)]


def in_order(position, own, other, axis=0):
    return jnp.stack(choose(position, own, other), axis=axis)


def rows_major(array):
    return with_layout_constraint(array, Layout(major_to_minor=tuple(range(array.ndim))))


def gather_z(piece):
    return rows_major(lax.all_gather(rows_major(piece), "z", axis=0))


def gather_z_small(piece):
    size, here = lax.axis_size("z"), lax.axis_index("z")
    if size != 4:
        return [gather_z(piece)]
    return [piece] + [lax.ppermute(piece, "z", pairs) for pairs in (Z_NEAR, Z_FAR, Z_ACROSS)]


def join_pieces(pieces):
    if len(pieces) == 1:
        return pieces[0]
    here = lax.axis_index("z")
    whole = jnp.zeros((len(pieces),) + pieces[0].shape, pieces[0].dtype)
    for step, part in enumerate(pieces):
        whole = lax.dynamic_update_index_in_dim(whole, part, here ^ step, 0)
    return whole


def reduce_z(parts):
    return lax.psum_scatter(parts, "z", scatter_dimension=0)


def tie(*values):
    return lax.optimization_barrier(values)


def swap_blocks(rows, size, here):
    blocks = []
    for start in range(0, rows.shape[1], 2 * size):
        first, second = rows[:, start : start + size], rows[:, start + size : start + 2 * size]
        blocks += choose(here, first, second)
    return blocks


def gather_tensor(rows):
    beside = lax.ppermute(rows, "y", SWAP)
    return (
        rows,
        lax.ppermute(rows, "c", SWAP),
        beside,
        lax.ppermute(beside, "c", SWAP),
    )


def reduce_tensor(kept, sent):
    arrived = lax.ppermute(sent, "c", SWAP).astype(F32)
    moved = (kept[1].astype(F32) + arrived[1]).astype(BF16)
    return kept[0].astype(F32) + arrived[0] + lax.ppermute(moved, "y", SWAP).astype(F32)


def gather_planes(rows):
    return (
        rows,
        lax.ppermute(rows, "x", SWAP),
        lax.ppermute(rows, "y", SWAP),
        lax.ppermute(rows, ("x", "y"), DIAGONAL),
    )


def join_planes(planes):
    return jnp.concatenate(planes + tuple(lax.ppermute(plane, "c", SWAP) for plane in planes))


def reduce_eight(kept, sent):
    kept = kept.reshape((4, kept.shape[0] // 4) + kept.shape[1:])
    arrived = lax.ppermute(sent.reshape(kept.shape), "c", SWAP)
    sums = [kept[step].astype(F32) + arrived[step].astype(F32) for step in range(4)]
    return sums[0], [part.astype(BF16) for part in sums[1:]]


def send_eight(leaving):
    routes = (("x", SWAP), ("y", SWAP), (("x", "y"), DIAGONAL))
    return [lax.ppermute(part, axes, pairs) for part, (axes, pairs) in zip(leaving, routes)]


def body(
    tokens,
    cotangent,
    token_slots,
    lengths,
    query_weight,
    key_projection_weight,
    value_projection_weight,
    output_weight,
    gate_weight,
    up_weight,
    down_weight,
    prenorm_gain,
    midnorm_gain,
):
    z_size = lax.axis_size("z")
    here_x = lax.axis_index("x")
    devices = 8 * z_size
    micro, local_rows, width = tokens.shape
    flat_rows = micro * local_rows
    sends = local_rows // devices
    group_rows = 4 * local_rows
    query_cols = query_weight.shape[1]
    kv_cols = key_projection_weight.shape[1]
    fused_cols = query_cols + 2 * kv_cols
    shard_rows = query_weight.shape[0]
    hidden_cols = gate_weight.shape[1]
    block = hidden_cols // (2 * z_size)
    piece = block // CHUNKS
    chunk_cols = z_size * piece
    everywhere = ("z", "x", "y", "c")
    place = jnp.stack([2 * lax.axis_index("y") + lax.axis_index("c"), here_x]).astype(jnp.int32)

    fused_shard = jnp.concatenate(
        [query_weight, key_projection_weight, value_projection_weight], axis=1
    )
    fused_shard, token_slots = tie(fused_shard, token_slots)

    rank = jnp.sum(
        (token_slots[:, None, :] < token_slots[:, :, None]).astype(jnp.int32), axis=2
    )
    order = (
        (rank // sends) * (micro * sends)
        + jnp.arange(micro, dtype=jnp.int32)[:, None] * sends
        + rank % sends
    ).reshape(flat_rows)
    places = jnp.arange(flat_rows, dtype=jnp.int32)
    to_send = (places[:, None] == order[None, :]).astype(BF16)
    local_slot = (token_slots % local_rows).reshape(flat_rows)

    def by_device(rows):
        return rows.reshape((devices, micro * sends) + rows.shape[1:])

    def exchange(blocks):
        return lax.all_to_all(
            blocks, everywhere, split_axis=0, concat_axis=0, tiled=True
        ).reshape((flat_rows,) + blocks.shape[2:])

    gains = jnp.stack([prenorm_gain, midnorm_gain]).reshape(micro * sends, -1)
    leaving = jnp.concatenate(
        [
            tokens.reshape(flat_rows, width),
            jnp.broadcast_to(local_slot[:, None], (flat_rows, gains.shape[1])).astype(BF16),
        ],
        axis=1,
    )
    leaving = jnp.concatenate(
        [mm(to_send, leaving).astype(BF16), jnp.tile(gains, (devices, 1))], axis=1
    )
    leaving, gate_weight, down_weight, cotangent = tie(
        by_device(leaving), gate_weight, down_weight, cotangent
    )
    arrived = exchange(leaving)
    cot_leaving = mm(to_send, cotangent.reshape(flat_rows, width)).astype(BF16)
    cot_leaving, arrived = tie(cot_leaving, arrived)
    arrived_cot = exchange(by_device(cot_leaving))
    arrived_tokens = arrived[:, :width]
    arrived_slots = arrived[:, width].astype(jnp.int32)
    arrived_gains = arrived[:, width + gains.shape[1] :].reshape(
        2 * z_size, 4, 2, -1, gains.shape[1]
    )[:, 0]
    gains = jnp.swapaxes(arrived_gains, 0, 1).reshape(2, width).astype(F32)
    gain_one, gain_two = gains[0:1], gains[1:2]
    arrived_micro = (places // sends) % micro
    to_place = (
        (arrived_slots + arrived_micro * local_rows)[:, None] == places[None, :]
    ).astype(BF16)

    halves = split(place, gate_weight, up_weight, z_size)
    ff_shards = []
    for chunk in range(CHUNKS):
        kept, leaving = halves[2 * chunk : 2 * chunk + 2]
        down = down_weight[chunk * piece : (chunk + 1) * piece]
        down_parts = [
            down[:, start : start + 2 * chunk_cols] for start in range(0, width, 2 * chunk_cols)
        ]
        ff_shards.append(
            jnp.concatenate(
                choose(here_x, kept, lax.ppermute(leaving, "x", SWAP)) + down_parts
            )
        )

    fused_own = gather_z(fused_shard).reshape(width // 2, fused_cols)
    output_pieces = gather_z_small(output_weight)
    crossed = lax.ppermute(output_pieces[0], "x", SWAP)
    count = len(output_pieces)
    fused_own, arrived_tokens, crossed, *rest = tie(
        fused_own, arrived_tokens, crossed, *output_pieces, *ff_shards
    )
    output_pieces, ff_shards = rest[:count], rest[count:]
    crossed = [crossed] + [lax.ppermute(part, "x", SWAP) for part in output_pieces[1:]]
    *crossed, fused_own = tie(*crossed, fused_own)
    output_own, output_other = join_pieces(output_pieces), join_pieces(crossed)
    ff_weights = [gather_z(ff_shards[0])]
    fused_other = lax.ppermute(fused_own, "x", SWAP)

    inputs = outer_sum(to_place, arrived_tokens)
    first_scale = rms_scale(inputs)
    first_normed = (inputs * first_scale * gain_one).astype(BF16)
    blocks = swap_blocks(first_normed, shard_rows, here_x)
    first_normed = jnp.concatenate(blocks[0::2] + blocks[1::2], axis=1)
    segments, tables = [], []
    for index in range(micro):
        segment, positions = sequence_layout(lengths[index, 0], group_rows)
        segments.append(segment)
        tables.append(rope_tables(positions, HEAD_SIZE))
    segments = jnp.stack(segments)
    segments = (segments[:, :, None], segments[:, None, :])
    tables = tuple(jnp.stack(table) for table in zip(*tables))
    rows_own = first_normed.reshape(micro, local_rows, width)
    rows_beside = lax.ppermute(rows_own, "y", SWAP)
    rows_own, rows_beside, fused_other = tie(rows_own, rows_beside, fused_other)
    output_full = in_order(here_x, output_own, output_other, axis=1).reshape(query_cols, width)
    pieces = (
        rows_own,
        lax.ppermute(rows_own, "c", SWAP),
        rows_beside,
        lax.ppermute(rows_beside, "c", SWAP),
    )
    cot_rows = outer_sum(to_place, arrived_cot).astype(BF16)
    cot_beside = lax.ppermute(cot_rows, "y", SWAP)
    cot_rows, cot_beside, output_full = tie(cot_rows, cot_beside, output_full)
    cot_over_x = lax.ppermute(cot_rows, "x", SWAP)
    cot_across = lax.ppermute(cot_beside, "x", SWAP)
    shared = (fused_own, fused_other, output_full, tables, segments)
    normed_all, fused, heads, kept, sent = attention_forward(place, pieces, *shared)
    kept, sent, cot_over_x = tie(kept, sent, cot_over_x)
    for shard in ff_shards[1:]:
        shard, sent = tie(shard, sent)
        ff_weights.append(gather_z(shard))
    attended = reduce_tensor(kept, sent).reshape(flat_rows, width)
    cot_across, attended = tie(cot_across, attended)
    cot_all = join_planes((cot_rows, cot_over_x, cot_beside, cot_across))
    residual = inputs + attended

    second_scale = rms_scale(residual)
    normed_two = (residual * second_scale * gain_two).astype(BF16)
    planes = list(gather_planes(normed_two))
    planes[1], cot_all = tie(planes[1], cot_all)
    normed_two_all = join_planes(tuple(planes))

    earlier = []
    gate_kept, gate_moved, down_grads = [], [], []
    for chunk in range(CHUNKS):
        last = chunk == CHUNKS - 1
        hidden, d_both, *sums = feedforward(
            normed_two_all,
            cot_all,
            ff_weights[chunk],
            chunk_cols,
            earlier if last else [],
            last,
        )
        earlier.append((hidden, d_both, ff_weights[chunk]))
        if last:
            d_own, d_leaving = reduce_eight(*sums[2:])
            d_both, *d_leaving = tie(d_both, *d_leaving)
        part = feedforward_grads(normed_two_all, d_both, hidden, cot_all, z_size)
        if last:
            part, *d_arrived = tie(part, *send_eight(d_leaving))
        total = reduce_z(part)
        own, other = choose(here_x, total[:shard_rows], total[shard_rows : 2 * shard_rows])
        gate_kept.append(own)
        gate_moved.append(other)
        down_grads.append(
            jnp.concatenate(
                [
                    total[start : start + piece]
                    for start in range(2 * shard_rows, total.shape[0], piece)
                ],
                axis=1,
            )
        )
    down_grad = jnp.concatenate(down_grads, axis=0).astype(F32)

    d_normed_two = d_own + sum(part.astype(F32) for part in d_arrived)
    d_through, d_gain_two = norm_backward(residual, second_scale, gain_two, d_normed_two)
    d_residual = cot_rows.astype(F32) + d_through

    d_residual, *out_parts = tie(d_residual, *sums[:2])
    out_own, out_leaving = reduce_eight(*out_parts)
    pieces = gather_tensor(d_residual.astype(BF16).reshape(micro, local_rows, width))
    out_over_x = lax.ppermute(jnp.stack([out_leaving[0], out_leaving[2]]), "x", SWAP)
    kept, sent, *weight_parts = attention_backward(
        place, pieces, *shared, normed_all, fused, heads, output_weight.shape[0]
    )
    kept, sent, out_over_x = tie(kept, sent, out_over_x)
    out_over_y = (out_leaving[1].astype(F32) + out_over_x[1].astype(F32)).astype(BF16)
    layer_rows = (
        residual
        + (out_own + out_over_x[0].astype(F32))
        + lax.ppermute(out_over_y, "y", SWAP).astype(F32)
    )
    d_normed_one = reduce_tensor(kept, sent).reshape(flat_rows, width)
    swapped = swap_blocks(
        jnp.concatenate(
            [
                d_normed_one[:, side * (width // 2) + start : side * (width // 2) + start + shard_rows]
                for start in range(0, width // 2, shard_rows)
                for side in range(2)
            ],
            axis=1,
        ),
        shard_rows,
        here_x,
    )
    d_normed_one = jnp.concatenate(swapped, axis=1)

    def reduce_x(kept, leaving):
        return (kept.astype(F32) + lax.ppermute(leaving, "x", SWAP).astype(F32)).astype(BF16)

    def reduce_data(total):
        return reduce_z(total.reshape(z_size, -1, total.shape[-1])).astype(F32)

    output_total, fused_sent = tie(reduce_x(*weight_parts[2:]), weight_parts[1])
    fused_total, *gate_moved = tie(reduce_x(weight_parts[0], fused_sent), *gate_moved)
    gate_moved = [lax.ppermute(part, "x", SWAP) for part in gate_moved]
    output_grad = reduce_data(output_total)
    fused_grad = reduce_data(fused_total)
    d_first, d_gain_one = norm_backward(inputs, first_scale, gain_one, d_normed_one)
    input_grads = (d_residual + d_first).astype(BF16)

    gain_grads = jnp.stack([d_gain_one, d_gain_two])
    high = gain_grads.astype(BF16)
    low = (gain_grads - high.astype(F32)).astype(BF16)
    riders = jnp.stack([high, low]).reshape(2, 2, 2 * z_size, 1, shard_rows)
    riders = jnp.broadcast_to(
        jnp.transpose(riders, (2, 3, 0, 1, 4)), (2 * z_size, 4, 2, 2, shard_rows)
    ).reshape(flat_rows, -1)

    back = jnp.concatenate([layer_rows.astype(BF16), input_grads], axis=1)
    returned = exchange(
        by_device(jnp.concatenate([mm(to_place, back).astype(BF16), riders], axis=1))
    )
    gate_up_grads = assemble(
        place, [part for pair in zip(gate_kept, gate_moved) for part in pair], z_size, hidden_cols
    )
    returned, *gate_up_grads = tie(returned, *gate_up_grads)
    outputs = outer_sum(to_send, returned[:, : 2 * width]).astype(BF16)
    outputs = outputs.reshape(micro, local_rows, 2 * width)
    gain_grads = jnp.sum(
        returned[:, 2 * width :].astype(F32).reshape(devices, 2, 2, shard_rows), axis=(0, 1)
    )

    return (
        outputs[:, :, :width],
        outputs[:, :, width:],
        fused_grad[:, :query_cols],
        fused_grad[:, query_cols : query_cols + kv_cols],
        fused_grad[:, query_cols + kv_cols :],
        output_grad,
        *gate_up_grads,
        down_grad,
        gain_grads[0],
        gain_grads[1],
    )


def solution(mesh):
    z_size = mesh.shape["dp"] // 2
    fine = Mesh(mesh.devices.reshape(z_size, 2, 2, 2), ("z", "x", "y", "c"))
    dp, tensor = ("z", "x"), ("y", "c")
    rows, columns, stacked = P(None, dp + tensor, None), P(dp, tensor), P(tensor + dp, None)
    return jax.shard_map(
        body,
        mesh=fine,
        in_specs=(
            rows,
            rows,
            P(None, dp + tensor),
            P(None, dp, None),
            columns,
            columns,
            columns,
            stacked,
            columns,
            columns,
            stacked,
            P(dp),
            P(dp),
        ),
        out_specs=(
            rows,
            rows,
            columns,
            columns,
            columns,
            stacked,
            columns,
            columns,
            stacked,
            P(dp),
            P(dp),
        ),
        check_vma=False,
    )
```

```python
import functools
import math

import jax
import jax.numpy as jnp
from jax import lax
from jax.experimental import pallas as pl
from jax.experimental.layout import Layout, with_layout_constraint
from jax.experimental.pallas import tpu as pltpu
from jax.sharding import Mesh, PartitionSpec as P

HEAD_SIZE = 256
EPSILON = 1e-06
ROPE_BASE = 1000042.0
NEGATIVE = -1e30
LONGEST = 256
CHUNKS = 2
F32 = jnp.float32
BF16 = jnp.bfloat16

SWAP = [(0, 1), (1, 0)]
DIAGONAL = [(0, 3), (3, 0), (1, 2), (2, 1)]
Z_NEAR = [(0, 1), (1, 0), (2, 3), (3, 2)]
Z_FAR = [(0, 2), (2, 0), (1, 3), (3, 1)]
Z_ACROSS = [(0, 3), (3, 0), (1, 2), (2, 1)]


def rms_scale(values):
    return lax.rsqrt(jnp.mean(values * values, axis=-1, keepdims=True) + EPSILON)


def rope_tables(positions, head):
    half = head // 2
    frequency = jnp.exp(jnp.arange(half, dtype=F32) * (-2.0 * math.log(ROPE_BASE) / head))
    angles = positions.astype(F32)[:, None] * frequency[None, :]
    return (jnp.cos(angles), jnp.sin(angles))


def rotate(head, cosine, sine):
    half = head.shape[-1] // 2
    first, second = head[:, :half], head[:, half:]
    return jnp.concatenate(
        [first * cosine - second * sine, second * cosine + first * sine], axis=-1
    )


def sequence_layout(lens, total):
    rows = jnp.arange(total, dtype=jnp.int32)
    ends = jnp.cumsum(lens)
    segment = jnp.sum((rows[:, None] >= ends[None, :]).astype(jnp.int32), axis=1)
    starts = ends - lens
    which = segment[:, None] == jnp.arange(lens.shape[0], dtype=jnp.int32)[None, :]
    begin = jnp.sum(jnp.where(which, starts[None, :], 0), axis=1)
    return (segment, rows - begin)


def mm(left, right):
    return jnp.dot(left, right, preferred_element_type=F32)


def outer_sum(left, right):
    return lax.dot_general(left, right, (((0,), (0,)), ((), ())), preferred_element_type=F32)


def times_transposed(left, right):
    return lax.dot_general(left, right, (((1,), (1,)), ((), ())), preferred_element_type=F32)


def masked_scores(query, key, seg_query, seg_key, row_start, key_start):
    scores = times_transposed(query, key) * (1.0 / math.sqrt(HEAD_SIZE))
    rows = row_start + lax.broadcasted_iota(jnp.int32, scores.shape, 0)
    keys = key_start + lax.broadcasted_iota(jnp.int32, scores.shape, 1)
    allowed = (seg_query == seg_key) & (rows >= keys)
    scores = jnp.where(allowed, scores, NEGATIVE)
    expo = jnp.exp(scores - jnp.max(scores, axis=-1, keepdims=True))
    return expo / jnp.sum(expo, axis=-1, keepdims=True)


def query_blocks(total):
    size = LONGEST
    return [
        (start, start + size, max(0, start - LONGEST)) for start in range(0, total, size)
    ]


def place_rows(place_ref, piece_refs, rows_ref):
    here = place_ref[0]
    size = piece_refs[0].shape[1]
    for step, piece in enumerate(piece_refs):
        start = pl.multiple_of(jnp.bitwise_xor(here, step) * size, size)
        rows_ref[pl.ds(start, size), :] = piece[0]


def spread_rows(place_ref, rows_ref, kept_ref, sent_ref):
    here = place_ref[0]
    size = kept_ref.shape[2]
    for step in range(4):
        start = pl.multiple_of(jnp.bitwise_xor(here, step) * size, size)
        out_ref = sent_ref if step % 2 else kept_ref
        out_ref[step // 2, 0] = rows_ref[pl.ds(start, size), :]


def attention_forward_kernel(
    query_heads,
    place_ref,
    piece0,
    piece1,
    piece2,
    piece3,
    own_ref,
    other_ref,
    output_ref,
    cosine_ref,
    sine_ref,
    seg_query_ref,
    seg_key_ref,
    normed_ref,
    fused_ref,
    heads_ref,
    kept_ref,
    sent_ref,
    rows_ref,
    sums_ref,
):
    place_rows(place_ref, (piece0, piece1, piece2, piece3), rows_ref)
    normed_ref[...] = rows_ref[...]
    half = own_ref.shape[0]
    fused = mm(rows_ref[:, :half], own_ref[...]) + mm(rows_ref[:, half:], other_ref[...])
    cosine, sine = cosine_ref[0], sine_ref[0]
    total = rows_ref.shape[0]
    kv_heads = fused.shape[1] // HEAD_SIZE - query_heads
    for head in range(query_heads + kv_heads // 2):
        columns = slice(head * HEAD_SIZE, (head + 1) * HEAD_SIZE)
        fused_ref[:, columns] = rotate(fused[:, columns], cosine, sine).astype(BF16)
    first_value = (query_heads + kv_heads // 2) * HEAD_SIZE
    fused_ref[:, first_value:] = fused[:, first_value:].astype(BF16)
    per_group = 2 * query_heads // kv_heads
    for head in range(query_heads):
        group = head // per_group
        columns = slice(head * HEAD_SIZE, (head + 1) * HEAD_SIZE)
        at_key = (query_heads + group) * HEAD_SIZE
        at_value = first_value + group * HEAD_SIZE
        for start, stop, low in query_blocks(total):
            probs = masked_scores(
                fused_ref[start:stop, columns],
                fused_ref[low:stop, at_key : at_key + HEAD_SIZE],
                seg_query_ref[0, start:stop],
                seg_key_ref[0, :, low:stop],
                start,
                low,
            )
            heads_ref[start:stop, columns] = mm(
                probs.astype(BF16), fused_ref[low:stop, at_value : at_value + HEAD_SIZE]
            ).astype(BF16)
    sums_ref[...] = mm(heads_ref[...], output_ref[...]).astype(BF16)
    spread_rows(place_ref, sums_ref, kept_ref, sent_ref)


def attention_backward_kernel(
    query_heads,
    block_rows,
    place_ref,
    piece0,
    piece1,
    piece2,
    piece3,
    own_ref,
    other_ref,
    output_ref,
    cosine_ref,
    sine_ref,
    seg_query_ref,
    seg_key_ref,
    normed_ref,
    fused_ref,
    heads_ref,
    kept_ref,
    sent_ref,
    fused_kept_ref,
    fused_sent_ref,
    output_kept_ref,
    output_sent_ref,
    rows_ref,
    sums_ref,
    d_heads_ref,
    d_fused_ref,
    d_key_ref,
    d_value_ref,
    fused_acc,
    output_acc,
):
    index = pl.program_id(0)
    scale = 1.0 / math.sqrt(HEAD_SIZE)
    place_rows(place_ref, (piece0, piece1, piece2, piece3), rows_ref)
    d_heads_ref[...] = times_transposed(rows_ref[...], output_ref[...]).astype(BF16)
    cosine, sine = cosine_ref[0], sine_ref[0]
    total = rows_ref.shape[0]
    kv_heads = fused_ref.shape[1] // HEAD_SIZE - query_heads
    first_value = (query_heads + kv_heads // 2) * HEAD_SIZE
    per_group = 2 * query_heads // kv_heads
    for group in range(kv_heads // 2):
        at_key = (query_heads + group) * HEAD_SIZE
        at_value = first_value + group * HEAD_SIZE
        d_key_ref[...] = jnp.zeros_like(d_key_ref)
        d_value_ref[...] = jnp.zeros_like(d_value_ref)
        for head in range(group * per_group, (group + 1) * per_group):
            columns = slice(head * HEAD_SIZE, (head + 1) * HEAD_SIZE)
            for start, stop, low in query_blocks(total):
                query = fused_ref[start:stop, columns]
                key = fused_ref[low:stop, at_key : at_key + HEAD_SIZE]
                value = fused_ref[low:stop, at_value : at_value + HEAD_SIZE]
                d_heads = d_heads_ref[start:stop, columns]
                probs = masked_scores(
                    query,
                    key,
                    seg_query_ref[0, start:stop],
                    seg_key_ref[0, :, low:stop],
                    start,
                    low,
                )
                d_probs = times_transposed(d_heads, value)
                delta = jnp.sum(probs * d_probs, axis=-1, keepdims=True)
                d_scores = (probs * (d_probs - delta)).astype(BF16)
                d_query = mm(d_scores, key) * scale
                d_fused_ref[start:stop, columns] = rotate(
                    d_query, cosine[start:stop], -sine[start:stop]
                ).astype(BF16)
                d_key_ref[low:stop] += outer_sum(d_scores, query) * scale
                d_value_ref[low:stop] += outer_sum(probs.astype(BF16), d_heads)
        d_fused_ref[:, at_key : at_key + HEAD_SIZE] = rotate(
            d_key_ref[...], cosine, -sine
        ).astype(BF16)
        d_fused_ref[:, at_value : at_value + HEAD_SIZE] = d_value_ref[...].astype(BF16)
    half = own_ref.shape[0]
    sums_ref[:, :half] = times_transposed(d_fused_ref[...], own_ref[...]).astype(BF16)
    sums_ref[:, half:] = times_transposed(d_fused_ref[...], other_ref[...]).astype(BF16)
    spread_rows(place_ref, sums_ref, kept_ref, sent_ref)
    fused_part = outer_sum(normed_ref[...], d_fused_ref[...])
    output_part = outer_sum(heads_ref[...], rows_ref[...])

    @pl.when(index == 0)
    def _():
        fused_acc[...] = fused_part
        output_acc[...] = output_part

    @pl.when(index > 0)
    def _():
        fused_acc[...] += fused_part
        output_acc[...] += output_part

    @pl.when(index == pl.num_programs(0) - 1)
    def _():
        fused_kept_ref[...] = fused_acc[:half].astype(BF16)
        fused_sent_ref[...] = fused_acc[half:].astype(BF16)
        here_x = place_ref[1]
        size = block_rows
        for step in range(output_acc.shape[0] // (2 * size)):
            kept = pl.multiple_of((2 * step + here_x) * size, size)
            sent = pl.multiple_of((2 * step + 1 - here_x) * size, size)
            rows = slice(step * size, (step + 1) * size)
            output_kept_ref[rows] = output_acc[pl.ds(kept, size), :].astype(BF16)
            output_sent_ref[rows] = output_acc[pl.ds(sent, size), :].astype(BF16)


def whole_spec(shape):
    zeros = (0,) * len(shape)
    return pl.BlockSpec(shape, lambda *_: zeros, pipeline_mode=pl.Buffered(1))


def attention_specs(pieces, own, other, output_full, tables, segments):
    micro, rows, width = pieces[0].shape
    total = 4 * rows
    half = tables[0].shape[-1]
    return (
        [pl.BlockSpec(memory_space=pltpu.SMEM)]
        + [pl.BlockSpec((1, rows, width), lambda m: (m, 0, 0))] * 4
        + [whole_spec(own.shape), whole_spec(other.shape), whole_spec(output_full.shape)]
        + [pl.BlockSpec((1, total, half), lambda m: (m, 0, 0))] * 2
        + [
            pl.BlockSpec((1, total, 1), lambda m: (m, 0, 0)),
            pl.BlockSpec((1, 1, total), lambda m: (m, 0, 0)),
        ]
    )


def attention_forward(place, pieces, own, other, output_full, tables, segments):
    micro, rows, width = pieces[0].shape
    total = 4 * rows
    query_cols, fused_cols = output_full.shape[0], own.shape[1]

    def by_micro(columns):
        return pl.BlockSpec((total, columns), lambda m: (m, 0))

    return pl.pallas_call(
        functools.partial(attention_forward_kernel, query_cols // HEAD_SIZE),
        grid=(micro,),
        in_specs=attention_specs(pieces, own, other, output_full, tables, segments),
        out_specs=[
            by_micro(width),
            by_micro(fused_cols),
            by_micro(query_cols),
            pl.BlockSpec((2, 1, rows, width), lambda m: (0, m, 0, 0)),
            pl.BlockSpec((2, 1, rows, width), lambda m: (0, m, 0, 0)),
        ],
        out_shape=[
            jax.ShapeDtypeStruct((micro * total, width), BF16),
            jax.ShapeDtypeStruct((micro * total, fused_cols), BF16),
            jax.ShapeDtypeStruct((micro * total, query_cols), BF16),
            jax.ShapeDtypeStruct((2, micro, rows, width), BF16),
            jax.ShapeDtypeStruct((2, micro, rows, width), BF16),
        ],
        scratch_shapes=[pltpu.VMEM((total, width), BF16), pltpu.VMEM((total, width), BF16)],
        compiler_params=pltpu.CompilerParams(vmem_limit_bytes=56 << 20),
    )(place, *pieces, own, other, output_full, *tables, *segments)


def attention_backward(
    place, pieces, own, other, output_full, tables, segments, normed, fused, heads, block_rows
):
    micro, rows, width = pieces[0].shape
    total = 4 * rows
    query_cols, fused_cols = output_full.shape[0], own.shape[1]

    def by_micro(columns):
        return pl.BlockSpec((total, columns), lambda m: (m, 0))

    return pl.pallas_call(
        functools.partial(attention_backward_kernel, query_cols // HEAD_SIZE, block_rows),
        grid=(micro,),
        in_specs=attention_specs(pieces, own, other, output_full, tables, segments)
        + [by_micro(width), by_micro(fused_cols), by_micro(query_cols)],
        out_specs=[
            pl.BlockSpec((2, 1, rows, width), lambda m: (0, m, 0, 0)),
            pl.BlockSpec((2, 1, rows, width), lambda m: (0, m, 0, 0)),
            whole_spec((width // 2, fused_cols)),
            whole_spec((width // 2, fused_cols)),
            whole_spec((query_cols // 2, width)),
            whole_spec((query_cols // 2, width)),
        ],
        out_shape=[
            jax.ShapeDtypeStruct((2, micro, rows, width), BF16),
            jax.ShapeDtypeStruct((2, micro, rows, width), BF16),
            jax.ShapeDtypeStruct((width // 2, fused_cols), BF16),
            jax.ShapeDtypeStruct((width // 2, fused_cols), BF16),
            jax.ShapeDtypeStruct((query_cols // 2, width), BF16),
            jax.ShapeDtypeStruct((query_cols // 2, width), BF16),
        ],
        scratch_shapes=[
            pltpu.VMEM((total, width), BF16),
            pltpu.VMEM((total, width), BF16),
            pltpu.VMEM((total, query_cols), BF16),
            pltpu.VMEM((total, fused_cols), BF16),
            pltpu.VMEM((total, HEAD_SIZE), F32),
            pltpu.VMEM((total, HEAD_SIZE), F32),
            pltpu.VMEM((width, fused_cols), F32),
            pltpu.VMEM((query_cols, width), F32),
        ],
        compiler_params=pltpu.CompilerParams(vmem_limit_bytes=60 << 20),
    )(place, *pieces, own, other, output_full, *tables, *segments, normed, fused, heads)


def feedforward_kernel(count, last, normed_ref, cot_ref, weights_ref, *refs):
    refs = list(refs)
    earlier = [[refs.pop(0) for _ in range(3)] for _ in range(count)]
    down_ref = refs.pop()
    hidden_ref, d_both_ref, *sums = refs
    pieces, _, fused = weights_ref.shape
    columns, width = down_ref.shape
    rows, piece = width // pieces, columns // pieces
    index = pl.program_id(0)

    @pl.when(index == 0)
    def _():
        for step in range(pieces):
            for part in range(width // fused):
                start = rows + part * piece
                down_ref[step * piece : (step + 1) * piece, part * fused : (part + 1) * fused] = (
                    weights_ref[step, start : start + piece, :]
                )

    both = mm(normed_ref[:, :rows], weights_ref[0, :rows, :])
    for step in range(1, pieces):
        both = both + mm(normed_ref[:, step * rows : (step + 1) * rows], weights_ref[step, :rows, :])
    gate, upward = both[:, :columns], both[:, columns:]
    sigmoid = 1.0 / (1.0 + jnp.exp(-gate))
    silu = gate * sigmoid
    hidden_ref[...] = (silu * upward).astype(BF16)
    d_hidden = times_transposed(cot_ref[...], down_ref[...])
    d_both_ref[:, :columns] = (
        d_hidden * upward * sigmoid * (1.0 + gate * (1.0 - sigmoid))
    ).astype(BF16)
    d_both_ref[:, columns:] = (d_hidden * silu).astype(BF16)

    if not last:
        return

    def write(out_ref, d_normed_ref):
        for part in range(width // fused):
            at = slice(part * fused, (part + 1) * fused)
            start = rows + part * piece
            out = mm(hidden_ref[...], down_ref[:, at])
            for hidden_before, _, weights_before in earlier:
                for step in range(pieces):
                    out = out + mm(
                        hidden_before[:, step * piece : (step + 1) * piece],
                        weights_before[step, start : start + piece, :],
                    )
            out_ref[:, at] = out.astype(BF16)
        for step in range(pieces):
            at = slice(step * rows, (step + 1) * rows)
            d_normed = times_transposed(d_both_ref[...], weights_ref[step, :rows, :])
            for _, d_both_before, weights_before in earlier:
                d_normed = d_normed + times_transposed(
                    d_both_before[...], weights_before[step, :rows, :]
                )
            d_normed_ref[:, at] = d_normed.astype(BF16)

    @pl.when(index < 4)
    def _():
        write(*sums[1::2])

    @pl.when(index >= 4)
    def _():
        write(*sums[0::2])


def feedforward(normed, cot, weights, columns, earlier, last):
    rows, width = normed.shape
    size = rows // 8

    def blocks(count):
        return pl.BlockSpec((size, count), lambda i: ((i + 4) % 8, 0))

    sums, shapes = [], []
    if last:
        sums = [
            pl.BlockSpec((size, width), lambda i: (jnp.maximum(i - 4, 0), 0)),
            pl.BlockSpec((size, width), lambda i: (jnp.minimum(i, 3), 0)),
        ] * 2
        shapes = [jax.ShapeDtypeStruct((rows // 2, width), BF16)] * 4
    earlier_specs = [
        spec
        for _, _, before in earlier
        for spec in (blocks(columns), blocks(2 * columns), whole_spec(before.shape))
    ]
    return pl.pallas_call(
        functools.partial(feedforward_kernel, len(earlier), last),
        grid=(8,),
        in_specs=[blocks(width), blocks(width), whole_spec(weights.shape)] + earlier_specs,
        out_specs=[blocks(columns), blocks(2 * columns)] + sums,
        out_shape=[
            jax.ShapeDtypeStruct((rows, columns), BF16),
            jax.ShapeDtypeStruct((rows, 2 * columns), BF16),
        ]
        + shapes,
        scratch_shapes=[pltpu.VMEM((columns, width), BF16)],
        compiler_params=pltpu.CompilerParams(vmem_limit_bytes=56 << 20),
    )(normed, cot, weights, *[array for before in earlier for array in before])


def feedforward_grads_kernel(normed_ref, d_both_ref, hidden_ref, cot_ref, out_ref, down_ref):
    index = pl.program_id(0)
    rows, fused = normed_ref.shape[1], d_both_ref.shape[1]
    piece = down_ref.shape[0] // pl.num_programs(0)

    @pl.when(index == 0)
    def _():
        down_ref[...] = outer_sum(hidden_ref[...], cot_ref[...]).astype(BF16)

    out_ref[0, :rows, :] = outer_sum(normed_ref[...], d_both_ref[...]).astype(BF16)
    mine = down_ref[pl.ds(pl.multiple_of(index * piece, piece), piece), :]
    for part in range(down_ref.shape[1] // fused):
        start = rows + part * piece
        out_ref[0, start : start + piece, :] = mine[:, part * fused : (part + 1) * fused]


def feedforward_grads(normed, d_both, hidden, cot, pieces):
    rows, width = normed.shape
    columns = hidden.shape[1]
    fused = d_both.shape[1]
    out_rows = width // pieces + (columns // pieces) * (width // fused)
    return pl.pallas_call(
        feedforward_grads_kernel,
        grid=(pieces,),
        in_specs=[
            pl.BlockSpec((rows, width // pieces), lambda i: (0, i)),
            whole_spec(d_both.shape),
            whole_spec(hidden.shape),
            whole_spec(cot.shape),
        ],
        out_specs=pl.BlockSpec((1, out_rows, fused), lambda i: (i, 0, 0)),
        out_shape=jax.ShapeDtypeStruct((pieces, out_rows, fused), BF16),
        scratch_shapes=[pltpu.VMEM((columns, width), BF16)],
        compiler_params=pltpu.CompilerParams(vmem_limit_bytes=56 << 20),
    )(normed, d_both, hidden, cot)


def split_kernel(pieces, place_ref, gate_ref, up_ref, *refs):
    here_x = place_ref[1]
    chunks = len(refs) // 2
    size = gate_ref.shape[1] // (2 * chunks * pieces)
    for chunk in range(chunks):
        sides = []
        for side in range(2):
            starts = [(2 * chunks * step + side * chunks + chunk) * size for step in range(pieces)]
            sides.append(
                jnp.concatenate(
                    [ref[:, at : at + size] for ref in (gate_ref, up_ref) for at in starts], axis=1
                )
            )
        refs[2 * chunk][...] = jnp.where(here_x == 0, sides[0], sides[1])
        refs[2 * chunk + 1][...] = jnp.where(here_x == 0, sides[1], sides[0])


def split(place, gate, up, pieces):
    rows, columns = gate.shape
    size = min(rows, 64)
    fused = 2 * columns // (2 * CHUNKS)
    return pl.pallas_call(
        functools.partial(split_kernel, pieces),
        grid=(rows // size,),
        in_specs=[pl.BlockSpec(memory_space=pltpu.SMEM)]
        + [pl.BlockSpec((size, columns), lambda i: (i, 0))] * 2,
        out_specs=[pl.BlockSpec((size, fused), lambda i: (i, 0))] * (2 * CHUNKS),
        out_shape=[jax.ShapeDtypeStruct((rows, fused), BF16)] * (2 * CHUNKS),
    )(place, gate, up)


def assemble_kernel(pieces, place_ref, *refs):
    inputs, outputs = refs[:-2], refs[-2:]
    here_x = place_ref[1]
    chunks = len(inputs) // 2
    half = inputs[0].shape[1] // 2
    size = half // pieces
    for which, out_ref in enumerate(outputs):
        for step in range(pieces):
            columns = slice(which * half + step * size, which * half + (step + 1) * size)
            own = [inputs[2 * chunk][:, columns].astype(F32) for chunk in range(chunks)]
            moved = [inputs[2 * chunk + 1][:, columns].astype(F32) for chunk in range(chunks)]
            even = [jnp.where(here_x == 0, a, b) for a, b in zip(own, moved)]
            odd = [jnp.where(here_x == 0, b, a) for a, b in zip(own, moved)]
            span = 2 * chunks * size
            out_ref[:, step * span : (step + 1) * span] = jnp.concatenate(even + odd, axis=1)


def assemble(place, inputs, pieces, columns):
    rows, width = inputs[0].shape
    size = min(rows, 64)
    return pl.pallas_call(
        functools.partial(assemble_kernel, pieces),
        grid=(rows // size,),
        in_specs=[pl.BlockSpec(memory_space=pltpu.SMEM)]
        + [pl.BlockSpec((size, width), lambda i: (i, 0))] * len(inputs),
        out_specs=[pl.BlockSpec((size, columns), lambda i: (i, 0))] * 2,
        out_shape=[jax.ShapeDtypeStruct((rows, columns), F32)] * 2,
    )(place, *inputs)


def norm_backward(values, scale, gain, d_normed):
    weighted = d_normed * gain
    d_values = scale * weighted - values * scale * scale * scale * jnp.mean(
        weighted * values, axis=-1, keepdims=True
    )
    return (d_values, jnp.sum(d_normed * values * scale, axis=0))


def take(array, index, axis=0):
    return lax.dynamic_index_in_dim(array, index, axis, keepdims=False)


def choose(position, own, other):
    return [jnp.where(position == 0, own, other), jnp.where(position == 0, other, own)]


def in_order(position, own, other, axis=0):
    return jnp.stack(choose(position, own, other), axis=axis)


def rows_major(array):
    return with_layout_constraint(array, Layout(major_to_minor=tuple(range(array.ndim))))


def gather_z(piece):
    return rows_major(lax.all_gather(rows_major(piece), "z", axis=0))


def gather_z_small(piece):
    size, here = lax.axis_size("z"), lax.axis_index("z")
    if size != 4:
        return [gather_z(piece)]
    return [piece] + [lax.ppermute(piece, "z", pairs) for pairs in (Z_NEAR, Z_FAR, Z_ACROSS)]


def join_pieces(pieces):
    if len(pieces) == 1:
        return pieces[0]
    here = lax.axis_index("z")
    whole = jnp.zeros((len(pieces),) + pieces[0].shape, pieces[0].dtype)
    for step, part in enumerate(pieces):
        whole = lax.dynamic_update_index_in_dim(whole, part, here ^ step, 0)
    return whole


def reduce_z(parts):
    return lax.psum_scatter(parts, "z", scatter_dimension=0)


def tie(*values):
    return lax.optimization_barrier(values)


def swap_blocks(rows, size, here):
    blocks = []
    for start in range(0, rows.shape[1], 2 * size):
        first, second = rows[:, start : start + size], rows[:, start + size : start + 2 * size]
        blocks += choose(here, first, second)
    return blocks


def gather_tensor(rows):
    beside = lax.ppermute(rows, "y", SWAP)
    return (
        rows,
        lax.ppermute(rows, "c", SWAP),
        beside,
        lax.ppermute(beside, "c", SWAP),
    )


def reduce_tensor(kept, sent):
    arrived = lax.ppermute(sent, "c", SWAP).astype(F32)
    moved = (kept[1].astype(F32) + arrived[1]).astype(BF16)
    return kept[0].astype(F32) + arrived[0] + lax.ppermute(moved, "y", SWAP).astype(F32)


def gather_planes(rows):
    return (
        rows,
        lax.ppermute(rows, "x", SWAP),
        lax.ppermute(rows, "y", SWAP),
        lax.ppermute(rows, ("x", "y"), DIAGONAL),
    )


def join_planes(planes):
    return jnp.concatenate(planes + tuple(lax.ppermute(plane, "c", SWAP) for plane in planes))


def reduce_eight(kept, sent):
    kept = kept.reshape((4, kept.shape[0] // 4) + kept.shape[1:])
    arrived = lax.ppermute(sent.reshape(kept.shape), "c", SWAP)
    sums = [kept[step].astype(F32) + arrived[step].astype(F32) for step in range(4)]
    return sums[0], [part.astype(BF16) for part in sums[1:]]


def send_eight(leaving):
    routes = (("x", SWAP), ("y", SWAP), (("x", "y"), DIAGONAL))
    return [lax.ppermute(part, axes, pairs) for part, (axes, pairs) in zip(leaving, routes)]


def body(
    tokens,
    cotangent,
    token_slots,
    lengths,
    query_weight,
    key_projection_weight,
    value_projection_weight,
    output_weight,
    gate_weight,
    up_weight,
    down_weight,
    prenorm_gain,
    midnorm_gain,
):
    z_size = lax.axis_size("z")
    here_x = lax.axis_index("x")
    devices = 8 * z_size
    micro, local_rows, width = tokens.shape
    flat_rows = micro * local_rows
    sends = local_rows // devices
    group_rows = 4 * local_rows
    query_cols = query_weight.shape[1]
    kv_cols = key_projection_weight.shape[1]
    fused_cols = query_cols + 2 * kv_cols
    shard_rows = query_weight.shape[0]
    hidden_cols = gate_weight.shape[1]
    block = hidden_cols // (2 * z_size)
    piece = block // CHUNKS
    chunk_cols = z_size * piece
    everywhere = ("z", "x", "y", "c")
    place = jnp.stack([2 * lax.axis_index("y") + lax.axis_index("c"), here_x]).astype(jnp.int32)

    fused_shard = jnp.concatenate(
        [query_weight, key_projection_weight, value_projection_weight], axis=1
    )
    fused_shard, token_slots = tie(fused_shard, token_slots)

    rank = jnp.sum(
        (token_slots[:, None, :] < token_slots[:, :, None]).astype(jnp.int32), axis=2
    )
    order = (
        (rank // sends) * (micro * sends)
        + jnp.arange(micro, dtype=jnp.int32)[:, None] * sends
        + rank % sends
    ).reshape(flat_rows)
    places = jnp.arange(flat_rows, dtype=jnp.int32)
    to_send = (places[:, None] == order[None, :]).astype(BF16)
    local_slot = (token_slots % local_rows).reshape(flat_rows)

    def by_device(rows):
        return rows.reshape((devices, micro * sends) + rows.shape[1:])

    def exchange(blocks):
        return lax.all_to_all(
            blocks, everywhere, split_axis=0, concat_axis=0, tiled=True
        ).reshape((flat_rows,) + blocks.shape[2:])

    gains = jnp.stack([prenorm_gain, midnorm_gain]).reshape(micro * sends, -1)
    leaving = jnp.concatenate(
        [
            tokens.reshape(flat_rows, width),
            jnp.broadcast_to(local_slot[:, None], (flat_rows, gains.shape[1])).astype(BF16),
        ],
        axis=1,
    )
    leaving = jnp.concatenate(
        [mm(to_send, leaving).astype(BF16), jnp.tile(gains, (devices, 1))], axis=1
    )
    leaving, gate_weight, down_weight, cotangent = tie(
        by_device(leaving), gate_weight, down_weight, cotangent
    )
    arrived = exchange(leaving)
    cot_leaving = mm(to_send, cotangent.reshape(flat_rows, width)).astype(BF16)
    cot_leaving, arrived = tie(cot_leaving, arrived)
    arrived_cot = exchange(by_device(cot_leaving))
    arrived_tokens = arrived[:, :width]
    arrived_slots = arrived[:, width].astype(jnp.int32)
    arrived_gains = arrived[:, width + gains.shape[1] :].reshape(
        2 * z_size, 4, 2, -1, gains.shape[1]
    )[:, 0]
    gains = jnp.swapaxes(arrived_gains, 0, 1).reshape(2, width).astype(F32)
    gain_one, gain_two = gains[0:1], gains[1:2]
    arrived_micro = (places // sends) % micro
    to_place = (
        (arrived_slots + arrived_micro * local_rows)[:, None] == places[None, :]
    ).astype(BF16)

    halves = split(place, gate_weight, up_weight, z_size)
    ff_shards = []
    for chunk in range(CHUNKS):
        kept, leaving = halves[2 * chunk : 2 * chunk + 2]
        down = down_weight[chunk * piece : (chunk + 1) * piece]
        down_parts = [
            down[:, start : start + 2 * chunk_cols] for start in range(0, width, 2 * chunk_cols)
        ]
        ff_shards.append(
            jnp.concatenate(
                choose(here_x, kept, lax.ppermute(leaving, "x", SWAP)) + down_parts
            )
        )

    fused_own = gather_z(fused_shard).reshape(width // 2, fused_cols)
    output_pieces = gather_z_small(output_weight)
    crossed = lax.ppermute(output_pieces[0], "x", SWAP)
    count = len(output_pieces)
    fused_own, arrived_tokens, crossed, *rest = tie(
        fused_own, arrived_tokens, crossed, *output_pieces, *ff_shards
    )
    output_pieces, ff_shards = rest[:count], rest[count:]
    crossed = [crossed] + [lax.ppermute(part, "x", SWAP) for part in output_pieces[1:]]
    *crossed, fused_own = tie(*crossed, fused_own)
    output_own, output_other = join_pieces(output_pieces), join_pieces(crossed)
    ff_weights = [gather_z(ff_shards[0])]
    fused_other = lax.ppermute(fused_own, "x", SWAP)

    inputs = outer_sum(to_place, arrived_tokens)
    first_scale = rms_scale(inputs)
    first_normed = (inputs * first_scale * gain_one).astype(BF16)
    blocks = swap_blocks(first_normed, shard_rows, here_x)
    first_normed = jnp.concatenate(blocks[0::2] + blocks[1::2], axis=1)
    segments, tables = [], []
    for index in range(micro):
        segment, positions = sequence_layout(lengths[index, 0], group_rows)
        segments.append(segment)
        tables.append(rope_tables(positions, HEAD_SIZE))
    segments = jnp.stack(segments)
    segments = (segments[:, :, None], segments[:, None, :])
    tables = tuple(jnp.stack(table) for table in zip(*tables))
    rows_own = first_normed.reshape(micro, local_rows, width)
    rows_beside = lax.ppermute(rows_own, "y", SWAP)
    rows_own, rows_beside, fused_other = tie(rows_own, rows_beside, fused_other)
    output_full = in_order(here_x, output_own, output_other, axis=1).reshape(query_cols, width)
    pieces = (
        rows_own,
        lax.ppermute(rows_own, "c", SWAP),
        rows_beside,
        lax.ppermute(rows_beside, "c", SWAP),
    )
    cot_rows = outer_sum(to_place, arrived_cot).astype(BF16)
    cot_beside = lax.ppermute(cot_rows, "y", SWAP)
    cot_rows, cot_beside, output_full = tie(cot_rows, cot_beside, output_full)
    cot_over_x = lax.ppermute(cot_rows, "x", SWAP)
    cot_across = lax.ppermute(cot_beside, "x", SWAP)
    shared = (fused_own, fused_other, output_full, tables, segments)
    normed_all, fused, heads, kept, sent = attention_forward(place, pieces, *shared)
    kept, sent, cot_over_x = tie(kept, sent, cot_over_x)
    for shard in ff_shards[1:]:
        shard, sent = tie(shard, sent)
        ff_weights.append(gather_z(shard))
    attended = reduce_tensor(kept, sent).reshape(flat_rows, width)
    cot_across, attended = tie(cot_across, attended)
    cot_all = join_planes((cot_rows, cot_over_x, cot_beside, cot_across))
    residual = inputs + attended

    second_scale = rms_scale(residual)
    normed_two = (residual * second_scale * gain_two).astype(BF16)
    planes = list(gather_planes(normed_two))
    planes[1], cot_all = tie(planes[1], cot_all)
    normed_two_all = join_planes(tuple(planes))

    earlier = []
    gate_kept, gate_moved, down_grads = [], [], []
    for chunk in range(CHUNKS):
        last = chunk == CHUNKS - 1
        hidden, d_both, *sums = feedforward(
            normed_two_all,
            cot_all,
            ff_weights[chunk],
            chunk_cols,
            earlier if last else [],
            last,
        )
        earlier.append((hidden, d_both, ff_weights[chunk]))
        if last:
            d_own, d_leaving = reduce_eight(*sums[2:])
            d_both, *d_leaving = tie(d_both, *d_leaving)
        part = feedforward_grads(normed_two_all, d_both, hidden, cot_all, z_size)
        if last:
            d_arrived = send_eight(d_leaving)
            part, d_arrived[0] = tie(part, d_arrived[0])
        total = reduce_z(part)
        own, other = choose(here_x, total[:shard_rows], total[shard_rows : 2 * shard_rows])
        gate_kept.append(own)
        gate_moved.append(other)
        down_grads.append(
            jnp.concatenate(
                [
                    total[start : start + piece]
                    for start in range(2 * shard_rows, total.shape[0], piece)
                ],
                axis=1,
            )
        )
    down_grad = jnp.concatenate(down_grads, axis=0).astype(F32)

    d_normed_two = d_own + sum(part.astype(F32) for part in d_arrived)
    d_through, d_gain_two = norm_backward(residual, second_scale, gain_two, d_normed_two)
    d_residual = cot_rows.astype(F32) + d_through

    d_residual, *out_parts = tie(d_residual, *sums[:2])
    out_own, out_leaving = reduce_eight(*out_parts)
    pieces = gather_tensor(d_residual.astype(BF16).reshape(micro, local_rows, width))
    out_over_x = lax.ppermute(jnp.stack([out_leaving[0], out_leaving[2]]), "x", SWAP)
    kept, sent, *weight_parts = attention_backward(
        place, pieces, *shared, normed_all, fused, heads, output_weight.shape[0]
    )
    kept, sent, out_over_x = tie(kept, sent, out_over_x)
    out_over_y = (out_leaving[1].astype(F32) + out_over_x[1].astype(F32)).astype(BF16)
    layer_rows = (
        residual
        + (out_own + out_over_x[0].astype(F32))
        + lax.ppermute(out_over_y, "y", SWAP).astype(F32)
    )
    d_normed_one = reduce_tensor(kept, sent).reshape(flat_rows, width)
    swapped = swap_blocks(
        jnp.concatenate(
            [
                d_normed_one[:, side * (width // 2) + start : side * (width // 2) + start + shard_rows]
                for start in range(0, width // 2, shard_rows)
                for side in range(2)
            ],
            axis=1,
        ),
        shard_rows,
        here_x,
    )
    d_normed_one = jnp.concatenate(swapped, axis=1)

    def reduce_x(kept, leaving):
        return (kept.astype(F32) + lax.ppermute(leaving, "x", SWAP).astype(F32)).astype(BF16)

    def reduce_data(total):
        return reduce_z(total.reshape(z_size, -1, total.shape[-1])).astype(F32)

    output_total, fused_sent = tie(reduce_x(*weight_parts[2:]), weight_parts[1])
    fused_total, *gate_moved = tie(reduce_x(weight_parts[0], fused_sent), *gate_moved)
    gate_moved = [lax.ppermute(part, "x", SWAP) for part in gate_moved]
    output_grad = reduce_data(output_total)
    fused_grad = reduce_data(fused_total)
    d_first, d_gain_one = norm_backward(inputs, first_scale, gain_one, d_normed_one)
    input_grads = (d_residual + d_first).astype(BF16)

    gain_grads = jnp.stack([d_gain_one, d_gain_two])
    high = gain_grads.astype(BF16)
    low = (gain_grads - high.astype(F32)).astype(BF16)
    riders = jnp.stack([high, low]).reshape(2, 2, 2 * z_size, 1, shard_rows)
    riders = jnp.broadcast_to(
        jnp.transpose(riders, (2, 3, 0, 1, 4)), (2 * z_size, 4, 2, 2, shard_rows)
    ).reshape(flat_rows, -1)

    back = jnp.concatenate([layer_rows.astype(BF16), input_grads], axis=1)
    returned = exchange(
        by_device(jnp.concatenate([mm(to_place, back).astype(BF16), riders], axis=1))
    )
    gate_up_grads = assemble(
        place, [part for pair in zip(gate_kept, gate_moved) for part in pair], z_size, hidden_cols
    )
    returned, *gate_up_grads = tie(returned, *gate_up_grads)
    outputs = outer_sum(to_send, returned[:, : 2 * width]).astype(BF16)
    outputs = outputs.reshape(micro, local_rows, 2 * width)
    gain_grads = jnp.sum(
        returned[:, 2 * width :].astype(F32).reshape(devices, 2, 2, shard_rows), axis=(0, 1)
    )

    return (
        outputs[:, :, :width],
        outputs[:, :, width:],
        fused_grad[:, :query_cols],
        fused_grad[:, query_cols : query_cols + kv_cols],
        fused_grad[:, query_cols + kv_cols :],
        output_grad,
        *gate_up_grads,
        down_grad,
        gain_grads[0],
        gain_grads[1],
    )


def solution(mesh):
    z_size = mesh.shape["dp"] // 2
    fine = Mesh(mesh.devices.reshape(z_size, 2, 2, 2), ("z", "x", "y", "c"))
    dp, tensor = ("z", "x"), ("y", "c")
    rows, columns, stacked = P(None, dp + tensor, None), P(dp, tensor), P(tensor + dp, None)
    return jax.shard_map(
        body,
        mesh=fine,
        in_specs=(
            rows,
            rows,
            P(None, dp + tensor),
            P(None, dp, None),
            columns,
            columns,
            columns,
            stacked,
            columns,
            columns,
            stacked,
            P(dp),
            P(dp),
        ),
        out_specs=(
            rows,
            rows,
            columns,
            columns,
            columns,
            stacked,
            columns,
            columns,
            stacked,
            P(dp),
            P(dp),
        ),
        check_vma=False,
    )
```

```python
import functools
import math

import jax
import jax.numpy as jnp
from jax import lax
from jax.experimental import pallas as pl
from jax.experimental.layout import Layout, with_layout_constraint
from jax.experimental.pallas import tpu as pltpu
from jax.sharding import Mesh, PartitionSpec as P

HEAD_SIZE = 256
EPSILON = 1e-06
ROPE_BASE = 1000042.0
NEGATIVE = -1e30
LONGEST = 256
CHUNKS = 2
F32 = jnp.float32
BF16 = jnp.bfloat16

SWAP = [(0, 1), (1, 0)]
DIAGONAL = [(0, 3), (3, 0), (1, 2), (2, 1)]
Z_NEAR = [(0, 1), (1, 0), (2, 3), (3, 2)]
Z_FAR = [(0, 2), (2, 0), (1, 3), (3, 1)]
Z_ACROSS = [(0, 3), (3, 0), (1, 2), (2, 1)]


def rms_scale(values):
    return lax.rsqrt(jnp.mean(values * values, axis=-1, keepdims=True) + EPSILON)


def rope_tables(positions, head):
    half = head // 2
    frequency = jnp.exp(jnp.arange(half, dtype=F32) * (-2.0 * math.log(ROPE_BASE) / head))
    angles = positions.astype(F32)[:, None] * frequency[None, :]
    return (jnp.cos(angles), jnp.sin(angles))


def rotate(head, cosine, sine):
    half = head.shape[-1] // 2
    first, second = head[:, :half], head[:, half:]
    return jnp.concatenate(
        [first * cosine - second * sine, second * cosine + first * sine], axis=-1
    )


def sequence_layout(lens, total):
    rows = jnp.arange(total, dtype=jnp.int32)
    ends = jnp.cumsum(lens)
    segment = jnp.sum((rows[:, None] >= ends[None, :]).astype(jnp.int32), axis=1)
    starts = ends - lens
    which = segment[:, None] == jnp.arange(lens.shape[0], dtype=jnp.int32)[None, :]
    begin = jnp.sum(jnp.where(which, starts[None, :], 0), axis=1)
    return (segment, rows - begin)


def mm(left, right):
    return jnp.dot(left, right, preferred_element_type=F32)


def outer_sum(left, right):
    return lax.dot_general(left, right, (((0,), (0,)), ((), ())), preferred_element_type=F32)


def times_transposed(left, right):
    return lax.dot_general(left, right, (((1,), (1,)), ((), ())), preferred_element_type=F32)


def masked_scores(query, key, seg_query, seg_key, row_start, key_start):
    scores = times_transposed(query, key) * (1.0 / math.sqrt(HEAD_SIZE))
    rows = row_start + lax.broadcasted_iota(jnp.int32, scores.shape, 0)
    keys = key_start + lax.broadcasted_iota(jnp.int32, scores.shape, 1)
    allowed = (seg_query == seg_key) & (rows >= keys)
    scores = jnp.where(allowed, scores, NEGATIVE)
    expo = jnp.exp(scores - jnp.max(scores, axis=-1, keepdims=True))
    return expo / jnp.sum(expo, axis=-1, keepdims=True)


def query_blocks(total):
    size = LONGEST
    return [
        (start, start + size, max(0, start - LONGEST)) for start in range(0, total, size)
    ]


def place_rows(place_ref, piece_refs, rows_ref):
    here = place_ref[0]
    size = piece_refs[0].shape[1]
    for step, piece in enumerate(piece_refs):
        start = pl.multiple_of(jnp.bitwise_xor(here, step) * size, size)
        rows_ref[pl.ds(start, size), :] = piece[0]


def spread_rows(place_ref, rows_ref, kept_ref, sent_ref):
    here = place_ref[0]
    size = kept_ref.shape[2]
    for step in range(4):
        start = pl.multiple_of(jnp.bitwise_xor(here, step) * size, size)
        out_ref = sent_ref if step % 2 else kept_ref
        out_ref[step // 2, 0] = rows_ref[pl.ds(start, size), :]


def attention_forward_kernel(
    query_heads,
    place_ref,
    piece0,
    piece1,
    piece2,
    piece3,
    own_ref,
    other_ref,
    output_ref,
    cosine_ref,
    sine_ref,
    seg_query_ref,
    seg_key_ref,
    normed_ref,
    fused_ref,
    heads_ref,
    kept_ref,
    sent_ref,
    rows_ref,
    sums_ref,
):
    place_rows(place_ref, (piece0, piece1, piece2, piece3), rows_ref)
    normed_ref[...] = rows_ref[...]
    half = own_ref.shape[0]
    fused = mm(rows_ref[:, :half], own_ref[...]) + mm(rows_ref[:, half:], other_ref[...])
    cosine, sine = cosine_ref[0], sine_ref[0]
    total = rows_ref.shape[0]
    kv_heads = fused.shape[1] // HEAD_SIZE - query_heads
    for head in range(query_heads + kv_heads // 2):
        columns = slice(head * HEAD_SIZE, (head + 1) * HEAD_SIZE)
        fused_ref[:, columns] = rotate(fused[:, columns], cosine, sine).astype(BF16)
    first_value = (query_heads + kv_heads // 2) * HEAD_SIZE
    fused_ref[:, first_value:] = fused[:, first_value:].astype(BF16)
    per_group = 2 * query_heads // kv_heads
    for head in range(query_heads):
        group = head // per_group
        columns = slice(head * HEAD_SIZE, (head + 1) * HEAD_SIZE)
        at_key = (query_heads + group) * HEAD_SIZE
        at_value = first_value + group * HEAD_SIZE
        for start, stop, low in query_blocks(total):
            probs = masked_scores(
                fused_ref[start:stop, columns],
                fused_ref[low:stop, at_key : at_key + HEAD_SIZE],
                seg_query_ref[0, start:stop],
                seg_key_ref[0, :, low:stop],
                start,
                low,
            )
            heads_ref[start:stop, columns] = mm(
                probs.astype(BF16), fused_ref[low:stop, at_value : at_value + HEAD_SIZE]
            ).astype(BF16)
    sums_ref[...] = mm(heads_ref[...], output_ref[...]).astype(BF16)
    spread_rows(place_ref, sums_ref, kept_ref, sent_ref)


def attention_backward_kernel(
    query_heads,
    block_rows,
    place_ref,
    piece0,
    piece1,
    piece2,
    piece3,
    own_ref,
    other_ref,
    output_ref,
    cosine_ref,
    sine_ref,
    seg_query_ref,
    seg_key_ref,
    normed_ref,
    fused_ref,
    heads_ref,
    kept_ref,
    sent_ref,
    fused_kept_ref,
    fused_sent_ref,
    output_kept_ref,
    output_sent_ref,
    rows_ref,
    sums_ref,
    d_heads_ref,
    d_fused_ref,
    d_key_ref,
    d_value_ref,
    fused_acc,
    output_acc,
):
    index = pl.program_id(0)
    scale = 1.0 / math.sqrt(HEAD_SIZE)
    place_rows(place_ref, (piece0, piece1, piece2, piece3), rows_ref)
    d_heads_ref[...] = times_transposed(rows_ref[...], output_ref[...]).astype(BF16)
    cosine, sine = cosine_ref[0], sine_ref[0]
    total = rows_ref.shape[0]
    kv_heads = fused_ref.shape[1] // HEAD_SIZE - query_heads
    first_value = (query_heads + kv_heads // 2) * HEAD_SIZE
    per_group = 2 * query_heads // kv_heads
    for group in range(kv_heads // 2):
        at_key = (query_heads + group) * HEAD_SIZE
        at_value = first_value + group * HEAD_SIZE
        d_key_ref[...] = jnp.zeros_like(d_key_ref)
        d_value_ref[...] = jnp.zeros_like(d_value_ref)
        for head in range(group * per_group, (group + 1) * per_group):
            columns = slice(head * HEAD_SIZE, (head + 1) * HEAD_SIZE)
            for start, stop, low in query_blocks(total):
                query = fused_ref[start:stop, columns]
                key = fused_ref[low:stop, at_key : at_key + HEAD_SIZE]
                value = fused_ref[low:stop, at_value : at_value + HEAD_SIZE]
                d_heads = d_heads_ref[start:stop, columns]
                probs = masked_scores(
                    query,
                    key,
                    seg_query_ref[0, start:stop],
                    seg_key_ref[0, :, low:stop],
                    start,
                    low,
                )
                d_probs = times_transposed(d_heads, value)
                delta = jnp.sum(probs * d_probs, axis=-1, keepdims=True)
                d_scores = (probs * (d_probs - delta)).astype(BF16)
                d_query = mm(d_scores, key) * scale
                d_fused_ref[start:stop, columns] = rotate(
                    d_query, cosine[start:stop], -sine[start:stop]
                ).astype(BF16)
                d_key_ref[low:stop] += outer_sum(d_scores, query) * scale
                d_value_ref[low:stop] += outer_sum(probs.astype(BF16), d_heads)
        d_fused_ref[:, at_key : at_key + HEAD_SIZE] = rotate(
            d_key_ref[...], cosine, -sine
        ).astype(BF16)
        d_fused_ref[:, at_value : at_value + HEAD_SIZE] = d_value_ref[...].astype(BF16)
    half = own_ref.shape[0]
    sums_ref[:, :half] = times_transposed(d_fused_ref[...], own_ref[...]).astype(BF16)
    sums_ref[:, half:] = times_transposed(d_fused_ref[...], other_ref[...]).astype(BF16)
    spread_rows(place_ref, sums_ref, kept_ref, sent_ref)
    fused_part = outer_sum(normed_ref[...], d_fused_ref[...])
    output_part = outer_sum(heads_ref[...], rows_ref[...])

    @pl.when(index == 0)
    def _():
        fused_acc[...] = fused_part
        output_acc[...] = output_part

    @pl.when(index > 0)
    def _():
        fused_acc[...] += fused_part
        output_acc[...] += output_part

    @pl.when(index == pl.num_programs(0) - 1)
    def _():
        fused_kept_ref[...] = fused_acc[:half].astype(BF16)
        fused_sent_ref[...] = fused_acc[half:].astype(BF16)
        here_x = place_ref[1]
        size = block_rows
        for step in range(output_acc.shape[0] // (2 * size)):
            kept = pl.multiple_of((2 * step + here_x) * size, size)
            sent = pl.multiple_of((2 * step + 1 - here_x) * size, size)
            rows = slice(step * size, (step + 1) * size)
            output_kept_ref[rows] = output_acc[pl.ds(kept, size), :].astype(BF16)
            output_sent_ref[rows] = output_acc[pl.ds(sent, size), :].astype(BF16)


def whole_spec(shape):
    zeros = (0,) * len(shape)
    return pl.BlockSpec(shape, lambda *_: zeros, pipeline_mode=pl.Buffered(1))


def attention_specs(pieces, own, other, output_full, tables, segments):
    micro, rows, width = pieces[0].shape
    total = 4 * rows
    half = tables[0].shape[-1]
    return (
        [pl.BlockSpec(memory_space=pltpu.SMEM)]
        + [pl.BlockSpec((1, rows, width), lambda m: (m, 0, 0))] * 4
        + [whole_spec(own.shape), whole_spec(other.shape), whole_spec(output_full.shape)]
        + [pl.BlockSpec((1, total, half), lambda m: (m, 0, 0))] * 2
        + [
            pl.BlockSpec((1, total, 1), lambda m: (m, 0, 0)),
            pl.BlockSpec((1, 1, total), lambda m: (m, 0, 0)),
        ]
    )


def attention_forward(place, pieces, own, other, output_full, tables, segments):
    micro, rows, width = pieces[0].shape
    total = 4 * rows
    query_cols, fused_cols = output_full.shape[0], own.shape[1]

    def by_micro(columns):
        return pl.BlockSpec((total, columns), lambda m: (m, 0))

    return pl.pallas_call(
        functools.partial(attention_forward_kernel, query_cols // HEAD_SIZE),
        grid=(micro,),
        in_specs=attention_specs(pieces, own, other, output_full, tables, segments),
        out_specs=[
            by_micro(width),
            by_micro(fused_cols),
            by_micro(query_cols),
            pl.BlockSpec((2, 1, rows, width), lambda m: (0, m, 0, 0)),
            pl.BlockSpec((2, 1, rows, width), lambda m: (0, m, 0, 0)),
        ],
        out_shape=[
            jax.ShapeDtypeStruct((micro * total, width), BF16),
            jax.ShapeDtypeStruct((micro * total, fused_cols), BF16),
            jax.ShapeDtypeStruct((micro * total, query_cols), BF16),
            jax.ShapeDtypeStruct((2, micro, rows, width), BF16),
            jax.ShapeDtypeStruct((2, micro, rows, width), BF16),
        ],
        scratch_shapes=[pltpu.VMEM((total, width), BF16), pltpu.VMEM((total, width), BF16)],
        compiler_params=pltpu.CompilerParams(vmem_limit_bytes=56 << 20),
    )(place, *pieces, own, other, output_full, *tables, *segments)


def attention_backward(
    place, pieces, own, other, output_full, tables, segments, normed, fused, heads, block_rows
):
    micro, rows, width = pieces[0].shape
    total = 4 * rows
    query_cols, fused_cols = output_full.shape[0], own.shape[1]

    def by_micro(columns):
        return pl.BlockSpec((total, columns), lambda m: (m, 0))

    return pl.pallas_call(
        functools.partial(attention_backward_kernel, query_cols // HEAD_SIZE, block_rows),
        grid=(micro,),
        in_specs=attention_specs(pieces, own, other, output_full, tables, segments)
        + [by_micro(width), by_micro(fused_cols), by_micro(query_cols)],
        out_specs=[
            pl.BlockSpec((2, 1, rows, width), lambda m: (0, m, 0, 0)),
            pl.BlockSpec((2, 1, rows, width), lambda m: (0, m, 0, 0)),
            whole_spec((width // 2, fused_cols)),
            whole_spec((width // 2, fused_cols)),
            whole_spec((query_cols // 2, width)),
            whole_spec((query_cols // 2, width)),
        ],
        out_shape=[
            jax.ShapeDtypeStruct((2, micro, rows, width), BF16),
            jax.ShapeDtypeStruct((2, micro, rows, width), BF16),
            jax.ShapeDtypeStruct((width // 2, fused_cols), BF16),
            jax.ShapeDtypeStruct((width // 2, fused_cols), BF16),
            jax.ShapeDtypeStruct((query_cols // 2, width), BF16),
            jax.ShapeDtypeStruct((query_cols // 2, width), BF16),
        ],
        scratch_shapes=[
            pltpu.VMEM((total, width), BF16),
            pltpu.VMEM((total, width), BF16),
            pltpu.VMEM((total, query_cols), BF16),
            pltpu.VMEM((total, fused_cols), BF16),
            pltpu.VMEM((total, HEAD_SIZE), F32),
            pltpu.VMEM((total, HEAD_SIZE), F32),
            pltpu.VMEM((width, fused_cols), F32),
            pltpu.VMEM((query_cols, width), F32),
        ],
        compiler_params=pltpu.CompilerParams(vmem_limit_bytes=60 << 20),
    )(place, *pieces, own, other, output_full, *tables, *segments, normed, fused, heads)


def feedforward_kernel(count, last, normed_ref, cot_ref, weights_ref, *refs):
    refs = list(refs)
    earlier = [[refs.pop(0) for _ in range(3)] for _ in range(count)]
    down_ref = refs.pop()
    hidden_ref, d_both_ref, *sums = refs
    pieces, _, fused = weights_ref.shape
    columns, width = down_ref.shape
    rows, piece = width // pieces, columns // pieces
    index = pl.program_id(0)

    @pl.when(index == 0)
    def _():
        for step in range(pieces):
            for part in range(width // fused):
                start = rows + part * piece
                down_ref[step * piece : (step + 1) * piece, part * fused : (part + 1) * fused] = (
                    weights_ref[step, start : start + piece, :]
                )

    both = mm(normed_ref[:, :rows], weights_ref[0, :rows, :])
    for step in range(1, pieces):
        both = both + mm(normed_ref[:, step * rows : (step + 1) * rows], weights_ref[step, :rows, :])
    gate, upward = both[:, :columns], both[:, columns:]
    sigmoid = 1.0 / (1.0 + jnp.exp(-gate))
    silu = gate * sigmoid
    hidden_ref[...] = (silu * upward).astype(BF16)
    d_hidden = times_transposed(cot_ref[...], down_ref[...])
    d_both_ref[:, :columns] = (
        d_hidden * upward * sigmoid * (1.0 + gate * (1.0 - sigmoid))
    ).astype(BF16)
    d_both_ref[:, columns:] = (d_hidden * silu).astype(BF16)

    if not last:
        return

    def write(out_ref, d_normed_ref):
        for part in range(width // fused):
            at = slice(part * fused, (part + 1) * fused)
            start = rows + part * piece
            out = mm(hidden_ref[...], down_ref[:, at])
            for hidden_before, _, weights_before in earlier:
                for step in range(pieces):
                    out = out + mm(
                        hidden_before[:, step * piece : (step + 1) * piece],
                        weights_before[step, start : start + piece, :],
                    )
            out_ref[:, at] = out.astype(BF16)
        for step in range(pieces):
            at = slice(step * rows, (step + 1) * rows)
            d_normed = times_transposed(d_both_ref[...], weights_ref[step, :rows, :])
            for _, d_both_before, weights_before in earlier:
                d_normed = d_normed + times_transposed(
                    d_both_before[...], weights_before[step, :rows, :]
                )
            d_normed_ref[:, at] = d_normed.astype(BF16)

    @pl.when(index < 4)
    def _():
        write(*sums[1::2])

    @pl.when(index >= 4)
    def _():
        write(*sums[0::2])


def feedforward(normed, cot, weights, columns, earlier, last):
    rows, width = normed.shape
    size = rows // 8

    def blocks(count):
        return pl.BlockSpec((size, count), lambda i: ((i + 4) % 8, 0))

    sums, shapes = [], []
    if last:
        sums = [
            pl.BlockSpec((size, width), lambda i: (jnp.maximum(i - 4, 0), 0)),
            pl.BlockSpec((size, width), lambda i: (jnp.minimum(i, 3), 0)),
        ] * 2
        shapes = [jax.ShapeDtypeStruct((rows // 2, width), BF16)] * 4
    earlier_specs = [
        spec
        for _, _, before in earlier
        for spec in (blocks(columns), blocks(2 * columns), whole_spec(before.shape))
    ]
    return pl.pallas_call(
        functools.partial(feedforward_kernel, len(earlier), last),
        grid=(8,),
        in_specs=[blocks(width), blocks(width), whole_spec(weights.shape)] + earlier_specs,
        out_specs=[blocks(columns), blocks(2 * columns)] + sums,
        out_shape=[
            jax.ShapeDtypeStruct((rows, columns), BF16),
            jax.ShapeDtypeStruct((rows, 2 * columns), BF16),
        ]
        + shapes,
        scratch_shapes=[pltpu.VMEM((columns, width), BF16)],
        compiler_params=pltpu.CompilerParams(vmem_limit_bytes=56 << 20),
    )(normed, cot, weights, *[array for before in earlier for array in before])


def feedforward_grads_kernel(normed_ref, d_both_ref, hidden_ref, cot_ref, out_ref, down_ref):
    index = pl.program_id(0)
    rows, fused = normed_ref.shape[1], d_both_ref.shape[1]
    piece = down_ref.shape[0] // pl.num_programs(0)

    @pl.when(index == 0)
    def _():
        down_ref[...] = outer_sum(hidden_ref[...], cot_ref[...]).astype(BF16)

    out_ref[0, :rows, :] = outer_sum(normed_ref[...], d_both_ref[...]).astype(BF16)
    mine = down_ref[pl.ds(pl.multiple_of(index * piece, piece), piece), :]
    for part in range(down_ref.shape[1] // fused):
        start = rows + part * piece
        out_ref[0, start : start + piece, :] = mine[:, part * fused : (part + 1) * fused]


def feedforward_grads(normed, d_both, hidden, cot, pieces):
    rows, width = normed.shape
    columns = hidden.shape[1]
    fused = d_both.shape[1]
    out_rows = width // pieces + (columns // pieces) * (width // fused)
    return pl.pallas_call(
        feedforward_grads_kernel,
        grid=(pieces,),
        in_specs=[
            pl.BlockSpec((rows, width // pieces), lambda i: (0, i)),
            whole_spec(d_both.shape),
            whole_spec(hidden.shape),
            whole_spec(cot.shape),
        ],
        out_specs=pl.BlockSpec((1, out_rows, fused), lambda i: (i, 0, 0)),
        out_shape=jax.ShapeDtypeStruct((pieces, out_rows, fused), BF16),
        scratch_shapes=[pltpu.VMEM((columns, width), BF16)],
        compiler_params=pltpu.CompilerParams(vmem_limit_bytes=56 << 20),
    )(normed, d_both, hidden, cot)


def split_kernel(pieces, place_ref, gate_ref, up_ref, *refs):
    here_x = place_ref[1]
    chunks = len(refs) // 2
    size = gate_ref.shape[1] // (2 * chunks * pieces)
    for chunk in range(chunks):
        sides = []
        for side in range(2):
            starts = [(2 * chunks * step + side * chunks + chunk) * size for step in range(pieces)]
            sides.append(
                jnp.concatenate(
                    [ref[:, at : at + size] for ref in (gate_ref, up_ref) for at in starts], axis=1
                )
            )
        refs[2 * chunk][...] = jnp.where(here_x == 0, sides[0], sides[1])
        refs[2 * chunk + 1][...] = jnp.where(here_x == 0, sides[1], sides[0])


def split(place, gate, up, pieces):
    rows, columns = gate.shape
    size = min(rows, 64)
    fused = 2 * columns // (2 * CHUNKS)
    return pl.pallas_call(
        functools.partial(split_kernel, pieces),
        grid=(rows // size,),
        in_specs=[pl.BlockSpec(memory_space=pltpu.SMEM)]
        + [pl.BlockSpec((size, columns), lambda i: (i, 0))] * 2,
        out_specs=[pl.BlockSpec((size, fused), lambda i: (i, 0))] * (2 * CHUNKS),
        out_shape=[jax.ShapeDtypeStruct((rows, fused), BF16)] * (2 * CHUNKS),
    )(place, gate, up)


def assemble_kernel(pieces, place_ref, *refs):
    inputs, outputs = refs[:-2], refs[-2:]
    here_x = place_ref[1]
    chunks = len(inputs) // 2
    half = inputs[0].shape[1] // 2
    size = half // pieces
    for which, out_ref in enumerate(outputs):
        for step in range(pieces):
            columns = slice(which * half + step * size, which * half + (step + 1) * size)
            own = [inputs[2 * chunk][:, columns].astype(F32) for chunk in range(chunks)]
            moved = [inputs[2 * chunk + 1][:, columns].astype(F32) for chunk in range(chunks)]
            even = [jnp.where(here_x == 0, a, b) for a, b in zip(own, moved)]
            odd = [jnp.where(here_x == 0, b, a) for a, b in zip(own, moved)]
            span = 2 * chunks * size
            out_ref[:, step * span : (step + 1) * span] = jnp.concatenate(even + odd, axis=1)


def assemble(place, inputs, pieces, columns):
    rows, width = inputs[0].shape
    size = min(rows, 64)
    return pl.pallas_call(
        functools.partial(assemble_kernel, pieces),
        grid=(rows // size,),
        in_specs=[pl.BlockSpec(memory_space=pltpu.SMEM)]
        + [pl.BlockSpec((size, width), lambda i: (i, 0))] * len(inputs),
        out_specs=[pl.BlockSpec((size, columns), lambda i: (i, 0))] * 2,
        out_shape=[jax.ShapeDtypeStruct((rows, columns), F32)] * 2,
    )(place, *inputs)


def norm_backward(values, scale, gain, d_normed):
    weighted = d_normed * gain
    d_values = scale * weighted - values * scale * scale * scale * jnp.mean(
        weighted * values, axis=-1, keepdims=True
    )
    return (d_values, jnp.sum(d_normed * values * scale, axis=0))


def take(array, index, axis=0):
    return lax.dynamic_index_in_dim(array, index, axis, keepdims=False)


def choose(position, own, other):
    return [jnp.where(position == 0, own, other), jnp.where(position == 0, other, own)]


def in_order(position, own, other, axis=0):
    return jnp.stack(choose(position, own, other), axis=axis)


def rows_major(array):
    return with_layout_constraint(array, Layout(major_to_minor=tuple(range(array.ndim))))


def gather_z(piece):
    return rows_major(lax.all_gather(rows_major(piece), "z", axis=0))


def gather_z_small(piece):
    size, here = lax.axis_size("z"), lax.axis_index("z")
    if size != 4:
        return [gather_z(piece)]
    return [piece] + [lax.ppermute(piece, "z", pairs) for pairs in (Z_NEAR, Z_FAR, Z_ACROSS)]


def join_pieces(pieces):
    if len(pieces) == 1:
        return pieces[0]
    here = lax.axis_index("z")
    whole = jnp.zeros((len(pieces),) + pieces[0].shape, pieces[0].dtype)
    for step, part in enumerate(pieces):
        whole = lax.dynamic_update_index_in_dim(whole, part, here ^ step, 0)
    return whole


def reduce_z(parts):
    return lax.psum_scatter(parts, "z", scatter_dimension=0)


def tie(*values):
    return lax.optimization_barrier(values)


def swap_blocks(rows, size, here):
    blocks = []
    for start in range(0, rows.shape[1], 2 * size):
        first, second = rows[:, start : start + size], rows[:, start + size : start + 2 * size]
        blocks += choose(here, first, second)
    return blocks


def gather_tensor(rows):
    beside = lax.ppermute(rows, "y", SWAP)
    return (
        rows,
        lax.ppermute(rows, "c", SWAP),
        beside,
        lax.ppermute(beside, "c", SWAP),
    )


def reduce_tensor(kept, sent):
    arrived = lax.ppermute(sent, "c", SWAP).astype(F32)
    moved = (kept[1].astype(F32) + arrived[1]).astype(BF16)
    return kept[0].astype(F32) + arrived[0] + lax.ppermute(moved, "y", SWAP).astype(F32)


def gather_planes(rows):
    return (
        rows,
        lax.ppermute(rows, "x", SWAP),
        lax.ppermute(rows, "y", SWAP),
        lax.ppermute(rows, ("x", "y"), DIAGONAL),
    )


def join_planes(planes):
    return jnp.concatenate(planes + tuple(lax.ppermute(plane, "c", SWAP) for plane in planes))


def reduce_eight(kept, sent):
    kept = kept.reshape((4, kept.shape[0] // 4) + kept.shape[1:])
    arrived = lax.ppermute(sent.reshape(kept.shape), "c", SWAP)
    sums = [kept[step].astype(F32) + arrived[step].astype(F32) for step in range(4)]
    return sums[0], [part.astype(BF16) for part in sums[1:]]


def send_eight(leaving):
    routes = (("x", SWAP), ("y", SWAP), (("x", "y"), DIAGONAL))
    return [lax.ppermute(part, axes, pairs) for part, (axes, pairs) in zip(leaving, routes)]


def body(
    tokens,
    cotangent,
    token_slots,
    lengths,
    query_weight,
    key_projection_weight,
    value_projection_weight,
    output_weight,
    gate_weight,
    up_weight,
    down_weight,
    prenorm_gain,
    midnorm_gain,
):
    z_size = lax.axis_size("z")
    here_x = lax.axis_index("x")
    devices = 8 * z_size
    micro, local_rows, width = tokens.shape
    flat_rows = micro * local_rows
    sends = local_rows // devices
    group_rows = 4 * local_rows
    query_cols = query_weight.shape[1]
    kv_cols = key_projection_weight.shape[1]
    fused_cols = query_cols + 2 * kv_cols
    shard_rows = query_weight.shape[0]
    hidden_cols = gate_weight.shape[1]
    block = hidden_cols // (2 * z_size)
    piece = block // CHUNKS
    chunk_cols = z_size * piece
    everywhere = ("z", "x", "y", "c")
    place = jnp.stack([2 * lax.axis_index("y") + lax.axis_index("c"), here_x]).astype(jnp.int32)

    fused_shard = jnp.concatenate(
        [query_weight, key_projection_weight, value_projection_weight], axis=1
    )
    fused_shard, token_slots = tie(fused_shard, token_slots)

    rank = jnp.sum(
        (token_slots[:, None, :] < token_slots[:, :, None]).astype(jnp.int32), axis=2
    )
    order = (
        (rank // sends) * (micro * sends)
        + jnp.arange(micro, dtype=jnp.int32)[:, None] * sends
        + rank % sends
    ).reshape(flat_rows)
    places = jnp.arange(flat_rows, dtype=jnp.int32)
    to_send = (places[:, None] == order[None, :]).astype(BF16)
    local_slot = (token_slots % local_rows).reshape(flat_rows)

    def by_device(rows):
        return rows.reshape((devices, micro * sends) + rows.shape[1:])

    def exchange(blocks):
        return lax.all_to_all(
            blocks, everywhere, split_axis=0, concat_axis=0, tiled=True
        ).reshape((flat_rows,) + blocks.shape[2:])

    gains = jnp.stack([prenorm_gain, midnorm_gain]).reshape(micro * sends, -1)
    leaving = jnp.concatenate(
        [
            tokens.reshape(flat_rows, width),
            jnp.broadcast_to(local_slot[:, None], (flat_rows, gains.shape[1])).astype(BF16),
        ],
        axis=1,
    )
    leaving = jnp.concatenate(
        [mm(to_send, leaving).astype(BF16), jnp.tile(gains, (devices, 1))], axis=1
    )
    leaving, gate_weight, down_weight, cotangent = tie(
        by_device(leaving), gate_weight, down_weight, cotangent
    )
    arrived = exchange(leaving)
    cot_leaving = mm(to_send, cotangent.reshape(flat_rows, width)).astype(BF16)
    cot_leaving, arrived = tie(cot_leaving, arrived)
    arrived_cot = exchange(by_device(cot_leaving))
    arrived_tokens = arrived[:, :width]
    arrived_slots = arrived[:, width].astype(jnp.int32)
    arrived_gains = arrived[:, width + gains.shape[1] :].reshape(
        2 * z_size, 4, 2, -1, gains.shape[1]
    )[:, 0]
    gains = jnp.swapaxes(arrived_gains, 0, 1).reshape(2, width).astype(F32)
    gain_one, gain_two = gains[0:1], gains[1:2]
    arrived_micro = (places // sends) % micro
    to_place = (
        (arrived_slots + arrived_micro * local_rows)[:, None] == places[None, :]
    ).astype(BF16)

    halves = split(place, gate_weight, up_weight, z_size)
    ff_shards = []
    for chunk in range(CHUNKS):
        kept, leaving = halves[2 * chunk : 2 * chunk + 2]
        down = down_weight[chunk * piece : (chunk + 1) * piece]
        down_parts = [
            down[:, start : start + 2 * chunk_cols] for start in range(0, width, 2 * chunk_cols)
        ]
        ff_shards.append(
            jnp.concatenate(
                choose(here_x, kept, lax.ppermute(leaving, "x", SWAP)) + down_parts
            )
        )

    fused_own = gather_z(fused_shard).reshape(width // 2, fused_cols)
    output_pieces = gather_z_small(output_weight)
    crossed = lax.ppermute(output_pieces[0], "x", SWAP)
    count = len(output_pieces)
    fused_own, arrived_tokens, crossed, *rest = tie(
        fused_own, arrived_tokens, crossed, *output_pieces, *ff_shards
    )
    output_pieces, ff_shards = rest[:count], rest[count:]
    crossed = [crossed] + [lax.ppermute(part, "x", SWAP) for part in output_pieces[1:]]
    output_own, output_other = join_pieces(output_pieces), join_pieces(crossed)
    ff_weights = [gather_z(ff_shards[0])]
    fused_other = lax.ppermute(fused_own, "x", SWAP)

    inputs = outer_sum(to_place, arrived_tokens)
    first_scale = rms_scale(inputs)
    first_normed = (inputs * first_scale * gain_one).astype(BF16)
    blocks = swap_blocks(first_normed, shard_rows, here_x)
    first_normed = jnp.concatenate(blocks[0::2] + blocks[1::2], axis=1)
    segments, tables = [], []
    for index in range(micro):
        segment, positions = sequence_layout(lengths[index, 0], group_rows)
        segments.append(segment)
        tables.append(rope_tables(positions, HEAD_SIZE))
    segments = jnp.stack(segments)
    segments = (segments[:, :, None], segments[:, None, :])
    tables = tuple(jnp.stack(table) for table in zip(*tables))
    rows_own = first_normed.reshape(micro, local_rows, width)
    rows_beside = lax.ppermute(rows_own, "y", SWAP)
    rows_own, rows_beside, fused_other = tie(rows_own, rows_beside, fused_other)
    output_full = in_order(here_x, output_own, output_other, axis=1).reshape(query_cols, width)
    pieces = (
        rows_own,
        lax.ppermute(rows_own, "c", SWAP),
        rows_beside,
        lax.ppermute(rows_beside, "c", SWAP),
    )
    cot_rows = outer_sum(to_place, arrived_cot).astype(BF16)
    cot_beside = lax.ppermute(cot_rows, "y", SWAP)
    cot_rows, cot_beside, output_full = tie(cot_rows, cot_beside, output_full)
    cot_over_x = lax.ppermute(cot_rows, "x", SWAP)
    cot_across = lax.ppermute(cot_beside, "x", SWAP)
    shared = (fused_own, fused_other, output_full, tables, segments)
    normed_all, fused, heads, kept, sent = attention_forward(place, pieces, *shared)
    kept, sent, cot_over_x = tie(kept, sent, cot_over_x)
    for shard in ff_shards[1:]:
        shard, sent = tie(shard, sent)
        ff_weights.append(gather_z(shard))
    attended = reduce_tensor(kept, sent).reshape(flat_rows, width)
    cot_across, attended = tie(cot_across, attended)
    cot_all = join_planes((cot_rows, cot_over_x, cot_beside, cot_across))
    residual = inputs + attended

    second_scale = rms_scale(residual)
    normed_two = (residual * second_scale * gain_two).astype(BF16)
    planes = list(gather_planes(normed_two))
    planes[1], cot_all = tie(planes[1], cot_all)
    normed_two_all = join_planes(tuple(planes))

    earlier = []
    gate_kept, gate_moved, down_grads = [], [], []
    for chunk in range(CHUNKS):
        last = chunk == CHUNKS - 1
        hidden, d_both, *sums = feedforward(
            normed_two_all,
            cot_all,
            ff_weights[chunk],
            chunk_cols,
            earlier if last else [],
            last,
        )
        earlier.append((hidden, d_both, ff_weights[chunk]))
        if last:
            d_own, d_leaving = reduce_eight(*sums[2:])
            d_both, *d_leaving = tie(d_both, *d_leaving)
        part = feedforward_grads(normed_two_all, d_both, hidden, cot_all, z_size)
        if last:
            d_arrived = send_eight(d_leaving)
            part, d_arrived[0] = tie(part, d_arrived[0])
        total = reduce_z(part)
        own, other = choose(here_x, total[:shard_rows], total[shard_rows : 2 * shard_rows])
        gate_kept.append(own)
        gate_moved.append(other)
        down_grads.append(
            jnp.concatenate(
                [
                    total[start : start + piece]
                    for start in range(2 * shard_rows, total.shape[0], piece)
                ],
                axis=1,
            )
        )
    down_grad = jnp.concatenate(down_grads, axis=0).astype(F32)

    d_normed_two = d_own + sum(part.astype(F32) for part in d_arrived)
    d_through, d_gain_two = norm_backward(residual, second_scale, gain_two, d_normed_two)
    d_residual = cot_rows.astype(F32) + d_through

    d_residual, *out_parts = tie(d_residual, *sums[:2])
    out_own, out_leaving = reduce_eight(*out_parts)
    pieces = gather_tensor(d_residual.astype(BF16).reshape(micro, local_rows, width))
    out_over_x = lax.ppermute(jnp.stack([out_leaving[0], out_leaving[2]]), "x", SWAP)
    kept, sent, *weight_parts = attention_backward(
        place, pieces, *shared, normed_all, fused, heads, output_weight.shape[0]
    )
    kept, sent, out_over_x = tie(kept, sent, out_over_x)
    out_over_y = (out_leaving[1].astype(F32) + out_over_x[1].astype(F32)).astype(BF16)
    layer_rows = (
        residual
        + (out_own + out_over_x[0].astype(F32))
        + lax.ppermute(out_over_y, "y", SWAP).astype(F32)
    )
    d_normed_one = reduce_tensor(kept, sent).reshape(flat_rows, width)
    swapped = swap_blocks(
        jnp.concatenate(
            [
                d_normed_one[:, side * (width // 2) + start : side * (width // 2) + start + shard_rows]
                for start in range(0, width // 2, shard_rows)
                for side in range(2)
            ],
            axis=1,
        ),
        shard_rows,
        here_x,
    )
    d_normed_one = jnp.concatenate(swapped, axis=1)

    def reduce_x(kept, leaving):
        return (kept.astype(F32) + lax.ppermute(leaving, "x", SWAP).astype(F32)).astype(BF16)

    def reduce_data(total):
        return reduce_z(total.reshape(z_size, -1, total.shape[-1])).astype(F32)

    output_total, fused_sent = tie(reduce_x(*weight_parts[2:]), weight_parts[1])
    fused_total, *gate_moved = tie(reduce_x(weight_parts[0], fused_sent), *gate_moved)
    gate_moved = [lax.ppermute(part, "x", SWAP) for part in gate_moved]
    output_grad = reduce_data(output_total)
    fused_grad = reduce_data(fused_total)
    d_first, d_gain_one = norm_backward(inputs, first_scale, gain_one, d_normed_one)
    input_grads = (d_residual + d_first).astype(BF16)

    gain_grads = jnp.stack([d_gain_one, d_gain_two])
    high = gain_grads.astype(BF16)
    low = (gain_grads - high.astype(F32)).astype(BF16)
    riders = jnp.stack([high, low]).reshape(2, 2, 2 * z_size, 1, shard_rows)
    riders = jnp.broadcast_to(
        jnp.transpose(riders, (2, 3, 0, 1, 4)), (2 * z_size, 4, 2, 2, shard_rows)
    ).reshape(flat_rows, -1)

    back = jnp.concatenate([layer_rows.astype(BF16), input_grads], axis=1)
    returned = exchange(
        by_device(jnp.concatenate([mm(to_place, back).astype(BF16), riders], axis=1))
    )
    gate_up_grads = assemble(
        place, [part for pair in zip(gate_kept, gate_moved) for part in pair], z_size, hidden_cols
    )
    returned, *gate_up_grads = tie(returned, *gate_up_grads)
    outputs = outer_sum(to_send, returned[:, : 2 * width]).astype(BF16)
    outputs = outputs.reshape(micro, local_rows, 2 * width)
    gain_grads = jnp.sum(
        returned[:, 2 * width :].astype(F32).reshape(devices, 2, 2, shard_rows), axis=(0, 1)
    )

    return (
        outputs[:, :, :width],
        outputs[:, :, width:],
        fused_grad[:, :query_cols],
        fused_grad[:, query_cols : query_cols + kv_cols],
        fused_grad[:, query_cols + kv_cols :],
        output_grad,
        *gate_up_grads,
        down_grad,
        gain_grads[0],
        gain_grads[1],
    )


def solution(mesh):
    z_size = mesh.shape["dp"] // 2
    fine = Mesh(mesh.devices.reshape(z_size, 2, 2, 2), ("z", "x", "y", "c"))
    dp, tensor = ("z", "x"), ("y", "c")
    rows, columns, stacked = P(None, dp + tensor, None), P(dp, tensor), P(tensor + dp, None)
    return jax.shard_map(
        body,
        mesh=fine,
        in_specs=(
            rows,
            rows,
            P(None, dp + tensor),
            P(None, dp, None),
            columns,
            columns,
            columns,
            stacked,
            columns,
            columns,
            stacked,
            P(dp),
            P(dp),
        ),
        out_specs=(
            rows,
            rows,
            columns,
            columns,
            columns,
            stacked,
            columns,
            columns,
            stacked,
            P(dp),
            P(dp),
        ),
        check_vma=False,
    )
```
